128 devices in a mesh: ctx: 8 (over x, core), tp: 16 (over z, y).
Axes of the slice: x: 4, y: 4, z: 4, core: 2. Of those that a mesh axis runs over, the one named last changes fastest.
Arguments:
- out_grad: bfloat16 [8192, 4096], P('ctx', 'tp'), may hold values from -6 to 6
- pre_act: bfloat16 [8192, 4096], P('ctx', 'tp'), may hold values from -6 to 6
- normed: bfloat16 [8192, 12800], P('ctx', 'tp'), may hold values from -5 to 5
- inverse_std: float32 [8192], P('ctx'), may hold values from 0.5 to 2
- w_up: bfloat16 [4096, 12800], P(None, 'tp')
- w_down: bfloat16 [4096, 4096], P(None, 'tp'), may hold values from -0.09375 to 0.09375
- ln_gain: float32 [12800], P('tp'), may hold values from 0.25 to 1.75
- owner_map: int32 [8, 4], P('ctx'), may hold values from 0 to 15, as said below
Outputs:
- grad_w2: float32 [4096, 4096], P('ctx', 'tp')
- grad_w1: float32 [4096, 12800], P('ctx', 'tp')
- grad_b1: float32 [4096], P('tp')
- grad_b2: float32 [4096], P('tp')
- ln_grads: float32 [2, 12800], P(None, 'tp')
- vit_grad: bfloat16 [32768, 12800], P(('ctx', 'tp'))
The draws below stay inside these ranges and needn't reach their ends.
Inputs may be any that keep to these rules, and one draw needn't show every extreme that they name: `owner_map`: within each context shard, every encoder rank owns at most 1 of the 4 images, and some rank owns exactly 1.
All inputs are finite; a program needn't handle non-finite values.
Results may differ from the reference program's by a relative error of at most 0.007.
Values may be sent and summed in bfloat16 or wider, within the bound.
A program may use at most 192 MiB of HBM per device.

```python
import math
import jax
import jax.numpy as jnp

D = 4096
PH = 4096
PW = 12800
ROWS = 1024
IMG = 256
IMGS_GRP = 4
MOST = 1
NV = 8192
OWNER_ROWS = 32768
N_CTX = 8
N_TP = 16


def owner_group(group_key):
    key_busy, key_rest, key_shuffle = jax.random.split(group_key, 3)
    busiest = jax.random.randint(key_busy, (), 0, N_TP).astype(jnp.int32)
    others = jax.random.permutation(key_rest, (N_TP - 1) * MOST).astype(jnp.int32)
    remainder = (busiest + 1 + others // MOST) % N_TP
    listing = jnp.concatenate([jnp.full((MOST,), 1, jnp.int32) * busiest, remainder.astype(jnp.int32)])[:IMGS_GRP]
    shuffle = jax.random.permutation(key_shuffle, IMGS_GRP)
    return listing[shuffle].astype(jnp.int32)


def draw_owner_map(key, part):
    group_keys = jax.random.split(jax.random.fold_in(key, 17), N_CTX)
    return jax.vmap(owner_group)(group_keys)


def draw_w_up(key, part):
    key_noise, key_common = jax.random.split(jax.random.fold_in(key, 29))
    noise = jax.random.normal(key_noise, (PH, PW), jnp.float32)
    common = jax.random.normal(key_common, (PH, 1), jnp.float32)
    return ((noise + common) * float(PH) ** (-0.5)).astype(jnp.bfloat16)


def spiked(drawn, own_key, source, target, blocks, factor):
    def block_of(axis_at):
        return (jnp.arange(drawn.shape[axis_at]) // (drawn.shape[axis_at] // blocks)).reshape((-1,) + (1,) * (drawn.ndim - 1 - axis_at))

    first = jax.random.permutation(own_key, blocks)[block_of(target)]
    other_side = (block_of(target) + blocks // 2) % blocks
    return jnp.where((block_of(source) == first) | (block_of(source) == other_side), factor * drawn, drawn)


def level_of(rng, dims, shards, smallest, high):
    def one(dim, parts):
        heights = jax.random.uniform(jax.random.fold_in(jax.random.fold_in(rng, 6), dim), (parts,), jnp.float32, smallest / len(shards), high / len(shards))
        return jnp.repeat(jnp.exp(heights), dims[dim] // parts).reshape((-1,) + (1,) * (len(dims) - dim - 1))

    loudness = one(*shards[0])
    for cut in shards[1:]:
        loudness = loudness * one(*cut)
    return loudness


def centred(rng, extent, spread, reach, shards=(), dtype=jnp.bfloat16):
    level = level_of(rng, extent, shards, -0.22, 0.18) if shards else 1.0
    result = jax.random.normal(rng, extent, jnp.float32) * spread * level
    return jnp.minimum(jnp.maximum(result, -reach), reach).astype(dtype)


def heavy_noise(stream_key, extent, spread, most, cuts, heavy, dtype=jnp.bfloat16):
    result = spread * jax.random.normal(stream_key, extent, jnp.float32)
    if cuts:
        result = result * level_of(stream_key, extent, cuts, -0.22, 0.18)
    return jnp.clip(spiked(result, jax.random.fold_in(stream_key, 3), *heavy), -most, most).astype(dtype)


def setup_inputs(seed: int = 0) -> dict:
    streams_of = jax.random.split(jax.random.key(seed), 9)
    return {
        "out_grad": heavy_noise(streams_of[0], (NV, D), 1.0, 6.0, ((0, 8), (1, 16)), (0, 1, 16, 2.0)),
        "pre_act": centred(streams_of[1], (NV, PH), 1.5, 6.0, ((0, 8), (1, 16))),
        "normed": centred(streams_of[2], (NV, PW), 1.0, 5.0, ((0, 8), (1, 16))),
        "inverse_std": jnp.clip(jnp.exp(math.log(2.0) - 1.3862944 * jax.random.uniform(streams_of[3], (NV,), jnp.float32) ** level_of(streams_of[3], (NV,), ((0, 8),), -0.2, 0.2)), 0.5, 2.0),
        "w_up": draw_w_up(jax.random.fold_in(streams_of[8], 71), 0),
        "w_down": centred(streams_of[5], (D, PH), D ** -0.5, 0.09375, ((1, 16),)),
        "ln_gain": jnp.clip(1.0 + 0.15 * jax.random.normal(streams_of[6], (PW,), jnp.float32), 0.25, 1.75),
        "owner_map": draw_owner_map(jax.random.fold_in(streams_of[8], 71), 0),
    }


def gelu_parts(linear):
    normal_cdf = 0.5 * (1.0 + jax.scipy.special.erf(linear * (2.0 ** -0.5)))
    density = jnp.exp(-0.5 * linear * linear) * ((2.0 * math.pi) ** -0.5)
    return linear * normal_cdf, normal_cdf + linear * density


def slot_numbers(owners, capacity):
    position = jnp.arange(owners.shape[0]).astype(jnp.int32)
    earlier = (owners[None, :] == owners[:, None]) & (position[None, :] < position[:, None])
    return owners * capacity + jnp.sum(earlier.astype(jnp.int32), axis=1).astype(jnp.int32)


def reference(out_grad, pre_act, normed, inverse_std, w_up, w_down, ln_gain, owner_map):
    grad_scale = float(NV) ** -0.5
    gelu_value, gelu_slope = gelu_parts(pre_act.astype(jnp.float32))
    hidden = gelu_value.astype(jnp.bfloat16)
    back_hidden = jnp.dot(out_grad, w_down, preferred_element_type=jnp.float32)
    back_linear = (back_hidden * gelu_slope).astype(jnp.bfloat16)
    grad_w2 = jnp.dot(out_grad.T, hidden, preferred_element_type=jnp.float32) * grad_scale
    grad_b1 = jnp.sum(back_linear.astype(jnp.float32), axis=0) * grad_scale
    grad_b2 = jnp.sum(out_grad.astype(jnp.float32), axis=0) * grad_scale
    grad_w1 = jnp.dot(back_linear.T, normed, preferred_element_type=jnp.float32) * grad_scale
    norm_grad = jnp.dot(back_linear, w_up, preferred_element_type=jnp.float32)
    features = normed.astype(jnp.float32)
    gained = ln_gain[None, :] * norm_grad
    mean_first = jnp.mean(gained, axis=-1, keepdims=True)
    mean_second = jnp.mean(gained * features, axis=-1, keepdims=True)
    visual_grad = (inverse_std[:, None] * (gained - mean_first - features * mean_second)).astype(jnp.bfloat16)
    ln_grads = jnp.stack([jnp.sum(norm_grad * features, axis=0), jnp.sum(norm_grad, axis=0)]) * grad_scale
    slot_table = jax.vmap(lambda owners: slot_numbers(owners, MOST))(owner_map)
    row_ids = jnp.arange(NV).astype(jnp.int32)
    group_ids = row_ids // ROWS
    image_ids = (row_ids % ROWS) // IMG
    within = row_ids % IMG
    target = (group_ids * (N_TP * MOST) + slot_table[group_ids, image_ids]) * IMG + within
    vit_grad = jnp.zeros((OWNER_ROWS, PW), jnp.bfloat16).at[target].set(visual_grad)
    return grad_w2, grad_w1, grad_b1, grad_b2, ln_grads, vit_grad
```

```python
import math

import jax
import jax.numpy as jnp
from jax import lax
from jax.experimental import pallas as pl
from jax.experimental.pallas import tpu as pltpu
from jax.sharding import PartitionSpec as P

MESH = pl.DeviceIdType.MESH
SIDE = 4
TP = SIDE * SIDE
RINGS = 4
SUBS = 2
VMEM_LIMIT = 60 * 2**20


def gelu_parts(linear):
    normal_cdf = 0.5 * (1.0 + lax.erf(linear * 2.0 ** (-0.5)))
    density = jnp.exp(-0.5 * linear * linear) * (2.0 * math.pi) ** (-0.5)
    return (linear * normal_cdf, normal_cdf + linear * density)


def dot(left, right):
    return lax.dot_general(
        left, right, (((1,), (0,)), ((), ())), preferred_element_type=jnp.float32
    )


def row_product(left, right):
    return lax.dot_general(
        left, right, (((0,), (0,)), ((), ())), preferred_element_type=jnp.float32
    )


class Rings:
    def __init__(self, me):
        z, y = me // SIDE, me % SIDE
        b = (y + z) % SIDE
        last, first = b // 3, (3 - b) // 3

        def at(zz, yy):
            return ((zz + SIDE) % SIDE) * SIDE + (yy + SIDE) % SIDE

        self.positions = (z * SIDE + b, y * SIDE + b)
        self.targets = (
            at(z + last, y + 1 - last),
            at(z - first, y - 1 + first),
            at(z + 1 - last, y + last),
            at(z - 1 + first, y - first),
        )

    def origin(self, ring, step):
        signed = step if ring % 2 else TP - step
        q = (self.positions[ring // 2] + signed) % TP
        major, minor = q // SIDE, (q % SIDE - q // SIDE + SIDE) % SIDE
        return major * SIDE + minor if ring < 2 else minor * SIDE + major


def greet(targets):
    barrier = pltpu.get_barrier_semaphore()
    for target in targets:
        pl.semaphore_signal(barrier, inc=1, device_id={"tp": target}, device_id_type=MESH)
    pl.semaphore_wait(barrier, len(targets))


def ring_gather(prepare, rings, full_ref, send_sem, recv_sem, consume):
    quarter = full_ref.shape[1] // RINGS
    part = quarter // SUBS

    def copy(ring, step, sub, at):
        spot = full_ref.at[rings.origin(ring, at), pl.ds(ring * quarter + sub * part, part)]
        return pltpu.make_async_remote_copy(
            src_ref=spot,
            dst_ref=spot,
            send_sem=send_sem.at[ring, step, sub],
            recv_sem=recv_sem.at[ring, step, sub],
            device_id={"tp": rings.targets[ring]},
            device_id_type=MESH,
        )

    for sub in range(SUBS):
        for ring in range(RINGS):
            copy(ring, 0, sub, 0).start()
    prepare()

    def hop(step, carry):
        for sub in range(SUBS):
            for ring in range(RINGS):
                copy(ring, step - 1, sub, step).wait_recv()
                copy(ring, step, sub, step).start()
            for ring in range(RINGS // SUBS * sub, RINGS // SUBS * (sub + 1)):
                consume(rings.origin(ring, step - 1), ring)
        return carry

    lax.fori_loop(1, TP - 1, hop, 0)
    for ring in range(RINGS):
        consume(rings.origin(ring, TP - 2), ring)
    for ring in range(RINGS):
        for sub in range(SUBS):
            copy(ring, TP - 2, sub, TP - 1).wait_recv()
        consume(rings.origin(ring, TP - 1), ring)

    def drain(step, carry):
        for sub in range(SUBS):
            for ring in range(RINGS):
                copy(ring, step, sub, step).wait_send()
        return carry

    lax.fori_loop(0, TP - 1, drain, 0)


def down_kernel(
    grad_ref, w_hbm, pre_ref, part_ref, gw2_ref, full_ref, w_ref, total, gw2, hidden, slope, w_sem, send_sem, recv_sem
):
    me = lax.axis_index("tp")
    rings = Rings(me)
    load = pltpu.make_async_copy(w_hbm, w_ref, w_sem)
    load.start()
    full_ref[me] = grad_ref[...]
    greet(rings.targets)
    rows_all, width = grad_ref.shape
    quarter = rows_all // RINGS

    def prepare():
        def rows_of(i, carry):
            rows = pl.ds(pl.multiple_of(i * 64, 64), 64)
            value, steep = gelu_parts(pre_ref[rows, :].astype(jnp.float32))
            hidden[rows, :] = value.astype(jnp.bfloat16)
            slope[rows, :] = steep
            return carry

        lax.fori_loop(0, rows_all // 64, rows_of, 0)
        total[...] = jnp.zeros_like(total)
        gw2[...] = jnp.zeros_like(gw2)
        load.wait()

    def consume(origin, ring):
        rows = pl.ds(ring * quarter, quarter)
        features = pl.ds(pl.multiple_of(origin * width, width), width)
        block = full_ref[origin, rows, :]
        total[rows, :] += dot(block, w_ref[features, :])
        gw2[features, :] += row_product(block, hidden[rows, :])

    ring_gather(prepare, rings, full_ref, send_sem, recv_sem, consume)
    part_ref[...] = (total[...] * slope[...]).astype(jnp.bfloat16)
    gw2_ref[...] = gw2[...].astype(jnp.bfloat16)


def down(out_grad, w_down, pre_act):
    rows, width = out_grad.shape
    features, hid = w_down.shape
    vmem = pl.BlockSpec(memory_space=pltpu.VMEM)
    return pl.pallas_call(
        down_kernel,
        out_shape=(
            jax.ShapeDtypeStruct((rows, hid), jnp.bfloat16),
            jax.ShapeDtypeStruct((features, hid), jnp.bfloat16),
        ),
        in_specs=[vmem, pl.BlockSpec(memory_space=pl.ANY), vmem],
        out_specs=(vmem, vmem),
        scratch_shapes=[
            pltpu.VMEM((TP, rows, width), jnp.bfloat16),
            pltpu.VMEM((features, hid), jnp.bfloat16),
            pltpu.VMEM((rows, hid), jnp.float32),
            pltpu.VMEM((features, hid), jnp.float32),
            pltpu.VMEM((rows, hid), jnp.bfloat16),
            pltpu.VMEM((rows, hid), jnp.float32),
            pltpu.SemaphoreType.DMA,
            pltpu.SemaphoreType.DMA((RINGS, TP - 1, SUBS)),
            pltpu.SemaphoreType.DMA((RINGS, TP - 1, SUBS)),
        ],
        compiler_params=pltpu.CompilerParams(
            collective_id=0, has_side_effects=True, vmem_limit_bytes=VMEM_LIMIT
        ),
        name="down_ring",
    )(out_grad, w_down, pre_act)


def up_kernel(
    part_ref, w_hbm, normed_hbm, norm_ref, gw1_ref, full_ref, w_ref, normed_ref, gw1, w_sem, send_sem, recv_sem
):
    me = lax.axis_index("tp")
    rings = Rings(me)
    loads = [
        pltpu.make_async_copy(w_hbm, w_ref, w_sem.at[0]),
        pltpu.make_async_copy(normed_hbm, normed_ref, w_sem.at[1]),
    ]
    for load in loads:
        load.start()
    full_ref[me] = part_ref[...]
    greet(rings.targets)
    rows_all, width = part_ref.shape
    quarter = rows_all // RINGS

    def prepare():
        norm_ref[...] = jnp.zeros_like(norm_ref)
        gw1[...] = jnp.zeros_like(gw1)
        for load in loads:
            load.wait()

    def consume(origin, ring):
        rows = pl.ds(ring * quarter, quarter)
        units = pl.ds(pl.multiple_of(origin * width, width), width)
        block = full_ref[origin, rows, :]
        norm_ref[rows, :] += dot(block, w_ref[units, :])
        gw1[units, :] += row_product(block, normed_ref[rows, :])

    ring_gather(prepare, rings, full_ref, send_sem, recv_sem, consume)
    gw1_ref[...] = gw1[...].astype(jnp.bfloat16)


def up(back_part, w_up, normed):
    rows, width = back_part.shape
    units, channels = w_up.shape
    vmem = pl.BlockSpec(memory_space=pltpu.VMEM)
    anywhere = pl.BlockSpec(memory_space=pl.ANY)
    return pl.pallas_call(
        up_kernel,
        out_shape=(
            jax.ShapeDtypeStruct((rows, channels), jnp.float32),
            jax.ShapeDtypeStruct((units, channels), jnp.bfloat16),
        ),
        in_specs=[vmem, anywhere, anywhere],
        out_specs=(vmem, vmem),
        scratch_shapes=[
            pltpu.VMEM((TP, rows, width), jnp.bfloat16),
            pltpu.VMEM((units, channels), jnp.bfloat16),
            pltpu.VMEM((rows, channels), jnp.bfloat16),
            pltpu.VMEM((units, channels), jnp.float32),
            pltpu.SemaphoreType.DMA((2,)),
            pltpu.SemaphoreType.DMA((RINGS, TP - 1, SUBS)),
            pltpu.SemaphoreType.DMA((RINGS, TP - 1, SUBS)),
        ],
        compiler_params=pltpu.CompilerParams(
            collective_id=1, has_side_effects=True, vmem_limit_bytes=VMEM_LIMIT
        ),
        name="up_ring",
    )(back_part, w_up, normed)


def slot_numbers(owners, capacity):
    position = jnp.arange(owners.shape[0])
    earlier = (owners[None, :] == owners[:, None]) & (position[None, :] < position[:, None])
    return owners * capacity + jnp.sum(earlier.astype(jnp.int32), axis=1)


def per_device(out_grad, pre_act, normed, inverse_std, w_up, w_down, ln_gain, owner_map):
    ctx_count = lax.axis_size("ctx")
    tp_count = lax.axis_size("tp")
    row_count = out_grad.shape[0]
    grad_scale = float(row_count * ctx_count) ** (-0.5)
    back_part, gw2 = down(out_grad, w_down, pre_act)
    grad_w2 = (
        lax.psum_scatter(gw2, "ctx", scatter_dimension=0, tiled=True).astype(jnp.float32) * grad_scale
    )
    norm_grad, gw1 = up(back_part, w_up, normed)
    grad_w1 = (
        lax.psum_scatter(gw1, "ctx", scatter_dimension=0, tiled=True).astype(jnp.float32) * grad_scale
    )
    features = normed.astype(jnp.float32)
    gained = ln_gain[None, :] * norm_grad
    sum_first, sum_second = lax.psum(
        (jnp.sum(gained, axis=-1), jnp.sum(gained * features, axis=-1)), "tp"
    )
    full_width = float(normed.shape[1] * tp_count)
    mean_first = sum_first / full_width
    mean_second = sum_second / full_width
    visual = (
        inverse_std[:, None] * (gained - mean_first[:, None] - features * mean_second[:, None])
    ).astype(jnp.bfloat16)
    bias_down, bias_up, gain_sum, bias_sum = lax.psum(
        (
            jnp.sum(out_grad.astype(jnp.float32), axis=0),
            jnp.sum(back_part.astype(jnp.float32), axis=0),
            jnp.sum(norm_grad * features, axis=0),
            jnp.sum(norm_grad, axis=0),
        ),
        "ctx",
    )
    ln_grads = jnp.stack([gain_sum, bias_sum]) * grad_scale
    owners = owner_map[0]
    image_count = owners.shape[0]
    image_rows = row_count // image_count
    slot_of = slot_numbers(owners, 1)
    images = visual.reshape(image_count, image_rows, visual.shape[1])
    slot_ids = jnp.arange(tp_count)[:, None, None]
    outgoing = jnp.zeros((), jnp.bfloat16)
    for i in range(image_count):
        outgoing = jnp.where(slot_ids == slot_of[i], images[i][None], outgoing)
    outgoing = outgoing.reshape(tp_count * image_rows, visual.shape[1])
    vit_grad = lax.all_to_all(outgoing, "tp", split_axis=0, concat_axis=1, tiled=True)
    return (grad_w2, grad_w1, bias_up * grad_scale, bias_down * grad_scale, ln_grads, vit_grad)


def solution(mesh):
    return jax.shard_map(
        per_device,
        mesh=mesh,
        in_specs=(
            P("ctx", "tp"),
            P("ctx", "tp"),
            P("ctx", "tp"),
            P("ctx"),
            P(None, "tp"),
            P(None, "tp"),
            P("tp"),
            P("ctx", None),
        ),
        out_specs=(
            P("ctx", "tp"),
            P("ctx", "tp"),
            P("tp"),
            P("tp"),
            P(None, "tp"),
            P(("ctx", "tp"), None),
        ),
        check_vma=False,
    )
```

```python
import functools
import math

import jax
import jax.numpy as jnp
from jax import lax
from jax.experimental import pallas as pl
from jax.experimental.pallas import tpu as pltpu
from jax.sharding import PartitionSpec as P

MESH = pl.DeviceIdType.MESH
SIDE = 4
TP = SIDE * SIDE
RINGS = 4
SUBS = 2
VMEM_LIMIT = 60 * 2**20


def gelu_parts(linear):
    normal_cdf = 0.5 * (1.0 + lax.erf(linear * 2.0 ** (-0.5)))
    density = jnp.exp(-0.5 * linear * linear) * (2.0 * math.pi) ** (-0.5)
    return (linear * normal_cdf, normal_cdf + linear * density)


def dot(left, right):
    return lax.dot_general(
        left, right, (((1,), (0,)), ((), ())), preferred_element_type=jnp.float32
    )


def row_product(left, right):
    return lax.dot_general(
        left, right, (((0,), (0,)), ((), ())), preferred_element_type=jnp.float32
    )


def dot_last(left, right):
    return lax.dot_general(
        left, right, (((1,), (1,)), ((), ())), preferred_element_type=jnp.float32
    )


class Rings:
    def __init__(self, me):
        z, y = me // SIDE, me % SIDE
        b = (y + z) % SIDE
        last, first = b // 3, (3 - b) // 3

        def at(zz, yy):
            return ((zz + SIDE) % SIDE) * SIDE + (yy + SIDE) % SIDE

        self.positions = (z * SIDE + b, y * SIDE + b)
        self.targets = (
            at(z + last, y + 1 - last),
            at(z - first, y - 1 + first),
            at(z + 1 - last, y + last),
            at(z - 1 + first, y - first),
        )

    def origin(self, ring, step):
        signed = step if ring % 2 else TP - step
        q = (self.positions[ring // 2] + signed) % TP
        major, minor = q // SIDE, (q % SIDE - q // SIDE + SIDE) % SIDE
        return major * SIDE + minor if ring < 2 else minor * SIDE + major


def greet(targets):
    barrier = pltpu.get_barrier_semaphore()
    for target in targets:
        pl.semaphore_signal(barrier, inc=1, device_id={"tp": target}, device_id_type=MESH)
    pl.semaphore_wait(barrier, len(targets))


def ring_gather(prepare, rings, full_ref, send_sem, recv_sem, consume):
    quarter = full_ref.shape[1] // RINGS
    part = quarter // SUBS

    def copy(ring, step, sub, at):
        spot = full_ref.at[rings.origin(ring, at), pl.ds(ring * quarter + sub * part, part)]
        return pltpu.make_async_remote_copy(
            src_ref=spot,
            dst_ref=spot,
            send_sem=send_sem.at[ring, step, sub],
            recv_sem=recv_sem.at[ring, step, sub],
            device_id={"tp": rings.targets[ring]},
            device_id_type=MESH,
        )

    for sub in range(SUBS):
        for ring in range(RINGS):
            copy(ring, 0, sub, 0).start()
    prepare()

    def hop(step, carry):
        for sub in range(SUBS):
            for ring in range(RINGS):
                copy(ring, step - 1, sub, step).wait_recv()
                copy(ring, step, sub, step).start()
            for ring in range(RINGS // SUBS * sub, RINGS // SUBS * (sub + 1)):
                consume(rings.origin(ring, step - 1), ring)
        return carry

    lax.fori_loop(1, TP - 1, hop, 0)
    for ring in range(RINGS):
        consume(rings.origin(ring, TP - 2), ring)
    for ring in range(RINGS):
        for sub in range(SUBS):
            copy(ring, TP - 2, sub, TP - 1).wait_recv()
        consume(rings.origin(ring, TP - 1), ring)

    def drain(step, carry):
        for sub in range(SUBS):
            for ring in range(RINGS):
                copy(ring, step, sub, step).wait_send()
        return carry

    lax.fori_loop(0, TP - 1, drain, 0)


def down_kernel(
    grad_ref, w_hbm, pre_ref, part_ref, gw2_ref, bias_ref, full_ref, w_ref, total, gw2, hidden, slope, w_sem, send_sem, recv_sem
):
    me = lax.axis_index("tp")
    rings = Rings(me)
    load = pltpu.make_async_copy(w_hbm, w_ref, w_sem)
    load.start()
    full_ref[me] = grad_ref[...]
    greet(rings.targets)
    rows_all, width = grad_ref.shape
    quarter = rows_all // RINGS

    def prepare():
        def rows_of(i, carry):
            rows = pl.ds(pl.multiple_of(i * 64, 64), 64)
            value, steep = gelu_parts(pre_ref[rows, :].astype(jnp.float32))
            hidden[rows, :] = value.astype(jnp.bfloat16)
            slope[rows, :] = steep
            return carry

        lax.fori_loop(0, rows_all // 64, rows_of, 0)
        bias_ref[0:1, :] = jnp.sum(grad_ref[...].astype(jnp.float32), axis=0, keepdims=True)
        total[...] = jnp.zeros_like(total)
        gw2[...] = jnp.zeros_like(gw2)
        load.wait()

    def consume(origin, ring):
        rows = pl.ds(ring * quarter, quarter)
        features = pl.ds(pl.multiple_of(origin * width, width), width)
        block = full_ref[origin, rows, :]
        total[rows, :] += dot(block, w_ref[features, :])
        gw2[features, :] += row_product(block, hidden[rows, :])

    ring_gather(prepare, rings, full_ref, send_sem, recv_sem, consume)
    part = (total[...] * slope[...]).astype(jnp.bfloat16)
    part_ref[...] = part
    bias_ref[1:2, :] = jnp.sum(part.astype(jnp.float32), axis=0, keepdims=True)
    gw2_ref[...] = gw2[...].astype(jnp.bfloat16)


def down(out_grad, w_down, pre_act):
    rows, width = out_grad.shape
    features, hid = w_down.shape
    vmem = pl.BlockSpec(memory_space=pltpu.VMEM)
    return pl.pallas_call(
        down_kernel,
        out_shape=(
            jax.ShapeDtypeStruct((rows, hid), jnp.bfloat16),
            jax.ShapeDtypeStruct((features, hid), jnp.bfloat16),
            jax.ShapeDtypeStruct((2, hid), jnp.float32),
        ),
        in_specs=[vmem, pl.BlockSpec(memory_space=pl.ANY), vmem],
        out_specs=(vmem, vmem, vmem),
        scratch_shapes=[
            pltpu.VMEM((TP, rows, width), jnp.bfloat16),
            pltpu.VMEM((features, hid), jnp.bfloat16),
            pltpu.VMEM((rows, hid), jnp.float32),
            pltpu.VMEM((features, hid), jnp.float32),
            pltpu.VMEM((rows, hid), jnp.bfloat16),
            pltpu.VMEM((rows, hid), jnp.float32),
            pltpu.SemaphoreType.DMA,
            pltpu.SemaphoreType.DMA((RINGS, TP - 1, SUBS)),
            pltpu.SemaphoreType.DMA((RINGS, TP - 1, SUBS)),
        ],
        compiler_params=pltpu.CompilerParams(
            collective_id=0, has_side_effects=True, vmem_limit_bytes=VMEM_LIMIT
        ),
        name="down_ring",
    )(out_grad, w_down, pre_act)


def up_kernel(
    part_ref, w_hbm, normed_hbm, norm_ref, gw1_ref, full_ref, w_ref, normed_ref, gw1, w_sem, send_sem, recv_sem
):
    me = lax.axis_index("tp")
    rings = Rings(me)
    loads = [
        pltpu.make_async_copy(w_hbm, w_ref, w_sem.at[0]),
        pltpu.make_async_copy(normed_hbm, normed_ref, w_sem.at[1]),
    ]
    for load in loads:
        load.start()
    full_ref[me] = part_ref[...]
    greet(rings.targets)
    rows_all, width = part_ref.shape
    quarter = rows_all // RINGS
    per_owner = gw1.shape[2] // width

    def prepare():
        norm_ref[...] = jnp.zeros_like(norm_ref)
        gw1[...] = jnp.zeros_like(gw1)
        for load in loads:
            load.wait()

    def consume(origin, ring):
        rows = pl.ds(ring * quarter, quarter)
        units = pl.ds(pl.multiple_of(origin * width, width), width)
        within = pl.ds(pl.multiple_of(origin % per_owner * width, width), width)
        block = full_ref[origin, rows, :]
        norm_ref[:, rows] += dot_last(w_ref[:, units], block)
        gw1[origin // per_owner, :, within] += dot(normed_ref[:, rows], block)

    ring_gather(prepare, rings, full_ref, send_sem, recv_sem, consume)
    gw1_ref[...] = gw1[...].astype(jnp.bfloat16)


def up(back_part, w_up_t, normed_t, ctx_count):
    rows, width = back_part.shape
    channels, units = w_up_t.shape
    vmem = pl.BlockSpec(memory_space=pltpu.VMEM)
    anywhere = pl.BlockSpec(memory_space=pl.ANY)
    return pl.pallas_call(
        up_kernel,
        out_shape=(
            jax.ShapeDtypeStruct((channels, rows), jnp.float32),
            jax.ShapeDtypeStruct((ctx_count, channels, units // ctx_count), jnp.bfloat16),
        ),
        in_specs=[vmem, anywhere, anywhere],
        out_specs=(vmem, vmem),
        scratch_shapes=[
            pltpu.VMEM((TP, rows, width), jnp.bfloat16),
            pltpu.VMEM((channels, units), jnp.bfloat16),
            pltpu.VMEM((channels, rows), jnp.bfloat16),
            pltpu.VMEM((ctx_count, channels, units // ctx_count), jnp.float32),
            pltpu.SemaphoreType.DMA((2,)),
            pltpu.SemaphoreType.DMA((RINGS, TP - 1, SUBS)),
            pltpu.SemaphoreType.DMA((RINGS, TP - 1, SUBS)),
        ],
        compiler_params=pltpu.CompilerParams(
            collective_id=1, has_side_effects=True, vmem_limit_bytes=VMEM_LIMIT
        ),
        cost_estimate=pl.CostEstimate(
            flops=4 * rows * units * channels, bytes_accessed=20 * 2**20, transcendentals=0
        ),
        name="up_ring",
    )(back_part, w_up_t, normed_t)


HALVES = 2
LANES = 128


class Torus:
    def __init__(self, half, me):
        z, y = me // SIDE, me % SIDE
        self.half = half
        self.along, self.cross = (y, z) if half == 0 else (z, y)

    def place(self, along, cross):
        along, cross = along % SIDE, cross % SIDE
        return cross * SIDE + along if self.half == 0 else along * SIDE + cross


def hand_kernel(
    full_width,
    grad_scale,
    norm_ref,
    normed_ref,
    gain_ref,
    std_ref,
    owner_ref,
    bias_ref,
    ln_ref,
    up_ref,
    down_ref,
    out_ref,
    own_y, next_y, far_y, prev_y,
    own_z, next_z, far_z, prev_z,
    message,
    final,
    product,
    stats_y,
    stats_z,
    sums,
    near_send, near_recv, relay_send, relay_recv, cross_send, cross_recv, stat_send, stat_recv, sum_send, sum_recv,
):
    me = lax.axis_index("tp")
    group = lax.axis_index("ctx")
    ctx_count = sums.shape[0]
    torus = [Torus(half, me) for half in range(HALVES)]
    held = [[own_y, next_y, far_y, prev_y], [own_z, next_z, far_z, prev_z]]
    images, channels, _ = own_y.shape
    image_rows = norm_ref.shape[1] // images
    chunk = channels // 5

    def along_peer(half, d):
        t = torus[half]
        return t.place(t.along + d, t.cross)

    def cross_peer(half, d):
        t = torus[half]
        return t.place(t.along, t.cross + d)

    barrier = pltpu.get_barrier_semaphore()
    for half in range(HALVES):
        for d in range(1, SIDE):
            pl.semaphore_signal(barrier, inc=1, device_id={"tp": along_peer(half, d)}, device_id_type=MESH)
    for d in range(1, ctx_count):
        pl.semaphore_signal(barrier, inc=1, device_id={"ctx": (group + d) % ctx_count}, device_id_type=MESH)

    ones = jnp.ones((8, image_rows), jnp.float32)
    columns = [jnp.zeros((8, channels), jnp.float32)] * 2
    for i in range(images):
        rows = pl.ds(i * image_rows, image_rows)

        def some(k, carry):
            part = pl.ds(pl.multiple_of(k * chunk, chunk), chunk)
            value = norm_ref[part, rows]
            feature = normed_ref[part, rows].astype(jnp.float32)
            gained = gain_ref[part, :] * value
            both = value * feature
            product[part, :] = both
            return (
                carry[0] + jnp.sum(gained, axis=0, keepdims=True),
                carry[1] + jnp.sum(gained * feature, axis=0, keepdims=True),
            )

        zero = jnp.zeros((1, image_rows), jnp.float32)
        first, second = lax.fori_loop(0, 5, some, (zero, zero))
        stats_y[0, i : i + 1, :] = first
        stats_y[0, images + i : images + i + 1, :] = second
        columns = [
            total
            + lax.dot_general(
                ones,
                right,
                (((1,), (1,)), ((), ())),
                precision=lax.Precision.HIGHEST,
                preferred_element_type=jnp.float32,
            )
            for total, right in zip(columns, (product[...], norm_ref[:, rows]))
        ]
    sums[0, 0:1, 0:channels] = columns[0][0:1]
    sums[0, 1:2, 0:channels] = columns[1][0:1]
    sums[0, 2:4, 0 : bias_ref.shape[1]] = bias_ref[...]
    pl.semaphore_wait(barrier, HALVES * (SIDE - 1) + ctx_count - 1)

    def stat_copy(half, d):
        buffer = (stats_y, stats_z)[half]
        return pltpu.make_async_remote_copy(
            src_ref=buffer.at[0],
            dst_ref=buffer.at[d],
            send_sem=stat_send.at[half, d - 1],
            recv_sem=stat_recv.at[half, d - 1],
            device_id={"tp": along_peer(half, d)},
            device_id_type=MESH,
        )

    def sum_copy(d):
        return pltpu.make_async_remote_copy(
            src_ref=sums.at[0],
            dst_ref=sums.at[d],
            send_sem=sum_send.at[d - 1],
            recv_sem=sum_recv.at[d - 1],
            device_id={"ctx": (group + d) % ctx_count},
            device_id_type=MESH,
        )

    for d in range(1, SIDE):
        stat_copy(0, d).start()
    for d in range(1, SIDE):
        stat_copy(0, d).wait_recv()
    stats_z[0] = stats_y[0] + stats_y[1] + stats_y[2] + stats_y[3]
    for d in range(1, SIDE):
        stat_copy(1, d).start()
    for d in range(1, SIDE):
        stat_copy(1, d).wait_recv()
    means = (stats_z[0] + stats_z[1] + stats_z[2] + stats_z[3]) * (1.0 / full_width)

    def near(half, sign, pair):
        piece = pl.ds(pair * (images // 2), images // 2)
        return pltpu.make_async_remote_copy(
            src_ref=held[half][0].at[piece],
            dst_ref=held[half][3 if sign == 1 else 1].at[piece],
            send_sem=near_send.at[half, sign // 2, pair],
            recv_sem=near_recv.at[half, sign // 2, pair],
            device_id={"tp": along_peer(half, sign)},
            device_id_type=MESH,
        )

    def relay(half, sign):
        pair = sign // 2
        piece = pl.ds(pair * (images // 2), images // 2)
        return pltpu.make_async_remote_copy(
            src_ref=held[half][3 if sign == 1 else 1].at[piece],
            dst_ref=held[half][2].at[piece],
            send_sem=relay_send.at[half, pair],
            recv_sem=relay_recv.at[half, pair],
            device_id={"tp": along_peer(half, sign)},
            device_id_type=MESH,
        )

    def across(half, target, d):
        t = torus[half]
        slot = (t.along + d) % SIDE
        if half == 0:
            spot = final.at[0, t.cross, pl.ds(pl.multiple_of(slot * channels, 16), channels)]
        else:
            spot = final.at[1, slot, pl.ds(pl.multiple_of(t.cross * channels, 16), channels)]
        if target == 0:
            return spot
        return pltpu.make_async_remote_copy(
            src_ref=message.at[half, target - 1, d],
            dst_ref=spot,
            send_sem=cross_send.at[half, target - 1, d],
            recv_sem=cross_recv.at[half, target - 1, d],
            device_id={"tp": cross_peer(half, target)},
            device_id_type=MESH,
        )

    for i in range(images):
        rows = pl.ds(i * image_rows, image_rows)
        mean_first, mean_second = means[i : i + 1, :], means[images + i : images + i + 1, :]
        inverse = std_ref[:, rows]

        def visual(k, carry):
            part = pl.ds(pl.multiple_of(k * chunk, chunk), chunk)
            value = gain_ref[part, :] * norm_ref[part, rows]
            feature = normed_ref[part, rows].astype(jnp.float32)
            seen = (inverse * (value - mean_first - feature * mean_second)).astype(jnp.bfloat16)
            own_y[i, part, :] = seen[:, :LANES]
            own_z[i, part, :] = seen[:, LANES:]
            return carry

        lax.fori_loop(0, 5, visual, 0)
        if i % 2:
            for half in range(HALVES):
                near(half, 1, i // 2).start()
                near(half, 3, i // 2).start()
    for d in range(1, ctx_count):
        sum_copy(d).start()

    owners = [owner_ref[0, i] for i in range(images)]
    slots = []
    for i in range(images):
        earlier = jnp.int32(0)
        for j in range(i):
            earlier += (owners[j] == owners[i]).astype(jnp.int32)
        slots.append(owners[i] + earlier)

    def choice(place):
        source, present = jnp.int32(0), jnp.int32(0)
        for i in range(images):
            match = (slots[i] == place).astype(jnp.int32)
            source += i * match
            present += match
        return source, present

    chosen = [[choice(cross_peer(half, target)) for target in range(SIDE)] for half in range(HALVES)]

    def forward(half, d):
        block = held[half][d]
        for target in (2, 1, 3, 0):
            source, present = chosen[half][target]
            spot = across(half, 0, d) if target == 0 else message.at[half, target - 1, d]

            def pick(k, carry):
                part = pl.ds(pl.multiple_of(k * chunk, chunk), chunk)
                value = block[source, part, :]
                spot[part, :] = jnp.where(present > 0, value, jnp.zeros_like(value))
                return carry

            lax.fori_loop(0, 5, pick, 0)
            if target:
                across(half, target, d).start()

    for half in range(HALVES):
        forward(half, 0)
    for half in range(HALVES):
        near(half, 1, 0).wait_recv()
        relay(half, 1).start()
    for half in range(HALVES):
        near(half, 3, 1).wait_recv()
        relay(half, 3).start()
    for half in range(HALVES):
        near(half, 1, 1).wait_recv()
        forward(half, 3)
        near(half, 3, 0).wait_recv()
        forward(half, 1)
    for half in range(HALVES):
        relay(half, 1).wait_recv()
        relay(half, 3).wait_recv()
        forward(half, 2)

    for d in range(1, ctx_count):
        sum_copy(d).wait_recv()
    whole = sums[0]
    for d in range(1, ctx_count):
        whole = whole + sums[d]
    whole = whole * grad_scale
    ln_ref[...] = whole[0:2, 0:channels]
    down_ref[...] = whole[2:3, 0 : bias_ref.shape[1]]
    up_ref[...] = whole[3:4, 0 : bias_ref.shape[1]]

    wide = SIDE * channels

    def turn(half, z):
        def tile(k, carry):
            block = final[half, z, pl.ds(pl.multiple_of(k * LANES, LANES), LANES), :]
            at = pl.ds(pl.multiple_of(z * wide + k * LANES, LANES), LANES)
            out_ref[half * LANES : (half + 1) * LANES, at] = block.T
            return carry

        lax.fori_loop(0, wide // LANES, tile, 0)

    for d in (0, 3, 1, 2):
        if d == 0:
            turn(0, torus[0].cross)
        else:
            for e in range(SIDE):
                across(0, d, e).wait_recv()
            turn(0, (torus[0].cross - d + SIDE) % SIDE)
    for e in (0, 3, 1, 2):
        for d in range(1, SIDE):
            across(1, d, e).wait_recv()
        turn(1, (torus[1].along + e) % SIDE)

    for half in range(HALVES):
        for sign in (1, 3):
            for pair in range(2):
                near(half, sign, pair).wait_send()
            relay(half, sign).wait_send()
        for d in range(1, SIDE):
            stat_copy(half, d).wait_send()
            for e in range(SIDE):
                across(half, d, e).wait_send()
    for d in range(1, ctx_count):
        sum_copy(d).wait_send()


def hand_over(norm_t, normed_t, gain, inverse_std, owner_map, bias, full_width, grad_scale, ctx_count):
    channels, rows = norm_t.shape
    images = owner_map.shape[1]
    image_rows = rows // images
    width = bias.shape[1]
    vmem = pl.BlockSpec(memory_space=pltpu.VMEM)
    block = pltpu.VMEM((images, channels, LANES), jnp.bfloat16)
    dma = pltpu.SemaphoreType.DMA
    return pl.pallas_call(
        functools.partial(hand_kernel, full_width, grad_scale),
        out_shape=(
            jax.ShapeDtypeStruct((2, channels), jnp.float32),
            jax.ShapeDtypeStruct((1, width), jnp.float32),
            jax.ShapeDtypeStruct((1, width), jnp.float32),
            jax.ShapeDtypeStruct((image_rows, TP * channels), jnp.bfloat16),
        ),
        in_specs=[vmem, vmem, vmem, vmem, pl.BlockSpec(memory_space=pltpu.SMEM), vmem],
        out_specs=(vmem, vmem, vmem, vmem),
        scratch_shapes=[block] * 8
        + [
            pltpu.VMEM((HALVES, SIDE - 1, SIDE, channels, LANES), jnp.bfloat16),
            pltpu.VMEM((HALVES, SIDE, SIDE * channels, LANES), jnp.bfloat16),
            pltpu.VMEM((channels, image_rows), jnp.float32),
            pltpu.VMEM((SIDE, 2 * images, image_rows), jnp.float32),
            pltpu.VMEM((SIDE, 2 * images, image_rows), jnp.float32),
            pltpu.VMEM((ctx_count, 8, 1024), jnp.float32),
            dma((HALVES, 2, 2)),
            dma((HALVES, 2, 2)),
            dma((HALVES, 2)),
            dma((HALVES, 2)),
            dma((HALVES, SIDE - 1, SIDE)),
            dma((HALVES, SIDE - 1, SIDE)),
            dma((HALVES, SIDE - 1)),
            dma((HALVES, SIDE - 1)),
            dma((ctx_count - 1,)),
            dma((ctx_count - 1,)),
        ],
        compiler_params=pltpu.CompilerParams(
            collective_id=2, has_side_effects=True, vmem_limit_bytes=VMEM_LIMIT
        ),
        cost_estimate=pl.CostEstimate(
            flops=20 * rows * channels, bytes_accessed=200 * 2**20, transcendentals=0
        ),
        name="hand_over",
    )(norm_t, normed_t, gain, inverse_std, owner_map, bias)


def per_device(out_grad, pre_act, normed, inverse_std, w_up, w_down, ln_gain, owner_map):
    ctx_count = lax.axis_size("ctx")
    tp_count = lax.axis_size("tp")
    row_count = out_grad.shape[0]
    grad_scale = float(row_count * ctx_count) ** (-0.5)
    back_part, gw2, bias = down(out_grad, w_down, pre_act)
    grad_w2 = (
        lax.psum_scatter(gw2, "ctx", scatter_dimension=0, tiled=True).astype(jnp.float32) * grad_scale
    )
    normed_t = normed.T
    norm_t, gw1 = up(back_part, w_up.T, normed_t, ctx_count)
    grad_w1_t = lax.psum_scatter(gw1, "ctx", scatter_dimension=0, tiled=True)
    grad_w1 = (grad_w1_t[0].astype(jnp.float32) * grad_scale).T
    ln_grads, bias_up, bias_down, vit_grad = hand_over(
        norm_t,
        normed_t,
        ln_gain[:, None],
        inverse_std[None, :],
        owner_map,
        bias,
        float(normed.shape[1] * tp_count),
        grad_scale,
        ctx_count,
    )
    return (grad_w2, grad_w1, bias_up[0], bias_down[0], ln_grads, vit_grad)


def solution(mesh):
    return jax.shard_map(
        per_device,
        mesh=mesh,
        in_specs=(
            P("ctx", "tp"),
            P("ctx", "tp"),
            P("ctx", "tp"),
            P("ctx"),
            P(None, "tp"),
            P(None, "tp"),
            P("tp"),
            P("ctx", None),
        ),
        out_specs=(
            P("ctx", "tp"),
            P("ctx", "tp"),
            P("tp"),
            P("tp"),
            P(None, "tp"),
            P(("ctx", "tp"), None),
        ),
        check_vma=False,
    )
```

```python
import functools
import math

import jax
import jax.numpy as jnp
from jax import lax
from jax.experimental import pallas as pl
from jax.experimental.pallas import tpu as pltpu
from jax.sharding import PartitionSpec as P

MESH = pl.DeviceIdType.MESH
SIDE = 4
TP = SIDE * SIDE
VMEM_LIMIT = 60 * 2**20


def gelu_parts(linear):
    normal_cdf = 0.5 * (1.0 + lax.erf(linear * 2.0 ** (-0.5)))
    density = jnp.exp(-0.5 * linear * linear) * (2.0 * math.pi) ** (-0.5)
    return (linear * normal_cdf, normal_cdf + linear * density)


def dot(left, right):
    return lax.dot_general(
        left, right, (((1,), (0,)), ((), ())), preferred_element_type=jnp.float32
    )


def row_product(left, right):
    return lax.dot_general(
        left, right, (((0,), (0,)), ((), ())), preferred_element_type=jnp.float32
    )


def dot_last(left, right):
    return lax.dot_general(
        left, right, (((1,), (1,)), ((), ())), preferred_element_type=jnp.float32
    )


def around(half, me):
    t = Torus(half, me)
    return ((t.along + 1, t.cross), (t.along + SIDE - 1, t.cross))


def greet(targets):
    barrier = pltpu.get_barrier_semaphore()
    for target in targets:
        pl.semaphore_signal(barrier, inc=1, device_id={"tp": target}, device_id_type=MESH)
    pl.semaphore_wait(barrier, len(targets))


class Torus:
    def __init__(self, half, me):
        z, y = me // SIDE, me % SIDE
        self.half = half
        self.along, self.cross = (y, z) if half == 0 else (z, y)

    def place(self, along, cross):
        along, cross = along % SIDE, cross % SIDE
        return cross * SIDE + along if self.half == 0 else along * SIDE + cross


QUARTERS = 4
ARRIVALS = (
    (3, 0), (1, 0), (0, 3), (2, 0), (3, 3), (1, 3), (0, 1), (2, 3),
    (3, 1), (0, 2), (1, 1), (3, 2), (2, 1), (1, 2), (2, 2),
)


def numbered(values, index):
    out = jnp.int32(values[0])
    for i, value in enumerate(values[1:], 1):
        out = jnp.where(index == i, jnp.int32(value), out)
    return out


def tree_gather(prepare, me, full_ref, send_sem, recv_sem, consume):
    rows = full_ref.shape[1] // QUARTERS
    torus = [Torus(half, me) for half in range(2)]

    def origin(quarter, along, cross):
        t, sign = torus[quarter // 2], 1 - quarter % 2 * 2
        return t.place(t.along + sign * along + SIDE, t.cross + sign * cross + SIDE)

    def copy(quarter, block, number, target):
        spot = full_ref.at[origin(quarter, *block), pl.ds(quarter * rows, rows)]
        return pltpu.make_async_remote_copy(
            src_ref=spot,
            dst_ref=spot,
            send_sem=send_sem.at[quarter, number],
            recv_sem=recv_sem.at[quarter, number],
            device_id={"tp": origin(quarter, *target)},
            device_id_type=MESH,
        )

    def send(block, seen):
        target = ((block[0] - seen[0]) % SIDE, (block[1] - seen[1]) % SIDE)
        for quarter in range(QUARTERS):
            copy(quarter, block, ARRIVALS.index(seen), target).start()

    send((0, 0), (3, 0))
    send((0, 0), (1, 0))
    send((0, 0), (0, 3))
    send((0, 0), (0, 1))
    prepare()
    for quarter in range(QUARTERS):
        consume(me, quarter)

    def arrive(k, carry):
        along = numbered([block[0] for block in ARRIVALS], k)
        cross = numbered([block[1] for block in ARRIVALS], k)
        for quarter in range(QUARTERS):
            copy(quarter, (along, cross), k, (1, 0)).wait_recv()
        for number, block in enumerate(ARRIVALS):
            if block[1] not in (0, 3):
                continue

            @pl.when(k == number)
            def _():
                if block == (3, 0):
                    send(block, (2, 0))
                if block[1] == 0:
                    send(block, (block[0], 3))
                    send(block, (block[0], 1))
                else:
                    send(block, (block[0], 2))

        for quarter in range(QUARTERS):
            consume(origin(quarter, along, cross), quarter)
        return carry

    lax.fori_loop(0, TP - 1, arrive, 0)

    def drain(k, carry):
        for quarter in range(QUARTERS):
            copy(quarter, (0, 0), k, (1, 0)).wait_send()
        return carry

    lax.fori_loop(0, TP - 1, drain, 0)


def down_kernel(
    grad_ref, w_hbm, pre_ref, part_ref, gw2_ref, bias_ref, full_ref, w_ref, total, gw2, hidden, slope, w_sem, send_sem, recv_sem
):
    me = lax.axis_index("tp")
    load = pltpu.make_async_copy(w_hbm, w_ref, w_sem)
    load.start()
    full_ref[me] = grad_ref[...]
    greet([Torus(half, me).place(*at) for half in range(2) for at in around(half, me)])
    rows_all, width = grad_ref.shape
    quarter = rows_all // QUARTERS

    def prepare():
        def rows_of(i, carry):
            rows = pl.ds(pl.multiple_of(i * 64, 64), 64)
            value, steep = gelu_parts(pre_ref[rows, :].astype(jnp.float32))
            hidden[rows, :] = value.astype(jnp.bfloat16)
            slope[rows, :] = steep
            return carry

        lax.fori_loop(0, rows_all // 64, rows_of, 0)
        bias_ref[0:1, :] = jnp.sum(grad_ref[...].astype(jnp.float32), axis=0, keepdims=True)
        total[...] = jnp.zeros_like(total)
        gw2[...] = jnp.zeros_like(gw2)
        load.wait()

    def consume(origin, part):
        rows = pl.ds(part * quarter, quarter)
        features = pl.ds(pl.multiple_of(origin * width, width), width)
        block = full_ref[origin, rows, :]
        total[rows, :] += dot(block, w_ref[features, :])
        gw2[features, :] += row_product(block, hidden[rows, :])

    tree_gather(prepare, me, full_ref, send_sem, recv_sem, consume)
    part = (total[...] * slope[...]).astype(jnp.bfloat16)
    part_ref[...] = part
    bias_ref[1:2, :] = jnp.sum(part.astype(jnp.float32), axis=0, keepdims=True)
    gw2_ref[...] = gw2[...].astype(jnp.bfloat16)


def down(out_grad, w_down, pre_act):
    rows, width = out_grad.shape
    features, hid = w_down.shape
    vmem = pl.BlockSpec(memory_space=pltpu.VMEM)
    return pl.pallas_call(
        down_kernel,
        out_shape=(
            jax.ShapeDtypeStruct((rows, hid), jnp.bfloat16),
            jax.ShapeDtypeStruct((features, hid), jnp.bfloat16),
            jax.ShapeDtypeStruct((2, hid), jnp.float32),
        ),
        in_specs=[vmem, pl.BlockSpec(memory_space=pl.ANY), vmem],
        out_specs=(vmem, vmem, vmem),
        scratch_shapes=[
            pltpu.VMEM((TP, rows, width), jnp.bfloat16),
            pltpu.VMEM((features, hid), jnp.bfloat16),
            pltpu.VMEM((rows, hid), jnp.float32),
            pltpu.VMEM((features, hid), jnp.float32),
            pltpu.VMEM((rows, hid), jnp.bfloat16),
            pltpu.VMEM((rows, hid), jnp.float32),
            pltpu.SemaphoreType.DMA,
            pltpu.SemaphoreType.DMA((QUARTERS, TP - 1)),
            pltpu.SemaphoreType.DMA((QUARTERS, TP - 1)),
        ],
        compiler_params=pltpu.CompilerParams(
            collective_id=0, has_side_effects=True, vmem_limit_bytes=VMEM_LIMIT
        ),
        name="down_gather",
    )(out_grad, w_down, pre_act)


def up_kernel(
    part_ref, w_hbm, normed_hbm, norm_ref, gw1_ref, full_ref, w_ref, normed_ref, gw1, w_sem, send_sem, recv_sem
):
    me = lax.axis_index("tp")
    loads = [
        pltpu.make_async_copy(w_hbm, w_ref, w_sem.at[0]),
        pltpu.make_async_copy(normed_hbm, normed_ref, w_sem.at[1]),
    ]
    for load in loads:
        load.start()
    full_ref[me] = part_ref[...]
    greet([Torus(half, me).place(*at) for half in range(2) for at in around(half, me)])
    rows_all, width = part_ref.shape
    quarter = rows_all // QUARTERS
    per_owner = gw1.shape[2] // width

    def prepare():
        norm_ref[...] = jnp.zeros_like(norm_ref)
        gw1[...] = jnp.zeros_like(gw1)
        for load in loads:
            load.wait()

    def consume(origin, part):
        rows = pl.ds(part * quarter, quarter)
        units = pl.ds(pl.multiple_of(origin * width, width), width)
        within = pl.ds(pl.multiple_of(origin % per_owner * width, width), width)
        block = full_ref[origin, rows, :]
        norm_ref[:, rows] += dot_last(w_ref[:, units], block)
        gw1[origin // per_owner, :, within] += dot(normed_ref[:, rows], block)

    tree_gather(prepare, me, full_ref, send_sem, recv_sem, consume)
    gw1_ref[...] = gw1[...].astype(jnp.bfloat16)


def up(back_part, w_up_t, normed_t, ctx_count):
    rows, width = back_part.shape
    channels, units = w_up_t.shape
    vmem = pl.BlockSpec(memory_space=pltpu.VMEM)
    anywhere = pl.BlockSpec(memory_space=pl.ANY)
    return pl.pallas_call(
        up_kernel,
        out_shape=(
            jax.ShapeDtypeStruct((channels, rows), jnp.float32),
            jax.ShapeDtypeStruct((ctx_count, channels, units // ctx_count), jnp.bfloat16),
        ),
        in_specs=[vmem, anywhere, anywhere],
        out_specs=(vmem, vmem),
        scratch_shapes=[
            pltpu.VMEM((TP, rows, width), jnp.bfloat16),
            pltpu.VMEM((channels, units), jnp.bfloat16),
            pltpu.VMEM((channels, rows), jnp.bfloat16),
            pltpu.VMEM((ctx_count, channels, units // ctx_count), jnp.float32),
            pltpu.SemaphoreType.DMA((2,)),
            pltpu.SemaphoreType.DMA((QUARTERS, TP - 1)),
            pltpu.SemaphoreType.DMA((QUARTERS, TP - 1)),
        ],
        compiler_params=pltpu.CompilerParams(
            collective_id=1, has_side_effects=True, vmem_limit_bytes=VMEM_LIMIT
        ),
        cost_estimate=pl.CostEstimate(
            flops=4 * rows * units * channels, bytes_accessed=20 * 2**20, transcendentals=0
        ),
        name="up_gather",
    )(back_part, w_up_t, normed_t)


HALVES = 2
LANES = 128


def hand_kernel(
    full_width,
    grad_scale,
    norm_ref,
    normed_ref,
    gain_ref,
    std_ref,
    owner_ref,
    bias_ref,
    ln_ref,
    up_ref,
    down_ref,
    out_ref,
    own_y, next_y, far_y, prev_y,
    own_z, next_z, far_z, prev_z,
    message,
    final,
    product,
    stats_y,
    stats_z,
    sums,
    near_send, near_recv, relay_send, relay_recv, cross_send, cross_recv, stat_send, stat_recv, sum_send, sum_recv,
):
    me = lax.axis_index("tp")
    group = lax.axis_index("ctx")
    ctx_count = sums.shape[0]
    torus = [Torus(half, me) for half in range(HALVES)]
    held = [[own_y, next_y, far_y, prev_y], [own_z, next_z, far_z, prev_z]]
    images, channels, _ = own_y.shape
    image_rows = norm_ref.shape[1] // images
    chunk = channels // 5

    def along_peer(half, d):
        t = torus[half]
        return t.place(t.along + d, t.cross)

    def cross_peer(half, d):
        t = torus[half]
        return t.place(t.along, t.cross + d)

    barrier = pltpu.get_barrier_semaphore()
    for half in range(HALVES):
        for d in range(1, SIDE):
            pl.semaphore_signal(barrier, inc=1, device_id={"tp": along_peer(half, d)}, device_id_type=MESH)
    for d in range(1, ctx_count):
        pl.semaphore_signal(barrier, inc=1, device_id={"ctx": (group + d) % ctx_count}, device_id_type=MESH)

    ones = jnp.ones((8, image_rows), jnp.float32)
    columns = [jnp.zeros((8, channels), jnp.float32)] * 2
    for i in range(images):
        rows = pl.ds(i * image_rows, image_rows)

        def some(k, carry):
            part = pl.ds(pl.multiple_of(k * chunk, chunk), chunk)
            value = norm_ref[part, rows]
            feature = normed_ref[part, rows].astype(jnp.float32)
            gained = gain_ref[part, :] * value
            both = value * feature
            product[part, :] = both
            return (
                carry[0] + jnp.sum(gained, axis=0, keepdims=True),
                carry[1] + jnp.sum(gained * feature, axis=0, keepdims=True),
            )

        zero = jnp.zeros((1, image_rows), jnp.float32)
        first, second = lax.fori_loop(0, 5, some, (zero, zero))
        stats_y[0, i : i + 1, :] = first
        stats_y[0, images + i : images + i + 1, :] = second
        columns = [
            total
            + lax.dot_general(
                ones,
                right,
                (((1,), (1,)), ((), ())),
                precision=lax.Precision.HIGHEST,
                preferred_element_type=jnp.float32,
            )
            for total, right in zip(columns, (product[...], norm_ref[:, rows]))
        ]
    sums[0, 0:1, 0:channels] = columns[0][0:1]
    sums[0, 1:2, 0:channels] = columns[1][0:1]
    sums[0, 2:4, 0 : bias_ref.shape[1]] = bias_ref[...]
    pl.semaphore_wait(barrier, HALVES * (SIDE - 1) + ctx_count - 1)

    def stat_copy(half, d):
        buffer = (stats_y, stats_z)[half]
        return pltpu.make_async_remote_copy(
            src_ref=buffer.at[0],
            dst_ref=buffer.at[d],
            send_sem=stat_send.at[half, d - 1],
            recv_sem=stat_recv.at[half, d - 1],
            device_id={"tp": along_peer(half, d)},
            device_id_type=MESH,
        )

    def sum_copy(d):
        return pltpu.make_async_remote_copy(
            src_ref=sums.at[0],
            dst_ref=sums.at[d],
            send_sem=sum_send.at[d - 1],
            recv_sem=sum_recv.at[d - 1],
            device_id={"ctx": (group + d) % ctx_count},
            device_id_type=MESH,
        )

    for d in range(1, SIDE):
        stat_copy(0, d).start()
    for d in range(1, SIDE):
        stat_copy(0, d).wait_recv()
    stats_z[0] = stats_y[0] + stats_y[1] + stats_y[2] + stats_y[3]
    for d in range(1, SIDE):
        stat_copy(1, d).start()
    for d in range(1, SIDE):
        stat_copy(1, d).wait_recv()
    means = (stats_z[0] + stats_z[1] + stats_z[2] + stats_z[3]) * (1.0 / full_width)

    def near(half, sign, pair):
        piece = pl.ds(pair * (images // 2), images // 2)
        return pltpu.make_async_remote_copy(
            src_ref=held[half][0].at[piece],
            dst_ref=held[half][3 if sign == 1 else 1].at[piece],
            send_sem=near_send.at[half, sign // 2, pair],
            recv_sem=near_recv.at[half, sign // 2, pair],
            device_id={"tp": along_peer(half, sign)},
            device_id_type=MESH,
        )

    def relay(half, sign):
        pair = sign // 2
        piece = pl.ds(pair * (images // 2), images // 2)
        return pltpu.make_async_remote_copy(
            src_ref=held[half][3 if sign == 1 else 1].at[piece],
            dst_ref=held[half][2].at[piece],
            send_sem=relay_send.at[half, pair],
            recv_sem=relay_recv.at[half, pair],
            device_id={"tp": along_peer(half, sign)},
            device_id_type=MESH,
        )

    def across(half, target, d):
        t = torus[half]
        slot = (t.along + d) % SIDE
        if half == 0:
            spot = final.at[0, t.cross, pl.ds(pl.multiple_of(slot * channels, 16), channels)]
        else:
            spot = final.at[1, slot, pl.ds(pl.multiple_of(t.cross * channels, 16), channels)]
        if target == 0:
            return spot
        return pltpu.make_async_remote_copy(
            src_ref=message.at[half, target - 1, d],
            dst_ref=spot,
            send_sem=cross_send.at[half, target - 1, d],
            recv_sem=cross_recv.at[half, target - 1, d],
            device_id={"tp": cross_peer(half, target)},
            device_id_type=MESH,
        )

    for i in range(images):
        rows = pl.ds(i * image_rows, image_rows)
        mean_first, mean_second = means[i : i + 1, :], means[images + i : images + i + 1, :]
        inverse = std_ref[:, rows]

        def visual(k, carry):
            part = pl.ds(pl.multiple_of(k * chunk, chunk), chunk)
            value = gain_ref[part, :] * norm_ref[part, rows]
            feature = normed_ref[part, rows].astype(jnp.float32)
            seen = (inverse * (value - mean_first - feature * mean_second)).astype(jnp.bfloat16)
            own_y[i, part, :] = seen[:, :LANES]
            own_z[i, part, :] = seen[:, LANES:]
            return carry

        lax.fori_loop(0, 5, visual, 0)
        if i % 2:
            for half in range(HALVES):
                near(half, 1, i // 2).start()
                near(half, 3, i // 2).start()
    for d in range(1, ctx_count):
        sum_copy(d).start()

    owners = [owner_ref[0, i] for i in range(images)]
    slots = []
    for i in range(images):
        earlier = jnp.int32(0)
        for j in range(i):
            earlier += (owners[j] == owners[i]).astype(jnp.int32)
        slots.append(owners[i] + earlier)

    def choice(place):
        source, present = jnp.int32(0), jnp.int32(0)
        for i in range(images):
            match = (slots[i] == place).astype(jnp.int32)
            source += i * match
            present += match
        return source, present

    chosen = [[choice(cross_peer(half, target)) for target in range(SIDE)] for half in range(HALVES)]

    def forward(half, d):
        block = held[half][d]
        for target in (2, 1, 3, 0):
            source, present = chosen[half][target]
            spot = across(half, 0, d) if target == 0 else message.at[half, target - 1, d]

            def pick(k, carry):
                part = pl.ds(pl.multiple_of(k * chunk, chunk), chunk)
                value = block[source, part, :]
                spot[part, :] = jnp.where(present > 0, value, jnp.zeros_like(value))
                return carry

            lax.fori_loop(0, 5, pick, 0)
            if target:
                across(half, target, d).start()

    for half in range(HALVES):
        forward(half, 0)
    for half in range(HALVES):
        near(half, 1, 0).wait_recv()
        relay(half, 1).start()
    for half in range(HALVES):
        near(half, 3, 1).wait_recv()
        relay(half, 3).start()
    for half in range(HALVES):
        near(half, 1, 1).wait_recv()
        forward(half, 3)
        near(half, 3, 0).wait_recv()
        forward(half, 1)
    for half in range(HALVES):
        relay(half, 1).wait_recv()
        relay(half, 3).wait_recv()
        forward(half, 2)

    for d in range(1, ctx_count):
        sum_copy(d).wait_recv()
    whole = sums[0]
    for d in range(1, ctx_count):
        whole = whole + sums[d]
    whole = whole * grad_scale
    ln_ref[...] = whole[0:2, 0:channels]
    down_ref[...] = whole[2:3, 0 : bias_ref.shape[1]]
    up_ref[...] = whole[3:4, 0 : bias_ref.shape[1]]

    wide = SIDE * channels

    def turn(half, z):
        def tile(k, carry):
            block = final[half, z, pl.ds(pl.multiple_of(k * LANES, LANES), LANES), :]
            at = pl.ds(pl.multiple_of(z * wide + k * LANES, LANES), LANES)
            out_ref[half * LANES : (half + 1) * LANES, at] = block.T
            return carry

        lax.fori_loop(0, wide // LANES, tile, 0)

    for d in (0, 3, 1, 2):
        if d == 0:
            turn(0, torus[0].cross)
        else:
            for e in range(SIDE):
                across(0, d, e).wait_recv()
            turn(0, (torus[0].cross - d + SIDE) % SIDE)
    for e in (0, 3, 1, 2):
        for d in range(1, SIDE):
            across(1, d, e).wait_recv()
        turn(1, (torus[1].along + e) % SIDE)

    for half in range(HALVES):
        for sign in (1, 3):
            for pair in range(2):
                near(half, sign, pair).wait_send()
            relay(half, sign).wait_send()
        for d in range(1, SIDE):
            stat_copy(half, d).wait_send()
            for e in range(SIDE):
                across(half, d, e).wait_send()
    for d in range(1, ctx_count):
        sum_copy(d).wait_send()


def hand_over(norm_t, normed_t, gain, inverse_std, owner_map, bias, full_width, grad_scale, ctx_count):
    channels, rows = norm_t.shape
    images = owner_map.shape[1]
    image_rows = rows // images
    width = bias.shape[1]
    vmem = pl.BlockSpec(memory_space=pltpu.VMEM)
    block = pltpu.VMEM((images, channels, LANES), jnp.bfloat16)
    dma = pltpu.SemaphoreType.DMA
    return pl.pallas_call(
        functools.partial(hand_kernel, full_width, grad_scale),
        out_shape=(
            jax.ShapeDtypeStruct((2, channels), jnp.float32),
            jax.ShapeDtypeStruct((1, width), jnp.float32),
            jax.ShapeDtypeStruct((1, width), jnp.float32),
            jax.ShapeDtypeStruct((image_rows, TP * channels), jnp.bfloat16),
        ),
        in_specs=[vmem, vmem, vmem, vmem, pl.BlockSpec(memory_space=pltpu.SMEM), vmem],
        out_specs=(vmem, vmem, vmem, vmem),
        scratch_shapes=[block] * 8
        + [
            pltpu.VMEM((HALVES, SIDE - 1, SIDE, channels, LANES), jnp.bfloat16),
            pltpu.VMEM((HALVES, SIDE, SIDE * channels, LANES), jnp.bfloat16),
            pltpu.VMEM((channels, image_rows), jnp.float32),
            pltpu.VMEM((SIDE, 2 * images, image_rows), jnp.float32),
            pltpu.VMEM((SIDE, 2 * images, image_rows), jnp.float32),
            pltpu.VMEM((ctx_count, 8, 1024), jnp.float32),
            dma((HALVES, 2, 2)),
            dma((HALVES, 2, 2)),
            dma((HALVES, 2)),
            dma((HALVES, 2)),
            dma((HALVES, SIDE - 1, SIDE)),
            dma((HALVES, SIDE - 1, SIDE)),
            dma((HALVES, SIDE - 1)),
            dma((HALVES, SIDE - 1)),
            dma((ctx_count - 1,)),
            dma((ctx_count - 1,)),
        ],
        compiler_params=pltpu.CompilerParams(
            collective_id=2, has_side_effects=True, vmem_limit_bytes=VMEM_LIMIT
        ),
        cost_estimate=pl.CostEstimate(
            flops=20 * rows * channels, bytes_accessed=200 * 2**20, transcendentals=0
        ),
        name="hand_over",
    )(norm_t, normed_t, gain, inverse_std, owner_map, bias)


def per_device(out_grad, pre_act, normed, inverse_std, w_up, w_down, ln_gain, owner_map):
    ctx_count = lax.axis_size("ctx")
    tp_count = lax.axis_size("tp")
    row_count = out_grad.shape[0]
    grad_scale = float(row_count * ctx_count) ** (-0.5)
    back_part, gw2, bias = down(out_grad, w_down, pre_act)
    grad_w2 = (
        lax.psum_scatter(gw2, "ctx", scatter_dimension=0, tiled=True).astype(jnp.float32) * grad_scale
    )
    normed_t = normed.T
    norm_t, gw1 = up(back_part, w_up.T, normed_t, ctx_count)
    grad_w1_t = lax.psum_scatter(gw1, "ctx", scatter_dimension=0, tiled=True)
    grad_w1 = (grad_w1_t[0].astype(jnp.float32) * grad_scale).T
    ln_grads, bias_up, bias_down, vit_grad = hand_over(
        norm_t,
        normed_t,
        ln_gain[:, None],
        inverse_std[None, :],
        owner_map,
        bias,
        float(normed.shape[1] * tp_count),
        grad_scale,
        ctx_count,
    )
    return (grad_w2, grad_w1, bias_up[0], bias_down[0], ln_grads, vit_grad)


def solution(mesh):
    return jax.shard_map(
        per_device,
        mesh=mesh,
        in_specs=(
            P("ctx", "tp"),
            P("ctx", "tp"),
            P("ctx", "tp"),
            P("ctx"),
            P(None, "tp"),
            P(None, "tp"),
            P("tp"),
            P("ctx", None),
        ),
        out_specs=(
            P("ctx", "tp"),
            P("ctx", "tp"),
            P("tp"),
            P("tp"),
            P(None, "tp"),
            P(("ctx", "tp"), None),
        ),
        check_vma=False,
    )
```

```python
import functools
import math

import jax
import jax.numpy as jnp
from jax import lax
from jax.experimental import pallas as pl
from jax.experimental.pallas import tpu as pltpu
from jax.sharding import PartitionSpec as P

MESH = pl.DeviceIdType.MESH
SIDE = 4
TP = SIDE * SIDE
VMEM_LIMIT = 60 * 2**20


def gelu_parts(linear):
    normal_cdf = 0.5 * (1.0 + lax.erf(linear * 2.0 ** (-0.5)))
    density = jnp.exp(-0.5 * linear * linear) * (2.0 * math.pi) ** (-0.5)
    return (linear * normal_cdf, normal_cdf + linear * density)


def dot(left, right):
    return lax.dot_general(
        left, right, (((1,), (0,)), ((), ())), preferred_element_type=jnp.float32
    )


def row_product(left, right):
    return lax.dot_general(
        left, right, (((0,), (0,)), ((), ())), preferred_element_type=jnp.float32
    )


def dot_last(left, right):
    return lax.dot_general(
        left, right, (((1,), (1,)), ((), ())), preferred_element_type=jnp.float32
    )


def around(half, me):
    t = Torus(half, me)
    return ((t.along + 1, t.cross), (t.along + SIDE - 1, t.cross))


def greet(targets):
    barrier = pltpu.get_barrier_semaphore()
    for target in targets:
        pl.semaphore_signal(barrier, inc=1, device_id={"tp": target}, device_id_type=MESH)
    pl.semaphore_wait(barrier, len(targets))


class Torus:
    def __init__(self, half, me):
        z, y = me // SIDE, me % SIDE
        self.half = half
        self.along, self.cross = (y, z) if half == 0 else (z, y)

    def place(self, along, cross):
        along, cross = along % SIDE, cross % SIDE
        return cross * SIDE + along if self.half == 0 else along * SIDE + cross


QUARTERS = 4
ARRIVALS = (
    (3, 0), (1, 0), (0, 3), (2, 0), (3, 3), (1, 3), (0, 1), (2, 3),
    (3, 1), (0, 2), (1, 1), (3, 2), (2, 1), (1, 2), (2, 2),
)


def numbered(values, index):
    out = jnp.int32(values[0])
    for i, value in enumerate(values[1:], 1):
        out = jnp.where(index == i, jnp.int32(value), out)
    return out


def tree_gather(prepare, me, full_ref, send_sem, recv_sem, consume):
    rows = full_ref.shape[1] // QUARTERS
    torus = [Torus(half, me) for half in range(2)]

    def origin(quarter, along, cross):
        t, sign = torus[quarter // 2], 1 - quarter % 2 * 2
        return t.place(t.along + sign * along + SIDE, t.cross + sign * cross + SIDE)

    def copy(quarter, block, number, target):
        spot = full_ref.at[origin(quarter, *block), pl.ds(quarter * rows, rows)]
        return pltpu.make_async_remote_copy(
            src_ref=spot,
            dst_ref=spot,
            send_sem=send_sem.at[quarter, number],
            recv_sem=recv_sem.at[quarter, number],
            device_id={"tp": origin(quarter, *target)},
            device_id_type=MESH,
        )

    def send(block, seen):
        target = ((block[0] - seen[0]) % SIDE, (block[1] - seen[1]) % SIDE)
        for quarter in range(QUARTERS):
            copy(quarter, block, ARRIVALS.index(seen), target).start()

    send((0, 0), (3, 0))
    send((0, 0), (1, 0))
    send((0, 0), (0, 3))
    send((0, 0), (0, 1))
    prepare()
    for quarter in range(QUARTERS):
        consume(me, quarter)

    def arrive(k, carry):
        along = numbered([block[0] for block in ARRIVALS], k)
        cross = numbered([block[1] for block in ARRIVALS], k)
        for quarter in range(QUARTERS):
            copy(quarter, (along, cross), k, (1, 0)).wait_recv()
        for number, block in enumerate(ARRIVALS):
            if block[1] not in (0, 3):
                continue

            @pl.when(k == number)
            def _():
                if block == (3, 0):
                    send(block, (2, 0))
                if block[1] == 0:
                    send(block, (block[0], 3))
                    send(block, (block[0], 1))
                else:
                    send(block, (block[0], 2))

        for quarter in range(QUARTERS):
            consume(origin(quarter, along, cross), quarter)
        return carry

    lax.fori_loop(0, TP - 1, arrive, 0)

    def drain(k, carry):
        for quarter in range(QUARTERS):
            copy(quarter, (0, 0), k, (1, 0)).wait_send()
        return carry

    lax.fori_loop(0, TP - 1, drain, 0)


def down_kernel(
    grad_ref, w_hbm, pre_ref, part_ref, gw2_ref, bias_ref, full_ref, w_ref, total, gw2, hidden, slope, w_sem, send_sem, recv_sem
):
    me = lax.axis_index("tp")
    load = pltpu.make_async_copy(w_hbm, w_ref, w_sem)
    load.start()
    full_ref[me] = grad_ref[...]
    greet([Torus(half, me).place(*at) for half in range(2) for at in around(half, me)])
    rows_all, width = grad_ref.shape
    quarter = rows_all // QUARTERS

    def prepare():
        def rows_of(i, carry):
            rows = pl.ds(pl.multiple_of(i * 64, 64), 64)
            value, steep = gelu_parts(pre_ref[rows, :].astype(jnp.float32))
            hidden[rows, :] = value.astype(jnp.bfloat16)
            slope[rows, :] = steep
            return carry

        lax.fori_loop(0, rows_all // 64, rows_of, 0)
        bias_ref[0:1, :] = jnp.sum(grad_ref[...].astype(jnp.float32), axis=0, keepdims=True)
        total[...] = jnp.zeros_like(total)
        gw2[...] = jnp.zeros_like(gw2)
        load.wait()

    def consume(origin, part):
        rows = pl.ds(part * quarter, quarter)
        features = pl.ds(pl.multiple_of(origin * width, width), width)
        block = full_ref[origin, rows, :]
        total[rows, :] += dot(block, w_ref[features, :])
        gw2[features, :] += row_product(block, hidden[rows, :])

    tree_gather(prepare, me, full_ref, send_sem, recv_sem, consume)
    part = (total[...] * slope[...]).astype(jnp.bfloat16)
    part_ref[...] = part
    bias_ref[1:2, :] = jnp.sum(part.astype(jnp.float32), axis=0, keepdims=True)
    gw2_ref[...] = gw2[...].astype(jnp.bfloat16)


def down(out_grad, w_down, pre_act):
    rows, width = out_grad.shape
    features, hid = w_down.shape
    vmem = pl.BlockSpec(memory_space=pltpu.VMEM)
    return pl.pallas_call(
        down_kernel,
        out_shape=(
            jax.ShapeDtypeStruct((rows, hid), jnp.bfloat16),
            jax.ShapeDtypeStruct((features, hid), jnp.bfloat16),
            jax.ShapeDtypeStruct((2, hid), jnp.float32),
        ),
        in_specs=[vmem, pl.BlockSpec(memory_space=pl.ANY), vmem],
        out_specs=(vmem, vmem, vmem),
        scratch_shapes=[
            pltpu.VMEM((TP, rows, width), jnp.bfloat16),
            pltpu.VMEM((features, hid), jnp.bfloat16),
            pltpu.VMEM((rows, hid), jnp.float32),
            pltpu.VMEM((features, hid), jnp.float32),
            pltpu.VMEM((rows, hid), jnp.bfloat16),
            pltpu.VMEM((rows, hid), jnp.float32),
            pltpu.SemaphoreType.DMA,
            pltpu.SemaphoreType.DMA((QUARTERS, TP - 1)),
            pltpu.SemaphoreType.DMA((QUARTERS, TP - 1)),
        ],
        compiler_params=pltpu.CompilerParams(
            collective_id=0, has_side_effects=True, vmem_limit_bytes=VMEM_LIMIT
        ),
        name="down_gather",
    )(out_grad, w_down, pre_act)


def up_kernel(
    part_ref, w_hbm, normed_hbm, norm_ref, gw1_ref, full_ref, w_ref, normed_ref, gw1, w_sem, send_sem, recv_sem
):
    me = lax.axis_index("tp")
    loads = [
        pltpu.make_async_copy(w_hbm, w_ref, w_sem.at[0]),
        pltpu.make_async_copy(normed_hbm, normed_ref, w_sem.at[1]),
    ]
    for load in loads:
        load.start()
    full_ref[me] = part_ref[...]
    greet([Torus(half, me).place(*at) for half in range(2) for at in around(half, me)])
    rows_all, width = part_ref.shape
    quarter = rows_all // QUARTERS
    per_owner = gw1.shape[2] // width

    def prepare():
        norm_ref[...] = jnp.zeros_like(norm_ref)
        gw1[...] = jnp.zeros_like(gw1)
        for load in loads:
            load.wait()

    def consume(origin, part):
        rows = pl.ds(part * quarter, quarter)
        units = pl.ds(pl.multiple_of(origin * width, width), width)
        within = pl.ds(pl.multiple_of(origin % per_owner * width, width), width)
        block = full_ref[origin, rows, :]
        norm_ref[:, rows] += dot_last(w_ref[:, units], block)
        gw1[origin // per_owner, :, within] += dot(normed_ref[:, rows], block)

    tree_gather(prepare, me, full_ref, send_sem, recv_sem, consume)
    gw1_ref[...] = gw1[...].astype(jnp.bfloat16)


def up(back_part, w_up_t, normed_t, ctx_count):
    rows, width = back_part.shape
    channels, units = w_up_t.shape
    vmem = pl.BlockSpec(memory_space=pltpu.VMEM)
    anywhere = pl.BlockSpec(memory_space=pl.ANY)
    return pl.pallas_call(
        up_kernel,
        out_shape=(
            jax.ShapeDtypeStruct((channels, rows), jnp.float32),
            jax.ShapeDtypeStruct((ctx_count, channels, units // ctx_count), jnp.bfloat16),
        ),
        in_specs=[vmem, anywhere, anywhere],
        out_specs=(vmem, vmem),
        scratch_shapes=[
            pltpu.VMEM((TP, rows, width), jnp.bfloat16),
            pltpu.VMEM((channels, units), jnp.bfloat16),
            pltpu.VMEM((channels, rows), jnp.bfloat16),
            pltpu.VMEM((ctx_count, channels, units // ctx_count), jnp.float32),
            pltpu.SemaphoreType.DMA((2,)),
            pltpu.SemaphoreType.DMA((QUARTERS, TP - 1)),
            pltpu.SemaphoreType.DMA((QUARTERS, TP - 1)),
        ],
        compiler_params=pltpu.CompilerParams(
            collective_id=1, has_side_effects=True, vmem_limit_bytes=VMEM_LIMIT
        ),
        cost_estimate=pl.CostEstimate(
            flops=4 * rows * units * channels, bytes_accessed=20 * 2**20, transcendentals=0
        ),
        name="up_gather",
    )(back_part, w_up_t, normed_t)


HALVES = 2
LANES = 128


def hand_kernel(
    full_width,
    grad_scale,
    norm_ref,
    normed_ref,
    gain_ref,
    std_ref,
    owner_ref,
    bias_ref,
    sum_ref,
    final,
    own_y, next_y, far_y, prev_y,
    own_z, next_z, far_z, prev_z,
    message,
    product,
    stats_y,
    stats_z,
    sums,
    near_send, near_recv, relay_send, relay_recv, cross_send, cross_recv, own_sem, stat_send, stat_recv, sum_send, sum_recv,
):
    me = lax.axis_index("tp")
    group = lax.axis_index("ctx")
    ctx_count = sums.shape[0]
    torus = [Torus(half, me) for half in range(HALVES)]
    held = [[own_y, next_y, far_y, prev_y], [own_z, next_z, far_z, prev_z]]
    images, channels, _ = own_y.shape
    image_rows = norm_ref.shape[1] // images
    chunk = channels // 5

    def along_peer(half, d):
        t = torus[half]
        return t.place(t.along + d, t.cross)

    def cross_peer(half, d):
        t = torus[half]
        return t.place(t.along, t.cross + d)

    barrier = pltpu.get_barrier_semaphore()
    for half in range(HALVES):
        for d in range(1, SIDE):
            pl.semaphore_signal(barrier, inc=1, device_id={"tp": along_peer(half, d)}, device_id_type=MESH)
    for d in range(1, ctx_count):
        pl.semaphore_signal(barrier, inc=1, device_id={"ctx": (group + d) % ctx_count}, device_id_type=MESH)

    for i in range(images):
        rows = pl.ds(i * image_rows, image_rows)

        def some(k, carry):
            part = pl.ds(pl.multiple_of(k * chunk, chunk), chunk)
            feature = normed_ref[part, rows].astype(jnp.float32)
            gained = gain_ref[part, :] * norm_ref[part, rows]
            return (
                carry[0] + jnp.sum(gained, axis=0, keepdims=True),
                carry[1] + jnp.sum(gained * feature, axis=0, keepdims=True),
            )

        zero = jnp.zeros((1, image_rows), jnp.float32)
        first, second = lax.fori_loop(0, 5, some, (zero, zero))
        stats_y[0, i : i + 1, :] = first
        stats_y[0, images + i : images + i + 1, :] = second
    pl.semaphore_wait(barrier, HALVES * (SIDE - 1) + ctx_count - 1)

    def stat_copy(half, d):
        buffer = (stats_y, stats_z)[half]
        return pltpu.make_async_remote_copy(
            src_ref=buffer.at[0],
            dst_ref=buffer.at[d],
            send_sem=stat_send.at[half, d - 1],
            recv_sem=stat_recv.at[half, d - 1],
            device_id={"tp": along_peer(half, d)},
            device_id_type=MESH,
        )

    def sum_copy(d):
        return pltpu.make_async_remote_copy(
            src_ref=sums.at[0],
            dst_ref=sums.at[d],
            send_sem=sum_send.at[d - 1],
            recv_sem=sum_recv.at[d - 1],
            device_id={"ctx": (group + d) % ctx_count},
            device_id_type=MESH,
        )

    for d in range(1, SIDE):
        stat_copy(0, d).start()
    for d in range(1, SIDE):
        stat_copy(0, d).wait_recv()
    stats_z[0] = stats_y[0] + stats_y[1] + stats_y[2] + stats_y[3]
    for d in range(1, SIDE):
        stat_copy(1, d).start()
    for d in range(1, SIDE):
        stat_copy(1, d).wait_recv()
    means = (stats_z[0] + stats_z[1] + stats_z[2] + stats_z[3]) * (1.0 / full_width)

    def near(half, sign, pair):
        piece = pl.ds(pair * (images // 2), images // 2)
        return pltpu.make_async_remote_copy(
            src_ref=held[half][0].at[piece],
            dst_ref=held[half][3 if sign == 1 else 1].at[piece],
            send_sem=near_send.at[half, sign // 2, pair],
            recv_sem=near_recv.at[half, sign // 2, pair],
            device_id={"tp": along_peer(half, sign)},
            device_id_type=MESH,
        )

    def relay(half, sign):
        pair = sign // 2
        piece = pl.ds(pair * (images // 2), images // 2)
        return pltpu.make_async_remote_copy(
            src_ref=held[half][3 if sign == 1 else 1].at[piece],
            dst_ref=held[half][2].at[piece],
            send_sem=relay_send.at[half, pair],
            recv_sem=relay_recv.at[half, pair],
            device_id={"tp": along_peer(half, sign)},
            device_id_type=MESH,
        )

    def across(half, target, d):
        t = torus[half]
        slot = (t.along + d) % SIDE
        source = t.cross * SIDE + slot if half == 0 else slot * SIDE + t.cross
        spot = final.at[half, pl.ds(pl.multiple_of(source * channels, 16), channels)]
        if target == 0:
            return pltpu.make_async_copy(message.at[half, 0, d], spot, own_sem.at[half, d])
        return pltpu.make_async_remote_copy(
            src_ref=message.at[half, target, d],
            dst_ref=spot,
            send_sem=cross_send.at[half, target - 1, d],
            recv_sem=cross_recv.at[half, target - 1, d],
            device_id={"tp": cross_peer(half, target)},
            device_id_type=MESH,
        )

    for i in range(images):
        rows = pl.ds(i * image_rows, image_rows)
        mean_first, mean_second = means[i : i + 1, :], means[images + i : images + i + 1, :]
        inverse = std_ref[:, rows]

        def visual(k, carry):
            part = pl.ds(pl.multiple_of(k * chunk, chunk), chunk)
            value = gain_ref[part, :] * norm_ref[part, rows]
            feature = normed_ref[part, rows].astype(jnp.float32)
            seen = (inverse * (value - mean_first - feature * mean_second)).astype(jnp.bfloat16)
            own_y[i, part, :] = seen[:, :LANES]
            own_z[i, part, :] = seen[:, LANES:]
            return carry

        lax.fori_loop(0, 5, visual, 0)
        if i % 2:
            for half in range(HALVES):
                near(half, 1, i // 2).start()
                near(half, 3, i // 2).start()
    owners = [owner_ref[0, i] for i in range(images)]
    slots = []
    for i in range(images):
        earlier = jnp.int32(0)
        for j in range(i):
            earlier += (owners[j] == owners[i]).astype(jnp.int32)
        slots.append(owners[i] + earlier)

    def choice(place):
        source, present = jnp.int32(0), jnp.int32(0)
        for i in range(images):
            match = (slots[i] == place).astype(jnp.int32)
            source += i * match
            present += match
        return source, present

    chosen = [[choice(cross_peer(half, target)) for target in range(SIDE)] for half in range(HALVES)]

    def forward(half, d):
        block = held[half][d]
        for target in (2, 1, 3, 0):
            source, present = chosen[half][target]
            spot = message.at[half, target, d]

            def pick(k, carry):
                part = pl.ds(pl.multiple_of(k * chunk, chunk), chunk)
                value = block[source, part, :]
                spot[part, :] = jnp.where(present > 0, value, jnp.zeros_like(value))
                return carry

            lax.fori_loop(0, 5, pick, 0)
            across(half, target, d).start()

    for half in range(HALVES):
        forward(half, 0)
    for half in range(HALVES):
        near(half, 1, 0).wait_recv()
        relay(half, 1).start()
    for half in range(HALVES):
        near(half, 3, 1).wait_recv()
        relay(half, 3).start()
    for half in range(HALVES):
        near(half, 1, 1).wait_recv()
        forward(half, 3)
        near(half, 3, 0).wait_recv()
        forward(half, 1)

    ones = jnp.ones((8, image_rows), jnp.float32)
    columns = [jnp.zeros((8, channels), jnp.float32)] * 2
    for i in range(images):
        rows = pl.ds(i * image_rows, image_rows)
        product[...] = norm_ref[:, rows] * normed_ref[:, rows].astype(jnp.float32)
        columns = [
            total
            + lax.dot_general(
                ones,
                right,
                (((1,), (1,)), ((), ())),
                precision=lax.Precision.HIGHEST,
                preferred_element_type=jnp.float32,
            )
            for total, right in zip(columns, (product[...], norm_ref[:, rows]))
        ]
    sums[0, 0:1, 0:channels] = columns[0][0:1]
    sums[0, 1:2, 0:channels] = columns[1][0:1]
    sums[0, 2:4, 0 : bias_ref.shape[1]] = bias_ref[...]
    for d in range(1, ctx_count):
        sum_copy(d).start()

    for half in range(HALVES):
        relay(half, 1).wait_recv()
        relay(half, 3).wait_recv()
        forward(half, 2)

    for d in range(1, ctx_count):
        sum_copy(d).wait_recv()
    whole = sums[0]
    for d in range(1, ctx_count):
        whole = whole + sums[d]
    sum_ref[...] = whole * grad_scale

    for half in range(HALVES):
        for d in range(SIDE):
            for target in range(1, SIDE):
                across(half, target, d).wait_recv()
            across(half, 0, d).wait()
    for half in range(HALVES):
        for sign in (1, 3):
            for pair in range(2):
                near(half, sign, pair).wait_send()
            relay(half, sign).wait_send()
        for d in range(1, SIDE):
            stat_copy(half, d).wait_send()
            for e in range(SIDE):
                across(half, d, e).wait_send()
    for d in range(1, ctx_count):
        sum_copy(d).wait_send()


def hand_over(norm_t, normed_t, gain, inverse_std, owner_map, bias, full_width, grad_scale, ctx_count):
    channels, rows = norm_t.shape
    images = owner_map.shape[1]
    image_rows = rows // images
    vmem = pl.BlockSpec(memory_space=pltpu.VMEM)
    block = pltpu.VMEM((images, channels, LANES), jnp.bfloat16)
    dma = pltpu.SemaphoreType.DMA
    return pl.pallas_call(
        functools.partial(hand_kernel, full_width, grad_scale),
        out_shape=(
            jax.ShapeDtypeStruct((8, 1024), jnp.float32),
            jax.ShapeDtypeStruct((HALVES, TP * channels, LANES), jnp.bfloat16),
        ),
        in_specs=[vmem, vmem, vmem, vmem, pl.BlockSpec(memory_space=pltpu.SMEM), vmem],
        out_specs=(vmem, pl.BlockSpec(memory_space=pl.ANY)),
        scratch_shapes=[block] * 8
        + [
            pltpu.VMEM((HALVES, SIDE, SIDE, channels, LANES), jnp.bfloat16),
            pltpu.VMEM((channels, image_rows), jnp.float32),
            pltpu.VMEM((SIDE, 2 * images, image_rows), jnp.float32),
            pltpu.VMEM((SIDE, 2 * images, image_rows), jnp.float32),
            pltpu.VMEM((ctx_count, 8, 1024), jnp.float32),
            dma((HALVES, 2, 2)),
            dma((HALVES, 2, 2)),
            dma((HALVES, 2)),
            dma((HALVES, 2)),
            dma((HALVES, SIDE - 1, SIDE)),
            dma((HALVES, SIDE - 1, SIDE)),
            dma((HALVES, SIDE)),
            dma((HALVES, SIDE - 1)),
            dma((HALVES, SIDE - 1)),
            dma((ctx_count - 1,)),
            dma((ctx_count - 1,)),
        ],
        compiler_params=pltpu.CompilerParams(
            collective_id=2, has_side_effects=True, vmem_limit_bytes=VMEM_LIMIT
        ),
        cost_estimate=pl.CostEstimate(
            flops=20 * rows * channels, bytes_accessed=200 * 2**20, transcendentals=0
        ),
        name="hand_over",
    )(norm_t, normed_t, gain, inverse_std, owner_map, bias)


def finish_kernel(grad_scale, final_ref, gw2_ref, gw1_ref, sum_ref, out_ref, grad_w2_ref, grad_w1_ref, ln_ref, up_ref, down_ref):
    lanes = out_ref.shape[0]
    row = lax.broadcasted_iota(jnp.int32, (lanes, lanes), 0)
    column = lax.broadcasted_iota(jnp.int32, (lanes, lanes), 1)
    identity = jnp.where(row == column, 1.0, 0.0).astype(jnp.bfloat16)
    block = jnp.concatenate([final_ref[0], final_ref[1]], axis=1)
    out_ref[...] = dot_last(identity, block).astype(jnp.bfloat16)
    grad_w2_ref[...] = gw2_ref[...].astype(jnp.float32) * grad_scale
    grad_w1_ref[...] = gw1_ref[...].astype(jnp.float32) * grad_scale
    ln_ref[...] = sum_ref[0:2, 0 : ln_ref.shape[1]]
    down_ref[...] = sum_ref[2:3, 0 : down_ref.shape[1]]
    up_ref[...] = sum_ref[3:4, 0 : up_ref.shape[1]]


def finish(final, gw2, gw1_t, sums, width, grad_scale):
    steps = 10
    wide = final.shape[1] // steps
    channels, units = gw1_t.shape
    vmem = pl.BlockSpec(memory_space=pltpu.VMEM)
    last = 7
    return pl.pallas_call(
        functools.partial(finish_kernel, grad_scale),
        grid=(steps,),
        out_shape=(
            jax.ShapeDtypeStruct((HALVES * LANES, final.shape[1]), jnp.bfloat16),
            jax.ShapeDtypeStruct(gw2.shape, jnp.float32),
            jax.ShapeDtypeStruct(gw1_t.shape, jnp.float32),
            jax.ShapeDtypeStruct((2, channels), jnp.float32),
            jax.ShapeDtypeStruct((1, width), jnp.float32),
            jax.ShapeDtypeStruct((1, width), jnp.float32),
        ),
        in_specs=[
            pl.BlockSpec((HALVES, wide, LANES), lambda k: (0, k, 0)),
            pl.BlockSpec((gw2.shape[0] // 8, width), lambda k: (jnp.minimum(k, last), 0)),
            pl.BlockSpec((channels // steps, units), lambda k: (k, 0)),
            vmem,
        ],
        out_specs=(
            pl.BlockSpec((HALVES * LANES, wide), lambda k: (0, k)),
            pl.BlockSpec((gw2.shape[0] // 8, width), lambda k: (jnp.minimum(k, last), 0)),
            pl.BlockSpec((channels // steps, units), lambda k: (k, 0)),
            vmem,
            vmem,
            vmem,
        ),
        compiler_params=pltpu.CompilerParams(vmem_limit_bytes=VMEM_LIMIT),
        name="finish",
    )(final, gw2, gw1_t, sums)


def per_device(out_grad, pre_act, normed, inverse_std, w_up, w_down, ln_gain, owner_map):
    ctx_count = lax.axis_size("ctx")
    tp_count = lax.axis_size("tp")
    row_count = out_grad.shape[0]
    grad_scale = float(row_count * ctx_count) ** (-0.5)
    back_part, gw2, bias = down(out_grad, w_down, pre_act)
    gw2 = lax.psum_scatter(gw2, "ctx", scatter_dimension=0, tiled=True)
    normed_t = normed.T
    norm_t, gw1 = up(back_part, w_up.T, normed_t, ctx_count)
    gw1 = lax.psum_scatter(gw1, "ctx", scatter_dimension=0, tiled=True)
    sums, final = hand_over(
        norm_t,
        normed_t,
        ln_gain[:, None],
        inverse_std[None, :],
        owner_map,
        bias,
        float(normed.shape[1] * tp_count),
        grad_scale,
        ctx_count,
    )
    vit_grad, grad_w2, grad_w1_t, ln_grads, bias_up, bias_down = finish(
        final, gw2, gw1[0], sums, bias.shape[1], grad_scale
    )
    return (grad_w2, grad_w1_t.T, bias_up[0], bias_down[0], ln_grads, vit_grad)


def solution(mesh):
    return jax.shard_map(
        per_device,
        mesh=mesh,
        in_specs=(
            P("ctx", "tp"),
            P("ctx", "tp"),
            P("ctx", "tp"),
            P("ctx"),
            P(None, "tp"),
            P(None, "tp"),
            P("tp"),
            P("ctx", None),
        ),
        out_specs=(
            P("ctx", "tp"),
            P("ctx", "tp"),
            P("tp"),
            P("tp"),
            P(None, "tp"),
            P(("ctx", "tp"), None),
        ),
        check_vma=False,
    )
```

```python
import functools
import math

import jax
import jax.numpy as jnp
from jax import lax
from jax.experimental import pallas as pl
from jax.experimental.pallas import tpu as pltpu
from jax.sharding import PartitionSpec as P

MESH = pl.DeviceIdType.MESH
SIDE = 4
TP = SIDE * SIDE
VMEM_LIMIT = 60 * 2**20


def gelu_parts(linear):
    normal_cdf = 0.5 * (1.0 + lax.erf(linear * 2.0 ** (-0.5)))
    density = jnp.exp(-0.5 * linear * linear) * (2.0 * math.pi) ** (-0.5)
    return (linear * normal_cdf, normal_cdf + linear * density)


def dot(left, right):
    return lax.dot_general(
        left, right, (((1,), (0,)), ((), ())), preferred_element_type=jnp.float32
    )


def row_product(left, right):
    return lax.dot_general(
        left, right, (((0,), (0,)), ((), ())), preferred_element_type=jnp.float32
    )


def dot_last(left, right):
    return lax.dot_general(
        left, right, (((1,), (1,)), ((), ())), preferred_element_type=jnp.float32
    )


def around(half, me):
    t = Torus(half, me)
    return ((t.along + 1, t.cross), (t.along + SIDE - 1, t.cross))


def greet(targets):
    barrier = pltpu.get_barrier_semaphore()
    for target in targets:
        pl.semaphore_signal(barrier, inc=1, device_id={"tp": target}, device_id_type=MESH)
    pl.semaphore_wait(barrier, len(targets))


class Torus:
    def __init__(self, half, me):
        z, y = me // SIDE, me % SIDE
        self.half = half
        self.along, self.cross = (y, z) if half == 0 else (z, y)

    def place(self, along, cross):
        along, cross = along % SIDE, cross % SIDE
        return cross * SIDE + along if self.half == 0 else along * SIDE + cross


QUARTERS = 4
ARRIVALS = (
    (3, 0), (1, 0), (0, 3), (2, 0), (3, 3), (1, 3), (0, 1), (2, 3),
    (3, 1), (0, 2), (1, 1), (3, 2), (2, 1), (1, 2), (2, 2),
)


def full_at(y, z):
    turns = ((y, z), (-y % SIDE, -z % SIDE), (z, y), (-z % SIDE, -y % SIDE))
    return max(ARRIVALS.index(turn) for turn in turns if turn != (0, 0))


FULL_AT = {(y, z): full_at(y, z) for y in range(SIDE) for z in range(SIDE) if (y, z) != (0, 0)}
FULL_AT[(0, 0)] = min(FULL_AT.values())


def gain_column(gain_ref, column_ref):
    channels = gain_ref.shape[0]
    rows = channels // 5
    at = lax.broadcasted_iota(jnp.int32, (rows, channels), 1) - lax.broadcasted_iota(
        jnp.int32, (rows, channels), 0
    )

    def some(k, carry):
        picked = jnp.where(at == k * rows, jnp.broadcast_to(gain_ref[...], (rows, channels)), 0.0)
        column_ref[pl.ds(pl.multiple_of(k * rows, rows), rows), :] = jnp.sum(picked, axis=1, keepdims=True)
        return carry

    lax.fori_loop(0, 5, some, 0)


def numbered(values, index):
    out = jnp.int32(values[0])
    for i, value in enumerate(values[1:], 1):
        out = jnp.where(index == i, jnp.int32(value), out)
    return out


def tree_gather(prepare, me, full_ref, send_sem, recv_sem, consume, complete):
    rows = full_ref.shape[1] // QUARTERS
    torus = [Torus(half, me) for half in range(2)]

    def origin(quarter, along, cross):
        t, sign = torus[quarter // 2], 1 - quarter % 2 * 2
        return t.place(t.along + sign * along + SIDE, t.cross + sign * cross + SIDE)

    def copy(quarter, block, number, target):
        spot = full_ref.at[origin(quarter, *block), pl.ds(quarter * rows, rows)]
        return pltpu.make_async_remote_copy(
            src_ref=spot,
            dst_ref=spot,
            send_sem=send_sem.at[quarter, number],
            recv_sem=recv_sem.at[quarter, number],
            device_id={"tp": origin(quarter, *target)},
            device_id_type=MESH,
        )

    def send(block, seen):
        target = ((block[0] - seen[0]) % SIDE, (block[1] - seen[1]) % SIDE)
        for quarter in range(QUARTERS):
            copy(quarter, block, ARRIVALS.index(seen), target).start()

    send((0, 0), (3, 0))
    send((0, 0), (1, 0))
    send((0, 0), (0, 3))
    send((0, 0), (0, 1))
    prepare()
    for quarter in range(QUARTERS):
        consume(me, quarter)

    def arrive(k, carry):
        along = numbered([block[0] for block in ARRIVALS], k)
        cross = numbered([block[1] for block in ARRIVALS], k)
        for quarter in range(QUARTERS):
            copy(quarter, (along, cross), k, (1, 0)).wait_recv()
        for number, block in enumerate(ARRIVALS):
            if block[1] not in (0, 3):
                continue

            @pl.when(k == number)
            def _():
                if block == (3, 0):
                    send(block, (2, 0))
                if block[1] == 0:
                    send(block, (block[0], 3))
                    send(block, (block[0], 1))
                else:
                    send(block, (block[0], 2))

        for quarter in range(QUARTERS):
            consume(origin(quarter, along, cross), quarter)
        for number in sorted(set(FULL_AT.values())):

            @pl.when(k == number)
            def _():
                for block, at in FULL_AT.items():
                    if at == number:
                        complete(torus[0].place(torus[0].along + block[0], torus[0].cross + block[1]))

        return carry

    lax.fori_loop(0, TP - 1, arrive, 0)

    def drain(k, carry):
        for quarter in range(QUARTERS):
            copy(quarter, (0, 0), k, (1, 0)).wait_send()
        return carry

    lax.fori_loop(0, TP - 1, drain, 0)


def down_kernel(
    grad_ref, w_hbm, pre_ref, part_ref, gw2_hbm, bias_ref, full_ref, w_ref, total, gw2, short, hidden, slope, w_sem, out_sem, send_sem, recv_sem
):
    me = lax.axis_index("tp")
    load = pltpu.make_async_copy(w_hbm, w_ref, w_sem)
    load.start()
    full_ref[me] = grad_ref[...]
    greet([Torus(half, me).place(*at) for half in range(2) for at in around(half, me)])
    rows_all, width = grad_ref.shape
    quarter = rows_all // QUARTERS

    def prepare():
        def rows_of(i, carry):
            rows = pl.ds(pl.multiple_of(i * 64, 64), 64)
            value, steep = gelu_parts(pre_ref[rows, :].astype(jnp.float32))
            hidden[rows, :] = value.astype(jnp.bfloat16)
            slope[rows, :] = steep
            return carry

        lax.fori_loop(0, rows_all // 64, rows_of, 0)
        bias_ref[0:1, :] = jnp.sum(grad_ref[...].astype(jnp.float32), axis=0, keepdims=True)
        total[...] = jnp.zeros_like(total)
        gw2[...] = jnp.zeros_like(gw2)
        load.wait()

    def consume(origin, part):
        rows = pl.ds(part * quarter, quarter)
        features = pl.ds(pl.multiple_of(origin * width, width), width)
        block = full_ref[origin, rows, :]
        total[rows, :] += dot(block, w_ref[features, :])
        gw2[features, :] += row_product(block, hidden[rows, :])

    def write(origin):
        features = pl.ds(pl.multiple_of(origin * width, width), width)
        return pltpu.make_async_copy(short.at[features], gw2_hbm.at[features], out_sem.at[origin])

    def complete(origin):
        features = pl.ds(pl.multiple_of(origin * width, width), width)
        short[features, :] = gw2[features, :].astype(jnp.bfloat16)
        write(origin).start()

    tree_gather(prepare, me, full_ref, send_sem, recv_sem, consume, complete)
    part = (total[...] * slope[...]).astype(jnp.bfloat16)
    part_ref[...] = part
    bias_ref[1:2, :] = jnp.sum(part.astype(jnp.float32), axis=0, keepdims=True)
    for origin in range(TP):
        write(origin).wait()


def down(out_grad, w_down, pre_act):
    rows, width = out_grad.shape
    features, hid = w_down.shape
    vmem = pl.BlockSpec(memory_space=pltpu.VMEM)
    return pl.pallas_call(
        down_kernel,
        out_shape=(
            jax.ShapeDtypeStruct((rows, hid), jnp.bfloat16),
            jax.ShapeDtypeStruct((features, hid), jnp.bfloat16),
            jax.ShapeDtypeStruct((2, hid), jnp.float32),
        ),
        in_specs=[vmem, pl.BlockSpec(memory_space=pl.ANY), vmem],
        out_specs=(vmem, pl.BlockSpec(memory_space=pl.ANY), vmem),
        scratch_shapes=[
            pltpu.VMEM((TP, rows, width), jnp.bfloat16),
            pltpu.VMEM((features, hid), jnp.bfloat16),
            pltpu.VMEM((rows, hid), jnp.float32),
            pltpu.VMEM((features, hid), jnp.float32),
            pltpu.VMEM((features, hid), jnp.bfloat16),
            pltpu.VMEM((rows, hid), jnp.bfloat16),
            pltpu.VMEM((rows, hid), jnp.float32),
            pltpu.SemaphoreType.DMA,
            pltpu.SemaphoreType.DMA((TP,)),
            pltpu.SemaphoreType.DMA((QUARTERS, TP - 1)),
            pltpu.SemaphoreType.DMA((QUARTERS, TP - 1)),
        ],
        compiler_params=pltpu.CompilerParams(
            collective_id=0, has_side_effects=True, vmem_limit_bytes=VMEM_LIMIT
        ),
        name="down_gather",
    )(out_grad, w_down, pre_act)


def up_kernel(
    part_ref, w_hbm, normed_hbm, gain_ref, norm_hbm, gw1_hbm, stat_ref,
    full_ref, w_ref, normed_ref, norm_ref, gw1, short, column, w_sem, out_sem, send_sem, recv_sem,
):
    me = lax.axis_index("tp")
    loads = [
        pltpu.make_async_copy(w_hbm, w_ref, w_sem.at[0]),
        pltpu.make_async_copy(normed_hbm, normed_ref, w_sem.at[1]),
    ]
    for load in loads:
        load.start()
    full_ref[me] = part_ref[...]
    greet([Torus(half, me).place(*at) for half in range(2) for at in around(half, me)])
    rows_all, width = part_ref.shape
    quarter = rows_all // QUARTERS
    per_owner = gw1.shape[2] // width
    channels = norm_ref.shape[0]
    chunk = channels // 5
    images = stat_ref.shape[0] // 2
    image_rows = rows_all // images

    def prepare():
        norm_ref[...] = jnp.zeros_like(norm_ref)
        gw1[...] = jnp.zeros_like(gw1)
        gain_column(gain_ref, column)
        for load in loads:
            load.wait()

    def consume(origin, part):
        rows = pl.ds(part * quarter, quarter)
        units = pl.ds(pl.multiple_of(origin * width, width), width)
        within = pl.ds(pl.multiple_of(origin % per_owner * width, width), width)
        block = full_ref[origin, rows, :]
        norm_ref[:, rows] += dot_last(w_ref[:, units], block)
        gw1[origin // per_owner, :, within] += dot(normed_ref[:, rows], block)

    def write(origin):
        within = pl.ds(pl.multiple_of(origin % per_owner * width, width), width)
        owner = origin // per_owner
        return pltpu.make_async_copy(
            short.at[owner, :, within], gw1_hbm.at[owner, :, within], out_sem.at[origin]
        )

    def complete(origin):
        within = pl.ds(pl.multiple_of(origin % per_owner * width, width), width)
        owner = origin // per_owner

        def some(k, carry):
            part = pl.ds(pl.multiple_of(k * chunk, chunk), chunk)
            short[owner, part, within] = gw1[owner, part, within].astype(jnp.bfloat16)
            return carry

        lax.fori_loop(0, 5, some, 0)
        write(origin).start()

    tree_gather(prepare, me, full_ref, send_sem, recv_sem, consume, complete)
    store = pltpu.make_async_copy(norm_ref, norm_hbm, w_sem.at[0])
    store.start()

    for i in range(images):
        rows = pl.ds(i * image_rows, image_rows)

        def some(k, carry):
            part = pl.ds(pl.multiple_of(k * chunk, chunk), chunk)
            feature = normed_ref[part, rows].astype(jnp.float32)
            gained = column[part, :] * norm_ref[part, rows]
            return (
                carry[0] + jnp.sum(gained, axis=0, keepdims=True),
                carry[1] + jnp.sum(gained * feature, axis=0, keepdims=True),
            )

        zero = jnp.zeros((1, image_rows), jnp.float32)
        first, second = lax.fori_loop(0, 5, some, (zero, zero))
        stat_ref[i : i + 1, :] = first
        stat_ref[images + i : images + i + 1, :] = second
    store.wait()
    for origin in range(TP):
        write(origin).wait()


def up(back_part, w_up_t, normed_t, gain, ctx_count, images):
    rows, width = back_part.shape
    channels, units = w_up_t.shape
    vmem = pl.BlockSpec(memory_space=pltpu.VMEM)
    anywhere = pl.BlockSpec(memory_space=pl.ANY)
    return pl.pallas_call(
        up_kernel,
        out_shape=(
            jax.ShapeDtypeStruct((channels, rows), jnp.float32),
            jax.ShapeDtypeStruct((ctx_count, channels, units // ctx_count), jnp.bfloat16),
            jax.ShapeDtypeStruct((2 * images, rows // images), jnp.float32),
        ),
        in_specs=[vmem, anywhere, anywhere, vmem],
        out_specs=(anywhere, anywhere, vmem),
        scratch_shapes=[
            pltpu.VMEM((TP, rows, width), jnp.bfloat16),
            pltpu.VMEM((channels, units), jnp.bfloat16),
            pltpu.VMEM((channels, rows), jnp.bfloat16),
            pltpu.VMEM((channels, rows), jnp.float32),
            pltpu.VMEM((ctx_count, channels, units // ctx_count), jnp.float32),
            pltpu.VMEM((ctx_count, channels, units // ctx_count), jnp.bfloat16),
            pltpu.VMEM((channels, 1), jnp.float32),
            pltpu.SemaphoreType.DMA((2,)),
            pltpu.SemaphoreType.DMA((TP,)),
            pltpu.SemaphoreType.DMA((QUARTERS, TP - 1)),
            pltpu.SemaphoreType.DMA((QUARTERS, TP - 1)),
        ],
        compiler_params=pltpu.CompilerParams(
            collective_id=1, has_side_effects=True, vmem_limit_bytes=VMEM_LIMIT
        ),
        cost_estimate=pl.CostEstimate(
            flops=4 * rows * units * channels, bytes_accessed=20 * 2**20, transcendentals=0
        ),
        name="up_gather",
    )(back_part, w_up_t, normed_t, gain)


HALVES = 2
LANES = 128


def hand_kernel(
    full_width,
    grad_scale,
    norm_hbm,
    normed_hbm,
    gain_row,
    std_ref,
    owner_ref,
    bias_ref,
    stat_ref,
    sum_ref,
    final,
    own_y, next_y, far_y, prev_y,
    own_z, next_z, far_z, prev_z,
    message,
    norm_ref,
    normed_ref,
    gain_ref,
    product,
    stats_y,
    stats_z,
    sums,
    load_sem, near_send, near_recv, relay_send, relay_recv, cross_send, cross_recv, own_sem, stat_send, stat_recv, sum_send, sum_recv,
):
    me = lax.axis_index("tp")
    group = lax.axis_index("ctx")
    ctx_count = sums.shape[0]
    torus = [Torus(half, me) for half in range(HALVES)]
    held = [[own_y, next_y, far_y, prev_y], [own_z, next_z, far_z, prev_z]]
    images, channels, _ = own_y.shape
    image_rows = norm_ref.shape[1] // images
    chunk = channels // 5

    def along_peer(half, d):
        t = torus[half]
        return t.place(t.along + d, t.cross)

    def cross_peer(half, d):
        t = torus[half]
        return t.place(t.along, t.cross + d)

    barrier = pltpu.get_barrier_semaphore()
    for half in range(HALVES):
        for d in range(1, SIDE):
            pl.semaphore_signal(barrier, inc=1, device_id={"tp": along_peer(half, d)}, device_id_type=MESH)
    for d in range(1, ctx_count):
        pl.semaphore_signal(barrier, inc=1, device_id={"ctx": (group + d) % ctx_count}, device_id_type=MESH)

    loads = [
        pltpu.make_async_copy(norm_hbm, norm_ref, load_sem.at[0]),
        pltpu.make_async_copy(normed_hbm, normed_ref, load_sem.at[1]),
    ]
    for load in loads:
        load.start()
    stats_y[0] = stat_ref[...]
    gain_column(gain_row, gain_ref)
    pl.semaphore_wait(barrier, HALVES * (SIDE - 1) + ctx_count - 1)

    def stat_copy(half, d):
        buffer = (stats_y, stats_z)[half]
        return pltpu.make_async_remote_copy(
            src_ref=buffer.at[0],
            dst_ref=buffer.at[d],
            send_sem=stat_send.at[half, d - 1],
            recv_sem=stat_recv.at[half, d - 1],
            device_id={"tp": along_peer(half, d)},
            device_id_type=MESH,
        )

    def sum_copy(d):
        return pltpu.make_async_remote_copy(
            src_ref=sums.at[0],
            dst_ref=sums.at[d],
            send_sem=sum_send.at[d - 1],
            recv_sem=sum_recv.at[d - 1],
            device_id={"ctx": (group + d) % ctx_count},
            device_id_type=MESH,
        )

    for d in range(1, SIDE):
        stat_copy(0, d).start()
    for d in range(1, SIDE):
        stat_copy(0, d).wait_recv()
    stats_z[0] = stats_y[0] + stats_y[1] + stats_y[2] + stats_y[3]
    for d in range(1, SIDE):
        stat_copy(1, d).start()
    for d in range(1, SIDE):
        stat_copy(1, d).wait_recv()
    for load in loads:
        load.wait()
    means = (stats_z[0] + stats_z[1] + stats_z[2] + stats_z[3]) * (1.0 / full_width)

    def near(half, sign, pair):
        piece = pl.ds(pair * (images // 2), images // 2)
        return pltpu.make_async_remote_copy(
            src_ref=held[half][0].at[piece],
            dst_ref=held[half][3 if sign == 1 else 1].at[piece],
            send_sem=near_send.at[half, sign // 2, pair],
            recv_sem=near_recv.at[half, sign // 2, pair],
            device_id={"tp": along_peer(half, sign)},
            device_id_type=MESH,
        )

    def relay(half, sign):
        pair = sign // 2
        piece = pl.ds(pair * (images // 2), images // 2)
        return pltpu.make_async_remote_copy(
            src_ref=held[half][3 if sign == 1 else 1].at[piece],
            dst_ref=held[half][2].at[piece],
            send_sem=relay_send.at[half, pair],
            recv_sem=relay_recv.at[half, pair],
            device_id={"tp": along_peer(half, sign)},
            device_id_type=MESH,
        )

    def across(half, target, d):
        t = torus[half]
        slot = (t.along + d) % SIDE
        source = t.cross * SIDE + slot if half == 0 else slot * SIDE + t.cross
        spot = final.at[half, pl.ds(pl.multiple_of(source * channels, 16), channels)]
        if target == 0:
            return pltpu.make_async_copy(message.at[half, 0, d], spot, own_sem.at[half, d])
        return pltpu.make_async_remote_copy(
            src_ref=message.at[half, target, d],
            dst_ref=spot,
            send_sem=cross_send.at[half, target - 1, d],
            recv_sem=cross_recv.at[half, target - 1, d],
            device_id={"tp": cross_peer(half, target)},
            device_id_type=MESH,
        )

    for i in range(images):
        rows = pl.ds(i * image_rows, image_rows)
        mean_first, mean_second = means[i : i + 1, :], means[images + i : images + i + 1, :]
        inverse = std_ref[:, rows]

        def visual(k, carry):
            part = pl.ds(pl.multiple_of(k * chunk, chunk), chunk)
            value = gain_ref[part, :] * norm_ref[part, rows]
            feature = normed_ref[part, rows].astype(jnp.float32)
            seen = (inverse * (value - mean_first - feature * mean_second)).astype(jnp.bfloat16)
            own_y[i, part, :] = seen[:, :LANES]
            own_z[i, part, :] = seen[:, LANES:]
            return carry

        lax.fori_loop(0, 5, visual, 0)
        if i % 2:
            for half in range(HALVES):
                near(half, 1, i // 2).start()
                near(half, 3, i // 2).start()
    owners = [owner_ref[0, i] for i in range(images)]
    slots = []
    for i in range(images):
        earlier = jnp.int32(0)
        for j in range(i):
            earlier += (owners[j] == owners[i]).astype(jnp.int32)
        slots.append(owners[i] + earlier)

    def choice(place):
        source, present = jnp.int32(0), jnp.int32(0)
        for i in range(images):
            match = (slots[i] == place).astype(jnp.int32)
            source += i * match
            present += match
        return source, present

    chosen = [[choice(cross_peer(half, target)) for target in range(SIDE)] for half in range(HALVES)]

    def forward(half, d):
        block = held[half][d]
        for target in (2, 1, 3, 0):
            source, present = chosen[half][target]
            spot = message.at[half, target, d]

            def pick(k, carry):
                part = pl.ds(pl.multiple_of(k * chunk, chunk), chunk)
                value = block[source, part, :]
                spot[part, :] = jnp.where(present > 0, value, jnp.zeros_like(value))
                return carry

            lax.fori_loop(0, 5, pick, 0)
            across(half, target, d).start()

    for half in range(HALVES):
        forward(half, 0)
    for half in range(HALVES):
        near(half, 1, 0).wait_recv()
        relay(half, 1).start()
    for half in range(HALVES):
        near(half, 3, 1).wait_recv()
        relay(half, 3).start()
    for half in range(HALVES):
        near(half, 1, 1).wait_recv()
        forward(half, 3)
        near(half, 3, 0).wait_recv()
        forward(half, 1)

    ones = jnp.ones((8, image_rows), jnp.float32)
    columns = [jnp.zeros((8, channels), jnp.float32)] * 2
    for i in range(images):
        rows = pl.ds(i * image_rows, image_rows)
        product[...] = norm_ref[:, rows] * normed_ref[:, rows].astype(jnp.float32)
        columns = [
            total
            + lax.dot_general(
                ones,
                right,
                (((1,), (1,)), ((), ())),
                precision=lax.Precision.HIGHEST,
                preferred_element_type=jnp.float32,
            )
            for total, right in zip(columns, (product[...], norm_ref[:, rows]))
        ]
    sums[0, 0:1, 0:channels] = columns[0][0:1]
    sums[0, 1:2, 0:channels] = columns[1][0:1]
    sums[0, 2:4, 0 : bias_ref.shape[1]] = bias_ref[...]
    for d in range(1, ctx_count):
        sum_copy(d).start()

    for half in range(HALVES):
        relay(half, 1).wait_recv()
        relay(half, 3).wait_recv()
        forward(half, 2)

    for d in range(1, ctx_count):
        sum_copy(d).wait_recv()
    whole = sums[0]
    for d in range(1, ctx_count):
        whole = whole + sums[d]
    sum_ref[...] = whole * grad_scale

    for half in range(HALVES):
        for d in range(SIDE):
            for target in range(1, SIDE):
                across(half, target, d).wait_recv()
            across(half, 0, d).wait()
    for half in range(HALVES):
        for sign in (1, 3):
            for pair in range(2):
                near(half, sign, pair).wait_send()
            relay(half, sign).wait_send()
        for d in range(1, SIDE):
            stat_copy(half, d).wait_send()
            for e in range(SIDE):
                across(half, d, e).wait_send()
    for d in range(1, ctx_count):
        sum_copy(d).wait_send()


def hand_over(norm_t, normed_t, gain, inverse_std, owner_map, bias, stats, full_width, grad_scale, ctx_count):
    channels, rows = norm_t.shape
    images = owner_map.shape[1]
    image_rows = rows // images
    vmem = pl.BlockSpec(memory_space=pltpu.VMEM)
    block = pltpu.VMEM((images, channels, LANES), jnp.bfloat16)
    dma = pltpu.SemaphoreType.DMA
    return pl.pallas_call(
        functools.partial(hand_kernel, full_width, grad_scale),
        out_shape=(
            jax.ShapeDtypeStruct((8, 1024), jnp.float32),
            jax.ShapeDtypeStruct((HALVES, TP * channels, LANES), jnp.bfloat16),
        ),
        in_specs=[
            pl.BlockSpec(memory_space=pl.ANY),
            pl.BlockSpec(memory_space=pl.ANY),
            vmem,
            vmem,
            pl.BlockSpec(memory_space=pltpu.SMEM),
            vmem,
            vmem,
        ],
        out_specs=(vmem, pl.BlockSpec(memory_space=pl.ANY)),
        scratch_shapes=[block] * 8
        + [
            pltpu.VMEM((HALVES, SIDE, SIDE, channels, LANES), jnp.bfloat16),
            pltpu.VMEM((channels, rows), jnp.float32),
            pltpu.VMEM((channels, rows), jnp.bfloat16),
            pltpu.VMEM((channels, 1), jnp.float32),
            pltpu.VMEM((channels, image_rows), jnp.float32),
            pltpu.VMEM((SIDE, 2 * images, image_rows), jnp.float32),
            pltpu.VMEM((SIDE, 2 * images, image_rows), jnp.float32),
            pltpu.VMEM((ctx_count, 8, 1024), jnp.float32),
            dma((2,)),
            dma((HALVES, 2, 2)),
            dma((HALVES, 2, 2)),
            dma((HALVES, 2)),
            dma((HALVES, 2)),
            dma((HALVES, SIDE - 1, SIDE)),
            dma((HALVES, SIDE - 1, SIDE)),
            dma((HALVES, SIDE)),
            dma((HALVES, SIDE - 1)),
            dma((HALVES, SIDE - 1)),
            dma((ctx_count - 1,)),
            dma((ctx_count - 1,)),
        ],
        compiler_params=pltpu.CompilerParams(
            collective_id=2, has_side_effects=True, vmem_limit_bytes=VMEM_LIMIT
        ),
        cost_estimate=pl.CostEstimate(
            flops=20 * rows * channels, bytes_accessed=200 * 2**20, transcendentals=0
        ),
        name="hand_over",
    )(norm_t, normed_t, gain, inverse_std, owner_map, bias, stats)


STEPS = 10


def finish_kernel(
    grad_scale, final_hbm, gw2_hbm, gw1_hbm, sum_ref, out_hbm, grad_w2_hbm, grad_w1_hbm, ln_ref, up_ref, down_ref,
    final, out, gw2, grad_w2, gw1, grad_w1, in_sem, out_sem,
):
    wide = final.shape[1] // STEPS
    small_in = [
        pltpu.make_async_copy(gw2_hbm, gw2, in_sem.at[STEPS]),
        pltpu.make_async_copy(gw1_hbm, gw1, in_sem.at[STEPS + 1]),
    ]
    small_out = [
        pltpu.make_async_copy(grad_w2, grad_w2_hbm, out_sem.at[STEPS]),
        pltpu.make_async_copy(grad_w1, grad_w1_hbm, out_sem.at[STEPS + 1]),
    ]

    def load(k):
        part = pl.ds(pl.multiple_of(k * wide, wide), wide)
        return pltpu.make_async_copy(final_hbm.at[:, part], final.at[:, part], in_sem.at[k])

    def store(k):
        part = pl.ds(pl.multiple_of(k * wide, wide), wide)
        return pltpu.make_async_copy(out.at[:, part], out_hbm.at[:, part], out_sem.at[k])

    load(0).start()
    load(1).start()
    for copy in small_in:
        copy.start()
    for k in range(2, STEPS):
        load(k).start()
    lanes = out.shape[0]
    row = lax.broadcasted_iota(jnp.int32, (lanes, lanes), 0)
    column = lax.broadcasted_iota(jnp.int32, (lanes, lanes), 1)
    identity = jnp.where(row == column, 1.0, 0.0).astype(jnp.bfloat16)

    def turn(k, carry):
        part = pl.ds(pl.multiple_of(k * wide, wide), wide)
        load(k).wait()
        block = jnp.concatenate([final[0, part, :], final[1, part, :]], axis=1)
        out[:, part] = dot_last(identity, block).astype(jnp.bfloat16)
        store(k).start()
        return carry

    lax.fori_loop(0, STEPS // 2, turn, 0)
    for copy in small_in:
        copy.wait()
    grad_w2[...] = gw2[...].astype(jnp.float32) * grad_scale
    small_out[0].start()
    grad_w1[...] = gw1[...].astype(jnp.float32) * grad_scale
    small_out[1].start()
    lax.fori_loop(STEPS // 2, STEPS, turn, 0)
    ln_ref[...] = sum_ref[0:2, 0 : ln_ref.shape[1]]
    down_ref[...] = sum_ref[2:3, 0 : down_ref.shape[1]]
    up_ref[...] = sum_ref[3:4, 0 : up_ref.shape[1]]
    for copy in small_out:
        copy.wait()
    for k in range(STEPS):
        store(k).wait()


def finish(final, gw2, gw1_t, sums, width, grad_scale):
    channels = gw1_t.shape[0]
    vmem = pl.BlockSpec(memory_space=pltpu.VMEM)
    anywhere = pl.BlockSpec(memory_space=pl.ANY)
    return pl.pallas_call(
        functools.partial(finish_kernel, grad_scale),
        out_shape=(
            jax.ShapeDtypeStruct((HALVES * LANES, final.shape[1]), jnp.bfloat16),
            jax.ShapeDtypeStruct(gw2.shape, jnp.float32),
            jax.ShapeDtypeStruct(gw1_t.shape, jnp.float32),
            jax.ShapeDtypeStruct((2, channels), jnp.float32),
            jax.ShapeDtypeStruct((1, width), jnp.float32),
            jax.ShapeDtypeStruct((1, width), jnp.float32),
        ),
        in_specs=[anywhere, anywhere, anywhere, vmem],
        out_specs=(anywhere, anywhere, anywhere, vmem, vmem, vmem),
        scratch_shapes=[
            pltpu.VMEM(final.shape, jnp.bfloat16),
            pltpu.VMEM((HALVES * LANES, final.shape[1]), jnp.bfloat16),
            pltpu.VMEM(gw2.shape, jnp.bfloat16),
            pltpu.VMEM(gw2.shape, jnp.float32),
            pltpu.VMEM(gw1_t.shape, jnp.bfloat16),
            pltpu.VMEM(gw1_t.shape, jnp.float32),
            pltpu.SemaphoreType.DMA((STEPS + 2,)),
            pltpu.SemaphoreType.DMA((STEPS + 2,)),
        ],
        compiler_params=pltpu.CompilerParams(vmem_limit_bytes=VMEM_LIMIT),
        name="finish",
    )(final, gw2, gw1_t, sums)


def per_device(out_grad, pre_act, normed, inverse_std, w_up, w_down, ln_gain, owner_map):
    ctx_count = lax.axis_size("ctx")
    tp_count = lax.axis_size("tp")
    row_count = out_grad.shape[0]
    grad_scale = float(row_count * ctx_count) ** (-0.5)
    back_part, gw2, bias = down(out_grad, w_down, pre_act)
    gw2 = lax.psum_scatter(gw2, "ctx", scatter_dimension=0, tiled=True)
    normed_t = normed.T
    gain = ln_gain
    norm_t, gw1, stats = up(back_part, w_up.T, normed_t, gain, ctx_count, owner_map.shape[1])
    gw1 = lax.psum_scatter(gw1, "ctx", scatter_dimension=0, tiled=True)
    sums, final = hand_over(
        norm_t,
        normed_t,
        gain,
        inverse_std[None, :],
        owner_map,
        bias,
        stats,
        float(normed.shape[1] * tp_count),
        grad_scale,
        ctx_count,
    )
    vit_grad, grad_w2, grad_w1_t, ln_grads, bias_up, bias_down = finish(
        final, gw2, gw1[0], sums, bias.shape[1], grad_scale
    )
    return (grad_w2, grad_w1_t.T, bias_up[0], bias_down[0], ln_grads, vit_grad)


def solution(mesh):
    return jax.shard_map(
        per_device,
        mesh=mesh,
        in_specs=(
            P("ctx", "tp"),
            P("ctx", "tp"),
            P("ctx", "tp"),
            P("ctx"),
            P(None, "tp"),
            P(None, "tp"),
            P("tp"),
            P("ctx", None),
        ),
        out_specs=(
            P("ctx", "tp"),
            P("ctx", "tp"),
            P("tp"),
            P("tp"),
            P(None, "tp"),
            P(("ctx", "tp"), None),
        ),
        check_vma=False,
    )
```

```python
import functools
import math

import jax
import jax.numpy as jnp
from jax import lax
from jax.experimental import pallas as pl
from jax.experimental.pallas import tpu as pltpu
from jax.sharding import PartitionSpec as P

MESH = pl.DeviceIdType.MESH
SIDE = 4
TP = SIDE * SIDE
VMEM_LIMIT = 60 * 2**20


def gelu_parts(linear):
    normal_cdf = 0.5 * (1.0 + lax.erf(linear * 2.0 ** (-0.5)))
    density = jnp.exp(-0.5 * linear * linear) * (2.0 * math.pi) ** (-0.5)
    return (linear * normal_cdf, normal_cdf + linear * density)


def dot(left, right):
    return lax.dot_general(
        left, right, (((1,), (0,)), ((), ())), preferred_element_type=jnp.float32
    )


def row_product(left, right):
    return lax.dot_general(
        left, right, (((0,), (0,)), ((), ())), preferred_element_type=jnp.float32
    )


def dot_last(left, right):
    return lax.dot_general(
        left, right, (((1,), (1,)), ((), ())), preferred_element_type=jnp.float32
    )


def greet(half_targets):
    barrier = pltpu.get_barrier_semaphore()
    for target in half_targets:
        pl.semaphore_signal(barrier, inc=1, device_id={"tp": target}, device_id_type=MESH)


def met(count):
    pl.semaphore_wait(pltpu.get_barrier_semaphore(), count)


def peers(me, steps):
    torus = [Torus(half, me) for half in range(2)]
    return [t.place(t.along + d, t.cross) for t in torus for d in steps]


class Torus:
    def __init__(self, half, me):
        z, y = me // SIDE, me % SIDE
        self.half = half
        self.along, self.cross = (y, z) if half == 0 else (z, y)

    def place(self, along, cross):
        along, cross = along % SIDE, cross % SIDE
        return cross * SIDE + along if self.half == 0 else along * SIDE + cross


QUARTERS = 4
ARRIVALS = (
    (3, 0), (1, 0), (0, 3), (2, 0), (3, 3), (1, 3), (0, 1), (2, 3),
    (3, 1), (0, 2), (1, 1), (3, 2), (2, 1), (1, 2), (2, 2),
)


def full_at(y, z):
    turns = ((y, z), (-y % SIDE, -z % SIDE), (z, y), (-z % SIDE, -y % SIDE))
    return max(ARRIVALS.index(turn) for turn in turns if turn != (0, 0))


FULL_AT = {(y, z): full_at(y, z) for y in range(SIDE) for z in range(SIDE) if (y, z) != (0, 0)}
FULL_AT[(0, 0)] = min(FULL_AT.values())


def gain_column(gain_ref, column_ref):
    channels = gain_ref.shape[0]
    rows = channels // 5
    at = lax.broadcasted_iota(jnp.int32, (rows, channels), 1) - lax.broadcasted_iota(
        jnp.int32, (rows, channels), 0
    )

    def some(k, carry):
        picked = jnp.where(at == k * rows, jnp.broadcast_to(gain_ref[...], (rows, channels)), 0.0)
        column_ref[pl.ds(pl.multiple_of(k * rows, rows), rows), :] = jnp.sum(picked, axis=1, keepdims=True)
        return carry

    lax.fori_loop(0, 5, some, 0)


def numbered(values, index):
    out = jnp.int32(values[0])
    for i, value in enumerate(values[1:], 1):
        out = jnp.where(index == i, jnp.int32(value), out)
    return out


def tree_gather(prepare, me, full_ref, send_sem, recv_sem, consume, complete):
    rows = full_ref.shape[1] // QUARTERS
    torus = [Torus(half, me) for half in range(2)]

    def origin(quarter, along, cross):
        t, sign = torus[quarter // 2], 1 - quarter % 2 * 2
        return t.place(t.along + sign * along + SIDE, t.cross + sign * cross + SIDE)

    def copy(quarter, block, number, target):
        spot = full_ref.at[origin(quarter, *block), pl.ds(quarter * rows, rows)]
        return pltpu.make_async_remote_copy(
            src_ref=spot,
            dst_ref=spot,
            send_sem=send_sem.at[quarter, number],
            recv_sem=recv_sem.at[quarter, number],
            device_id={"tp": origin(quarter, *target)},
            device_id_type=MESH,
        )

    def send(block, seen):
        target = ((block[0] - seen[0]) % SIDE, (block[1] - seen[1]) % SIDE)
        for quarter in range(QUARTERS):
            copy(quarter, block, ARRIVALS.index(seen), target).start()

    send((0, 0), (3, 0))
    send((0, 0), (1, 0))
    send((0, 0), (0, 3))
    send((0, 0), (0, 1))
    prepare()
    for quarter in range(QUARTERS):
        consume(me, quarter)

    def arrive(k, carry):
        along = numbered([block[0] for block in ARRIVALS], k)
        cross = numbered([block[1] for block in ARRIVALS], k)
        for quarter in range(QUARTERS):
            copy(quarter, (along, cross), k, (1, 0)).wait_recv()
        for number, block in enumerate(ARRIVALS):
            if block[1] not in (0, 3):
                continue

            @pl.when(k == number)
            def _():
                if block == (3, 0):
                    send(block, (2, 0))
                if block[1] == 0:
                    send(block, (block[0], 3))
                    send(block, (block[0], 1))
                else:
                    send(block, (block[0], 2))

        for quarter in range(QUARTERS):
            consume(origin(quarter, along, cross), quarter)
        for number in sorted(set(FULL_AT.values())):

            @pl.when(k == number)
            def _():
                for block, at in FULL_AT.items():
                    if at == number:
                        complete(torus[0].place(torus[0].along + block[0], torus[0].cross + block[1]))

        return carry

    lax.fori_loop(0, TP - 1, arrive, 0)

    def drain(k, carry):
        for quarter in range(QUARTERS):
            copy(quarter, (0, 0), k, (1, 0)).wait_send()
        return carry

    lax.fori_loop(0, TP - 1, drain, 0)


def gather_kernel(
    full_width, grad_ref, pre_ref, gain_ref, w_down_hbm, w_up_hbm, normed_hbm, norm_hbm, weight_hbm, mean_ref, bias_ref,
    grads, parts, w_down, w_up, normed, total, hidden, slope, gw2, norm, gw1, short, column, stats_y, stats_z,
    load_sem, out_sem, down_send, down_recv, up_send, up_recv, stat_send, stat_recv,
):
    me = lax.axis_index("tp")
    greet(peers(me, (1, 2, 3)))
    loads = [
        pltpu.make_async_copy(source, target, load_sem.at[i])
        for i, (source, target) in enumerate(((w_down_hbm, w_down), (w_up_hbm, w_up), (normed_hbm, normed)))
    ]
    for load in loads:
        load.start()
    grads[me] = grad_ref[...]
    met(6)
    rows_all, width = grad_ref.shape
    quarter = rows_all // QUARTERS
    per_owner = gw1.shape[2] // width
    channels = norm.shape[0]
    chunk = channels // 5
    images = mean_ref.shape[0] // 2
    image_rows = rows_all // images

    def block_of(ref, origin, first, count):
        within = pl.ds(pl.multiple_of(origin % per_owner * width, width), width)
        return ref.at[origin // per_owner, pl.ds(first, count), within]

    def write_down(origin):
        return pltpu.make_async_copy(
            block_of(short, origin, 0, width), block_of(weight_hbm, origin, channels, width), out_sem.at[0, origin]
        )

    def prepare_down():
        def rows_of(i, carry):
            rows = pl.ds(pl.multiple_of(i * 64, 64), 64)
            value, steep = gelu_parts(pre_ref[rows, :].astype(jnp.float32))
            hidden[rows, :] = value.astype(jnp.bfloat16)
            slope[rows, :] = steep
            return carry

        lax.fori_loop(0, rows_all // 64, rows_of, 0)
        bias_ref[0:1, :] = jnp.sum(grad_ref[...].astype(jnp.float32), axis=0, keepdims=True)
        total[...] = jnp.zeros_like(total)
        gw2[...] = jnp.zeros_like(gw2)
        loads[0].wait()

    def consume_down(origin, part):
        rows = pl.ds(part * quarter, quarter)
        features = pl.ds(pl.multiple_of(origin * width, width), width)
        block = grads[origin, rows, :]
        total[rows, :] += dot(block, w_down[features, :])
        gw2[features, :] += row_product(block, hidden[rows, :])

    def complete_down(origin):
        features = pl.ds(pl.multiple_of(origin * width, width), width)
        block_of(short, origin, 0, width)[...] = gw2[features, :].astype(jnp.bfloat16)
        write_down(origin).start()

    tree_gather(prepare_down, me, grads, down_send, down_recv, consume_down, complete_down)
    part = (total[...] * slope[...]).astype(jnp.bfloat16)
    parts[me] = part

    def write_up(origin):
        return pltpu.make_async_copy(
            block_of(short, origin, 0, channels), block_of(weight_hbm, origin, 0, channels), out_sem.at[1, origin]
        )

    def prepare_up():
        bias_ref[1:2, :] = jnp.sum(parts[me].astype(jnp.float32), axis=0, keepdims=True)
        norm[...] = jnp.zeros_like(norm)
        gw1[...] = jnp.zeros_like(gw1)
        gain_column(gain_ref, column)
        for origin in range(TP):
            write_down(origin).wait()
        for load in loads[1:]:
            load.wait()

    def consume_up(origin, part):
        rows = pl.ds(part * quarter, quarter)
        units = pl.ds(pl.multiple_of(origin * width, width), width)
        within = pl.ds(pl.multiple_of(origin % per_owner * width, width), width)
        block = parts[origin, rows, :]
        norm[:, rows] += dot_last(w_up[:, units], block)
        gw1[origin // per_owner, :, within] += dot(normed[:, rows], block)

    def complete_up(origin):
        within = pl.ds(pl.multiple_of(origin % per_owner * width, width), width)
        owner = origin // per_owner

        def some(k, carry):
            part = pl.ds(pl.multiple_of(k * chunk, chunk), chunk)
            short[owner, part, within] = gw1[owner, part, within].astype(jnp.bfloat16)
            return carry

        lax.fori_loop(0, 5, some, 0)
        write_up(origin).start()

    tree_gather(prepare_up, me, parts, up_send, up_recv, consume_up, complete_up)
    store = pltpu.make_async_copy(norm, norm_hbm, load_sem.at[0])
    store.start()

    for i in range(images):
        rows = pl.ds(i * image_rows, image_rows)

        def some(k, carry):
            part = pl.ds(pl.multiple_of(k * chunk, chunk), chunk)
            feature = normed[part, rows].astype(jnp.float32)
            gained = column[part, :] * norm[part, rows]
            return (
                carry[0] + jnp.sum(gained, axis=0, keepdims=True),
                carry[1] + jnp.sum(gained * feature, axis=0, keepdims=True),
            )

        zero = jnp.zeros((1, image_rows), jnp.float32)
        first, second = lax.fori_loop(0, 5, some, (zero, zero))
        stats_y[0, i : i + 1, :] = first
        stats_y[0, images + i : images + i + 1, :] = second

    def stat_copy(half, d):
        buffer = (stats_y, stats_z)[half]
        return pltpu.make_async_remote_copy(
            src_ref=buffer.at[0],
            dst_ref=buffer.at[d],
            send_sem=stat_send.at[half, d - 1],
            recv_sem=stat_recv.at[half, d - 1],
            device_id={"tp": peers(me, (d,))[half]},
            device_id_type=MESH,
        )

    for d in range(1, SIDE):
        stat_copy(0, d).start()
    for d in range(1, SIDE):
        stat_copy(0, d).wait_recv()
    stats_z[0] = stats_y[0] + stats_y[1] + stats_y[2] + stats_y[3]
    for d in range(1, SIDE):
        stat_copy(1, d).start()
    store.wait()
    for origin in range(TP):
        write_up(origin).wait()
    for d in range(1, SIDE):
        stat_copy(1, d).wait_recv()
    mean_ref[...] = (stats_z[0] + stats_z[1] + stats_z[2] + stats_z[3]) * (1.0 / full_width)
    for half in range(2):
        for d in range(1, SIDE):
            stat_copy(half, d).wait_send()


def gather(out_grad, pre_act, gain, w_down, w_up_t, normed_t, ctx_count, images, full_width):
    rows, width = out_grad.shape
    channels, units = w_up_t.shape
    features = w_down.shape[0]
    vmem = pl.BlockSpec(memory_space=pltpu.VMEM)
    anywhere = pl.BlockSpec(memory_space=pl.ANY)
    dma = pltpu.SemaphoreType.DMA
    each = units // ctx_count
    return pl.pallas_call(
        functools.partial(gather_kernel, full_width),
        out_shape=(
            jax.ShapeDtypeStruct((channels, rows), jnp.float32),
            jax.ShapeDtypeStruct((ctx_count, channels + width, each), jnp.bfloat16),
            jax.ShapeDtypeStruct((2 * images, rows // images), jnp.float32),
            jax.ShapeDtypeStruct((2, width), jnp.float32),
        ),
        in_specs=[vmem, vmem, vmem, anywhere, anywhere, anywhere],
        out_specs=(anywhere, anywhere, vmem, vmem),
        scratch_shapes=[
            pltpu.VMEM((TP, rows, width), jnp.bfloat16),
            pltpu.VMEM((TP, rows, width), jnp.bfloat16),
            pltpu.VMEM((features, width), jnp.bfloat16),
            pltpu.VMEM((channels, units), jnp.bfloat16),
            pltpu.VMEM((channels, rows), jnp.bfloat16),
            pltpu.VMEM((rows, width), jnp.float32),
            pltpu.VMEM((rows, width), jnp.bfloat16),
            pltpu.VMEM((rows, width), jnp.float32),
            pltpu.VMEM((features, width), jnp.float32),
            pltpu.VMEM((channels, rows), jnp.float32),
            pltpu.VMEM((ctx_count, channels, each), jnp.float32),
            pltpu.VMEM((ctx_count, channels, each), jnp.bfloat16),
            pltpu.VMEM((channels, 1), jnp.float32),
            pltpu.VMEM((SIDE, 2 * images, rows // images), jnp.float32),
            pltpu.VMEM((SIDE, 2 * images, rows // images), jnp.float32),
            dma((3,)),
            dma((2, TP)),
            dma((QUARTERS, TP - 1)),
            dma((QUARTERS, TP - 1)),
            dma((QUARTERS, TP - 1)),
            dma((QUARTERS, TP - 1)),
            dma((2, SIDE - 1)),
            dma((2, SIDE - 1)),
        ],
        compiler_params=pltpu.CompilerParams(
            collective_id=0, has_side_effects=True, vmem_limit_bytes=VMEM_LIMIT
        ),
        cost_estimate=pl.CostEstimate(
            flops=4 * rows * units * (channels + width), bytes_accessed=30 * 2**20, transcendentals=0
        ),
        name="gather",
    )(out_grad, pre_act, gain, w_down, w_up_t, normed_t)


HALVES = 2
LANES = 128


def hand_kernel(
    grad_scale,
    norm_hbm,
    normed_hbm,
    gain_row,
    std_ref,
    owner_ref,
    bias_ref,
    mean_ref,
    sum_ref,
    final,
    own_y, next_y, far_y, prev_y,
    own_z, next_z, far_z, prev_z,
    message,
    norm_ref,
    normed_ref,
    gain_ref,
    product,
    sums,
    load_sem, near_send, near_recv, relay_send, relay_recv, cross_send, cross_recv, own_sem, sum_send, sum_recv,
):
    me = lax.axis_index("tp")
    group = lax.axis_index("ctx")
    ctx_count = sums.shape[0]
    torus = [Torus(half, me) for half in range(HALVES)]
    held = [[own_y, next_y, far_y, prev_y], [own_z, next_z, far_z, prev_z]]
    images, channels, _ = own_y.shape
    image_rows = norm_ref.shape[1] // images
    chunk = channels // 5

    def along_peer(half, d):
        t = torus[half]
        return t.place(t.along + d, t.cross)

    def cross_peer(half, d):
        t = torus[half]
        return t.place(t.along, t.cross + d)

    barrier = pltpu.get_barrier_semaphore()
    for half in range(HALVES):
        for d in range(1, SIDE):
            pl.semaphore_signal(barrier, inc=1, device_id={"tp": along_peer(half, d)}, device_id_type=MESH)
    for d in range(1, ctx_count):
        pl.semaphore_signal(barrier, inc=1, device_id={"ctx": (group + d) % ctx_count}, device_id_type=MESH)

    loads = [
        pltpu.make_async_copy(norm_hbm, norm_ref, load_sem.at[0]),
        pltpu.make_async_copy(normed_hbm, normed_ref, load_sem.at[1]),
    ]
    for load in loads:
        load.start()
    gain_column(gain_row, gain_ref)

    def sum_copy(d):
        return pltpu.make_async_remote_copy(
            src_ref=sums.at[0],
            dst_ref=sums.at[d],
            send_sem=sum_send.at[d - 1],
            recv_sem=sum_recv.at[d - 1],
            device_id={"ctx": (group + d) % ctx_count},
            device_id_type=MESH,
        )

    def near(half, sign, pair):
        piece = pl.ds(pair * (images // 2), images // 2)
        return pltpu.make_async_remote_copy(
            src_ref=held[half][0].at[piece],
            dst_ref=held[half][3 if sign == 1 else 1].at[piece],
            send_sem=near_send.at[half, sign // 2, pair],
            recv_sem=near_recv.at[half, sign // 2, pair],
            device_id={"tp": along_peer(half, sign)},
            device_id_type=MESH,
        )

    def relay(half, sign):
        pair = sign // 2
        piece = pl.ds(pair * (images // 2), images // 2)
        return pltpu.make_async_remote_copy(
            src_ref=held[half][3 if sign == 1 else 1].at[piece],
            dst_ref=held[half][2].at[piece],
            send_sem=relay_send.at[half, pair],
            recv_sem=relay_recv.at[half, pair],
            device_id={"tp": along_peer(half, sign)},
            device_id_type=MESH,
        )

    def across(half, target, d):
        t = torus[half]
        slot = (t.along + d) % SIDE
        source = t.cross * SIDE + slot if half == 0 else slot * SIDE + t.cross
        spot = final.at[half, pl.ds(pl.multiple_of(source * channels, 16), channels)]
        if target == 0:
            return pltpu.make_async_copy(message.at[half, 0, d], spot, own_sem.at[half, d])
        return pltpu.make_async_remote_copy(
            src_ref=message.at[half, target, d],
            dst_ref=spot,
            send_sem=cross_send.at[half, target - 1, d],
            recv_sem=cross_recv.at[half, target - 1, d],
            device_id={"tp": cross_peer(half, target)},
            device_id_type=MESH,
        )

    for load in loads:
        load.wait()
    for i in range(images):
        rows = pl.ds(i * image_rows, image_rows)
        mean_first, mean_second = mean_ref[i : i + 1, :], mean_ref[images + i : images + i + 1, :]
        inverse = std_ref[:, rows]

        def visual(k, carry):
            part = pl.ds(pl.multiple_of(k * chunk, chunk), chunk)
            value = gain_ref[part, :] * norm_ref[part, rows]
            feature = normed_ref[part, rows].astype(jnp.float32)
            seen = (inverse * (value - mean_first - feature * mean_second)).astype(jnp.bfloat16)
            own_y[i, part, :] = seen[:, :LANES]
            own_z[i, part, :] = seen[:, LANES:]
            return carry

        lax.fori_loop(0, 5, visual, 0)
        if i == 1:
            pl.semaphore_wait(barrier, HALVES * (SIDE - 1) + ctx_count - 1)
        if i % 2:
            for half in range(HALVES):
                near(half, 1, i // 2).start()
                near(half, 3, i // 2).start()
    owners = [owner_ref[0, i] for i in range(images)]
    slots = []
    for i in range(images):
        earlier = jnp.int32(0)
        for j in range(i):
            earlier += (owners[j] == owners[i]).astype(jnp.int32)
        slots.append(owners[i] + earlier)

    def choice(place):
        source, present = jnp.int32(0), jnp.int32(0)
        for i in range(images):
            match = (slots[i] == place).astype(jnp.int32)
            source += i * match
            present += match
        return source, present

    chosen = [[choice(cross_peer(half, target)) for target in range(SIDE)] for half in range(HALVES)]

    def forward(half, d):
        block = held[half][d]
        for target in (2, 1, 3, 0):
            source, present = chosen[half][target]
            spot = message.at[half, target, d]

            def pick(k, carry):
                part = pl.ds(pl.multiple_of(k * chunk, chunk), chunk)
                value = block[source, part, :]
                spot[part, :] = jnp.where(present > 0, value, jnp.zeros_like(value))
                return carry

            lax.fori_loop(0, 5, pick, 0)
            across(half, target, d).start()

    for half in range(HALVES):
        forward(half, 0)
    for half in range(HALVES):
        near(half, 1, 0).wait_recv()
        relay(half, 1).start()
    for half in range(HALVES):
        near(half, 3, 1).wait_recv()
        relay(half, 3).start()
    for half in range(HALVES):
        near(half, 1, 1).wait_recv()
        forward(half, 3)
        near(half, 3, 0).wait_recv()
        forward(half, 1)

    ones = jnp.ones((8, image_rows), jnp.float32)
    columns = [jnp.zeros((8, channels), jnp.float32)] * 2
    for i in range(images):
        rows = pl.ds(i * image_rows, image_rows)
        product[...] = norm_ref[:, rows] * normed_ref[:, rows].astype(jnp.float32)
        columns = [
            total
            + lax.dot_general(
                ones,
                right,
                (((1,), (1,)), ((), ())),
                precision=lax.Precision.HIGHEST,
                preferred_element_type=jnp.float32,
            )
            for total, right in zip(columns, (product[...], norm_ref[:, rows]))
        ]
    sums[0, 0:1, 0:channels] = columns[0][0:1]
    sums[0, 1:2, 0:channels] = columns[1][0:1]
    sums[0, 2:4, 0 : bias_ref.shape[1]] = bias_ref[...]
    for d in range(1, ctx_count):
        sum_copy(d).start()

    for half in range(HALVES):
        relay(half, 1).wait_recv()
        relay(half, 3).wait_recv()
        forward(half, 2)

    for d in range(1, ctx_count):
        sum_copy(d).wait_recv()
    whole = sums[0]
    for d in range(1, ctx_count):
        whole = whole + sums[d]
    sum_ref[...] = whole * grad_scale

    for half in range(HALVES):
        for d in range(SIDE):
            for target in range(1, SIDE):
                across(half, target, d).wait_recv()
            across(half, 0, d).wait()
    for half in range(HALVES):
        for sign in (1, 3):
            for pair in range(2):
                near(half, sign, pair).wait_send()
            relay(half, sign).wait_send()
        for d in range(1, SIDE):
            for e in range(SIDE):
                across(half, d, e).wait_send()
    for d in range(1, ctx_count):
        sum_copy(d).wait_send()


def hand_over(norm_t, normed_t, gain, inverse_std, owner_map, bias, means, grad_scale, ctx_count):
    channels, rows = norm_t.shape
    images = owner_map.shape[1]
    image_rows = rows // images
    vmem = pl.BlockSpec(memory_space=pltpu.VMEM)
    block = pltpu.VMEM((images, channels, LANES), jnp.bfloat16)
    dma = pltpu.SemaphoreType.DMA
    return pl.pallas_call(
        functools.partial(hand_kernel, grad_scale),
        out_shape=(
            jax.ShapeDtypeStruct((8, 1024), jnp.float32),
            jax.ShapeDtypeStruct((HALVES, TP * channels, LANES), jnp.bfloat16),
        ),
        in_specs=[
            pl.BlockSpec(memory_space=pl.ANY),
            pl.BlockSpec(memory_space=pl.ANY),
            vmem,
            vmem,
            pl.BlockSpec(memory_space=pltpu.SMEM),
            vmem,
            vmem,
        ],
        out_specs=(vmem, pl.BlockSpec(memory_space=pl.ANY)),
        scratch_shapes=[block] * 8
        + [
            pltpu.VMEM((HALVES, SIDE, SIDE, channels, LANES), jnp.bfloat16),
            pltpu.VMEM((channels, rows), jnp.float32),
            pltpu.VMEM((channels, rows), jnp.bfloat16),
            pltpu.VMEM((channels, 1), jnp.float32),
            pltpu.VMEM((channels, image_rows), jnp.float32),
            pltpu.VMEM((ctx_count, 8, 1024), jnp.float32),
            dma((2,)),
            dma((HALVES, 2, 2)),
            dma((HALVES, 2, 2)),
            dma((HALVES, 2)),
            dma((HALVES, 2)),
            dma((HALVES, SIDE - 1, SIDE)),
            dma((HALVES, SIDE - 1, SIDE)),
            dma((HALVES, SIDE)),
            dma((ctx_count - 1,)),
            dma((ctx_count - 1,)),
        ],
        compiler_params=pltpu.CompilerParams(
            collective_id=1, has_side_effects=True, vmem_limit_bytes=VMEM_LIMIT
        ),
        cost_estimate=pl.CostEstimate(
            flops=20 * rows * channels, bytes_accessed=200 * 2**20, transcendentals=0
        ),
        name="hand_over",
    )(norm_t, normed_t, gain, inverse_std, owner_map, bias, means)


STEPS = 10


def finish_kernel(
    grad_scale, final_hbm, weight_hbm, sum_ref, out_hbm, grad_w2_hbm, grad_w1_hbm, ln_ref, up_ref, down_ref,
    final, out, weight, grad_w2, grad_w1, in_sem, out_sem,
):
    wide = final.shape[1] // STEPS
    small_in = pltpu.make_async_copy(weight_hbm, weight, in_sem.at[STEPS])
    small_out = [
        pltpu.make_async_copy(grad_w2, grad_w2_hbm, out_sem.at[STEPS]),
        pltpu.make_async_copy(grad_w1, grad_w1_hbm, out_sem.at[STEPS + 1]),
    ]

    def load(k):
        part = pl.ds(pl.multiple_of(k * wide, wide), wide)
        return pltpu.make_async_copy(final_hbm.at[:, part], final.at[:, part], in_sem.at[k])

    def store(k):
        part = pl.ds(pl.multiple_of(k * wide, wide), wide)
        return pltpu.make_async_copy(out.at[:, part], out_hbm.at[:, part], out_sem.at[k])

    load(0).start()
    load(1).start()
    small_in.start()
    for k in range(2, STEPS):
        load(k).start()
    lanes = out.shape[0]
    row = lax.broadcasted_iota(jnp.int32, (lanes, lanes), 0)
    column = lax.broadcasted_iota(jnp.int32, (lanes, lanes), 1)
    identity = jnp.where(row == column, 1.0, 0.0).astype(jnp.bfloat16)

    def turn(k, carry):
        part = pl.ds(pl.multiple_of(k * wide, wide), wide)
        load(k).wait()
        block = jnp.concatenate([final[0, part, :], final[1, part, :]], axis=1)
        out[:, part] = dot_last(identity, block).astype(jnp.bfloat16)
        store(k).start()
        return carry

    lax.fori_loop(0, STEPS // 2, turn, 0)
    small_in.wait()
    channels = grad_w1.shape[0]
    tall, width = grad_w2.shape
    for i in range(tall * width // ((weight.shape[0] - channels) * width)):
        part = weight.shape[0] - channels
        grad_w2[i * part : (i + 1) * part, :] = (
            weight[channels:, i * width : (i + 1) * width].astype(jnp.float32) * grad_scale
        )
    small_out[0].start()
    grad_w1[...] = weight[:channels, :].astype(jnp.float32) * grad_scale
    small_out[1].start()
    lax.fori_loop(STEPS // 2, STEPS, turn, 0)
    ln_ref[...] = sum_ref[0:2, 0 : ln_ref.shape[1]]
    down_ref[...] = sum_ref[2:3, 0 : down_ref.shape[1]]
    up_ref[...] = sum_ref[3:4, 0 : up_ref.shape[1]]
    for copy in small_out:
        copy.wait()
    for k in range(STEPS):
        store(k).wait()


def finish(final, weight, sums, width, grad_scale):
    each = weight.shape[1]
    channels = weight.shape[0] - width
    vmem = pl.BlockSpec(memory_space=pltpu.VMEM)
    anywhere = pl.BlockSpec(memory_space=pl.ANY)
    return pl.pallas_call(
        functools.partial(finish_kernel, grad_scale),
        out_shape=(
            jax.ShapeDtypeStruct((HALVES * LANES, final.shape[1]), jnp.bfloat16),
            jax.ShapeDtypeStruct((each, width), jnp.float32),
            jax.ShapeDtypeStruct((channels, each), jnp.float32),
            jax.ShapeDtypeStruct((2, channels), jnp.float32),
            jax.ShapeDtypeStruct((1, width), jnp.float32),
            jax.ShapeDtypeStruct((1, width), jnp.float32),
        ),
        in_specs=[anywhere, anywhere, vmem],
        out_specs=(anywhere, anywhere, anywhere, vmem, vmem, vmem),
        scratch_shapes=[
            pltpu.VMEM(final.shape, jnp.bfloat16),
            pltpu.VMEM((HALVES * LANES, final.shape[1]), jnp.bfloat16),
            pltpu.VMEM(weight.shape, jnp.bfloat16),
            pltpu.VMEM((each, width), jnp.float32),
            pltpu.VMEM((channels, each), jnp.float32),
            pltpu.SemaphoreType.DMA((STEPS + 1,)),
            pltpu.SemaphoreType.DMA((STEPS + 2,)),
        ],
        compiler_params=pltpu.CompilerParams(vmem_limit_bytes=VMEM_LIMIT),
        name="finish",
    )(final, weight, sums)


def per_device(out_grad, pre_act, normed, inverse_std, w_up, w_down, ln_gain, owner_map):
    ctx_count = lax.axis_size("ctx")
    tp_count = lax.axis_size("tp")
    row_count = out_grad.shape[0]
    grad_scale = float(row_count * ctx_count) ** (-0.5)
    gain = ln_gain
    normed_t = normed.T
    norm_t, weight, means, bias = gather(
        out_grad,
        pre_act,
        gain,
        w_down,
        w_up.T,
        normed_t,
        ctx_count,
        owner_map.shape[1],
        float(normed.shape[1] * tp_count),
    )
    weight = lax.psum_scatter(weight, "ctx", scatter_dimension=0, tiled=True)
    sums, final = hand_over(
        norm_t,
        normed_t,
        gain,
        inverse_std[None, :],
        owner_map,
        bias,
        means,
        grad_scale,
        ctx_count,
    )
    vit_grad, grad_w2, grad_w1_t, ln_grads, bias_up, bias_down = finish(
        final, weight[0], sums, bias.shape[1], grad_scale
    )
    return (grad_w2, grad_w1_t.T, bias_up[0], bias_down[0], ln_grads, vit_grad)


def solution(mesh):
    return jax.shard_map(
        per_device,
        mesh=mesh,
        in_specs=(
            P("ctx", "tp"),
            P("ctx", "tp"),
            P("ctx", "tp"),
            P("ctx"),
            P(None, "tp"),
            P(None, "tp"),
            P("tp"),
            P("ctx", None),
        ),
        out_specs=(
            P("ctx", "tp"),
            P("ctx", "tp"),
            P("tp"),
            P("tp"),
            P(None, "tp"),
            P(("ctx", "tp"), None),
        ),
        check_vma=False,
    )
```

```python
import functools
import math

import jax
import jax.numpy as jnp
from jax import lax
from jax.experimental import pallas as pl
from jax.experimental.pallas import tpu as pltpu
from jax.sharding import PartitionSpec as P

MESH = pl.DeviceIdType.MESH
SIDE = 4
TP = SIDE * SIDE
VMEM_LIMIT = 60 * 2**20


def gelu_parts(linear):
    normal_cdf = 0.5 * (1.0 + lax.erf(linear * 2.0 ** (-0.5)))
    density = jnp.exp(-0.5 * linear * linear) * (2.0 * math.pi) ** (-0.5)
    return (linear * normal_cdf, normal_cdf + linear * density)


def dot(left, right):
    return lax.dot_general(
        left, right, (((1,), (0,)), ((), ())), preferred_element_type=jnp.float32
    )


def row_product(left, right):
    return lax.dot_general(
        left, right, (((0,), (0,)), ((), ())), preferred_element_type=jnp.float32
    )


def dot_last(left, right):
    return lax.dot_general(
        left, right, (((1,), (1,)), ((), ())), preferred_element_type=jnp.float32
    )


def greet(half_targets):
    barrier = pltpu.get_barrier_semaphore()
    for target in half_targets:
        pl.semaphore_signal(barrier, inc=1, device_id={"tp": target}, device_id_type=MESH)


def met(count):
    pl.semaphore_wait(pltpu.get_barrier_semaphore(), count)


def peers(me, steps):
    torus = [Torus(half, me) for half in range(2)]
    return [t.place(t.along + d, t.cross) for t in torus for d in steps]


class Torus:
    def __init__(self, half, me):
        z, y = me // SIDE, me % SIDE
        self.half = half
        self.along, self.cross = (y, z) if half == 0 else (z, y)

    def place(self, along, cross):
        along, cross = along % SIDE, cross % SIDE
        return cross * SIDE + along if self.half == 0 else along * SIDE + cross


QUARTERS = 4
ARRIVALS = (
    (3, 0), (1, 0), (0, 3), (2, 0), (3, 3), (1, 3), (0, 1), (2, 3),
    (3, 1), (0, 2), (1, 1), (3, 2), (2, 1), (1, 2), (2, 2),
)


def full_at(y, z):
    turns = ((y, z), (-y % SIDE, -z % SIDE), (z, y), (-z % SIDE, -y % SIDE))
    return max(ARRIVALS.index(turn) for turn in turns if turn != (0, 0))


FULL_AT = {(y, z): full_at(y, z) for y in range(SIDE) for z in range(SIDE) if (y, z) != (0, 0)}
FULL_AT[(0, 0)] = min(FULL_AT.values())


def gain_column(gain_ref, column_ref):
    channels = gain_ref.shape[0]
    rows = channels // 5
    at = lax.broadcasted_iota(jnp.int32, (rows, channels), 1) - lax.broadcasted_iota(
        jnp.int32, (rows, channels), 0
    )

    def some(k, carry):
        picked = jnp.where(at == k * rows, jnp.broadcast_to(gain_ref[...], (rows, channels)), 0.0)
        column_ref[pl.ds(pl.multiple_of(k * rows, rows), rows), :] = jnp.sum(picked, axis=1, keepdims=True)
        return carry

    lax.fori_loop(0, 5, some, 0)


def numbered(values, index):
    out = jnp.int32(values[0])
    for i, value in enumerate(values[1:], 1):
        out = jnp.where(index == i, jnp.int32(value), out)
    return out


def tree_gather(prepare, me, full_ref, send_sem, recv_sem, consume, complete):
    rows = full_ref.shape[1] // QUARTERS
    torus = [Torus(half, me) for half in range(2)]

    def origin(quarter, along, cross):
        t, sign = torus[quarter // 2], 1 - quarter % 2 * 2
        return t.place(t.along + sign * along + SIDE, t.cross + sign * cross + SIDE)

    def copy(quarter, block, number, target):
        spot = full_ref.at[origin(quarter, *block), pl.ds(quarter * rows, rows)]
        return pltpu.make_async_remote_copy(
            src_ref=spot,
            dst_ref=spot,
            send_sem=send_sem.at[quarter, number],
            recv_sem=recv_sem.at[quarter, number],
            device_id={"tp": origin(quarter, *target)},
            device_id_type=MESH,
        )

    def send(block, seen):
        target = ((block[0] - seen[0]) % SIDE, (block[1] - seen[1]) % SIDE)
        for quarter in range(QUARTERS):
            copy(quarter, block, ARRIVALS.index(seen), target).start()

    send((0, 0), (3, 0))
    send((0, 0), (1, 0))
    send((0, 0), (0, 3))
    send((0, 0), (0, 1))
    prepare()
    for quarter in range(QUARTERS):
        consume(me, quarter)

    def arrive(k, carry):
        along = numbered([block[0] for block in ARRIVALS], k)
        cross = numbered([block[1] for block in ARRIVALS], k)
        for quarter in range(QUARTERS):
            copy(quarter, (along, cross), k, (1, 0)).wait_recv()
        for number, block in enumerate(ARRIVALS):
            if block[1] not in (0, 3):
                continue

            @pl.when(k == number)
            def _():
                if block == (3, 0):
                    send(block, (2, 0))
                if block[1] == 0:
                    send(block, (block[0], 3))
                    send(block, (block[0], 1))
                else:
                    send(block, (block[0], 2))

        for quarter in range(QUARTERS):
            consume(origin(quarter, along, cross), quarter)
        for number in sorted(set(FULL_AT.values())):

            @pl.when(k == number)
            def _():
                for block, at in FULL_AT.items():
                    if at == number:
                        complete(torus[0].place(torus[0].along + block[0], torus[0].cross + block[1]))

        return carry

    lax.fori_loop(0, TP - 1, arrive, 0)

    def drain(k, carry):
        for quarter in range(QUARTERS):
            copy(quarter, (0, 0), k, (1, 0)).wait_send()
        return carry

    return lambda: lax.fori_loop(0, TP - 1, drain, 0)


def gather_kernel(
    full_width, grad_ref, pre_ref, gain_ref, w_down_hbm, w_up_hbm, normed_hbm, norm_hbm, weight_hbm, mean_ref, bias_ref,
    grads, parts, w_down, w_up, normed, total, hidden, slope, gw2, norm, gw1, short, column, stats_y, stats_z,
    load_sem, out_sem, down_send, down_recv, up_send, up_recv, stat_send, stat_recv,
):
    me = lax.axis_index("tp")
    greet(peers(me, (1, 2, 3)))
    loads = [
        pltpu.make_async_copy(source, target, load_sem.at[i])
        for i, (source, target) in enumerate(((w_down_hbm, w_down), (w_up_hbm, w_up), (normed_hbm, normed)))
    ]
    for load in loads:
        load.start()
    grads[me] = grad_ref[...]
    met(6)
    rows_all, width = grad_ref.shape
    quarter = rows_all // QUARTERS
    per_owner = gw1.shape[2] // width
    channels = norm.shape[0]
    chunk = channels // 5
    images = mean_ref.shape[0] // 2
    image_rows = rows_all // images

    def block_of(ref, origin, first, count):
        within = pl.ds(pl.multiple_of(origin % per_owner * width, width), width)
        return ref.at[origin // per_owner, pl.ds(first, count), within]

    def write_down(origin):
        return pltpu.make_async_copy(
            block_of(short, origin, 0, width), block_of(weight_hbm, origin, channels, width), out_sem.at[0, origin]
        )

    def prepare_down():
        def rows_of(i, carry):
            rows = pl.ds(pl.multiple_of(i * 64, 64), 64)
            value, steep = gelu_parts(pre_ref[rows, :].astype(jnp.float32))
            hidden[rows, :] = value.astype(jnp.bfloat16)
            slope[rows, :] = steep
            return carry

        lax.fori_loop(0, rows_all // 64, rows_of, 0)
        bias_ref[0:1, :] = jnp.sum(grad_ref[...].astype(jnp.float32), axis=0, keepdims=True)
        total[...] = jnp.zeros_like(total)
        gw2[...] = jnp.zeros_like(gw2)
        loads[0].wait()

    def consume_down(origin, part):
        rows = pl.ds(part * quarter, quarter)
        features = pl.ds(pl.multiple_of(origin * width, width), width)
        block = grads[origin, rows, :]
        total[rows, :] += dot(block, w_down[features, :])
        gw2[features, :] += row_product(block, hidden[rows, :])

    def complete_down(origin):
        features = pl.ds(pl.multiple_of(origin * width, width), width)
        block_of(short, origin, 0, width)[...] = gw2[features, :].astype(jnp.bfloat16)
        write_down(origin).start()

    drain_down = tree_gather(prepare_down, me, grads, down_send, down_recv, consume_down, complete_down)
    part = (total[...] * slope[...]).astype(jnp.bfloat16)
    parts[me] = part

    def write_up(origin):
        return pltpu.make_async_copy(
            block_of(short, origin, 0, channels), block_of(weight_hbm, origin, 0, channels), out_sem.at[1, origin]
        )

    def prepare_up():
        bias_ref[1:2, :] = jnp.sum(parts[me].astype(jnp.float32), axis=0, keepdims=True)
        norm[...] = jnp.zeros_like(norm)
        gw1[...] = jnp.zeros_like(gw1)
        gain_column(gain_ref, column)
        for origin in range(TP):
            write_down(origin).wait()
        for load in loads[1:]:
            load.wait()

    def consume_up(origin, part):
        rows = pl.ds(part * quarter, quarter)
        units = pl.ds(pl.multiple_of(origin * width, width), width)
        within = pl.ds(pl.multiple_of(origin % per_owner * width, width), width)
        block = parts[origin, rows, :]
        norm[:, rows] += dot_last(w_up[:, units], block)
        gw1[origin // per_owner, :, within] += dot(normed[:, rows], block)

    def complete_up(origin):
        within = pl.ds(pl.multiple_of(origin % per_owner * width, width), width)
        owner = origin // per_owner

        def some(k, carry):
            part = pl.ds(pl.multiple_of(k * chunk, chunk), chunk)
            short[owner, part, within] = gw1[owner, part, within].astype(jnp.bfloat16)
            return carry

        lax.fori_loop(0, 5, some, 0)
        write_up(origin).start()

    drain_up = tree_gather(prepare_up, me, parts, up_send, up_recv, consume_up, complete_up)
    store = pltpu.make_async_copy(norm, norm_hbm, load_sem.at[0])
    store.start()

    for i in range(images):
        rows = pl.ds(i * image_rows, image_rows)

        def some(k, carry):
            part = pl.ds(pl.multiple_of(k * chunk, chunk), chunk)
            feature = normed[part, rows].astype(jnp.float32)
            gained = column[part, :] * norm[part, rows]
            return (
                carry[0] + jnp.sum(gained, axis=0, keepdims=True),
                carry[1] + jnp.sum(gained * feature, axis=0, keepdims=True),
            )

        zero = jnp.zeros((1, image_rows), jnp.float32)
        first, second = lax.fori_loop(0, 5, some, (zero, zero))
        stats_y[0, i : i + 1, :] = first
        stats_y[0, images + i : images + i + 1, :] = second

    def stat_copy(half, d):
        buffer = (stats_y, stats_z)[half]
        return pltpu.make_async_remote_copy(
            src_ref=buffer.at[0],
            dst_ref=buffer.at[d],
            send_sem=stat_send.at[half, d - 1],
            recv_sem=stat_recv.at[half, d - 1],
            device_id={"tp": peers(me, (d,))[half]},
            device_id_type=MESH,
        )

    for d in range(1, SIDE):
        stat_copy(0, d).start()
    for d in range(1, SIDE):
        stat_copy(0, d).wait_recv()
    stats_z[0] = stats_y[0] + stats_y[1] + stats_y[2] + stats_y[3]
    for d in range(1, SIDE):
        stat_copy(1, d).start()
    drain_down()
    drain_up()
    store.wait()
    for origin in range(TP):
        write_up(origin).wait()
    for d in range(1, SIDE):
        stat_copy(1, d).wait_recv()
    mean_ref[...] = (stats_z[0] + stats_z[1] + stats_z[2] + stats_z[3]) * (1.0 / full_width)
    for half in range(2):
        for d in range(1, SIDE):
            stat_copy(half, d).wait_send()


def gather(out_grad, pre_act, gain, w_down, w_up_t, normed_t, ctx_count, images, full_width):
    rows, width = out_grad.shape
    channels, units = w_up_t.shape
    features = w_down.shape[0]
    vmem = pl.BlockSpec(memory_space=pltpu.VMEM)
    anywhere = pl.BlockSpec(memory_space=pl.ANY)
    dma = pltpu.SemaphoreType.DMA
    each = units // ctx_count
    return pl.pallas_call(
        functools.partial(gather_kernel, full_width),
        out_shape=(
            jax.ShapeDtypeStruct((channels, rows), jnp.float32),
            jax.ShapeDtypeStruct((ctx_count, channels + width, each), jnp.bfloat16),
            jax.ShapeDtypeStruct((2 * images, rows // images), jnp.float32),
            jax.ShapeDtypeStruct((2, width), jnp.float32),
        ),
        in_specs=[vmem, vmem, vmem, anywhere, anywhere, anywhere],
        out_specs=(anywhere, anywhere, vmem, vmem),
        scratch_shapes=[
            pltpu.VMEM((TP, rows, width), jnp.bfloat16),
            pltpu.VMEM((TP, rows, width), jnp.bfloat16),
            pltpu.VMEM((features, width), jnp.bfloat16),
            pltpu.VMEM((channels, units), jnp.bfloat16),
            pltpu.VMEM((channels, rows), jnp.bfloat16),
            pltpu.VMEM((rows, width), jnp.float32),
            pltpu.VMEM((rows, width), jnp.bfloat16),
            pltpu.VMEM((rows, width), jnp.float32),
            pltpu.VMEM((features, width), jnp.float32),
            pltpu.VMEM((channels, rows), jnp.float32),
            pltpu.VMEM((ctx_count, channels, each), jnp.float32),
            pltpu.VMEM((ctx_count, channels, each), jnp.bfloat16),
            pltpu.VMEM((channels, 1), jnp.float32),
            pltpu.VMEM((SIDE, 2 * images, rows // images), jnp.float32),
            pltpu.VMEM((SIDE, 2 * images, rows // images), jnp.float32),
            dma((3,)),
            dma((2, TP)),
            dma((QUARTERS, TP - 1)),
            dma((QUARTERS, TP - 1)),
            dma((QUARTERS, TP - 1)),
            dma((QUARTERS, TP - 1)),
            dma((2, SIDE - 1)),
            dma((2, SIDE - 1)),
        ],
        compiler_params=pltpu.CompilerParams(
            collective_id=0, has_side_effects=True, vmem_limit_bytes=VMEM_LIMIT
        ),
        cost_estimate=pl.CostEstimate(
            flops=4 * rows * units * (channels + width), bytes_accessed=30 * 2**20, transcendentals=0
        ),
        name="gather",
    )(out_grad, pre_act, gain, w_down, w_up_t, normed_t)


HALVES = 2
LANES = 128


def hand_kernel(
    grad_scale,
    norm_hbm,
    normed_hbm,
    gain_row,
    std_ref,
    owner_ref,
    bias_ref,
    mean_ref,
    sum_ref,
    final,
    own_y, next_y, far_y, prev_y,
    own_z, next_z, far_z, prev_z,
    message,
    norm_ref,
    normed_ref,
    gain_ref,
    product,
    sums,
    load_sem, near_send, near_recv, relay_send, relay_recv, cross_send, cross_recv, own_sem, sum_send, sum_recv,
):
    me = lax.axis_index("tp")
    group = lax.axis_index("ctx")
    ctx_count = sums.shape[0]
    torus = [Torus(half, me) for half in range(HALVES)]
    held = [[own_y, next_y, far_y, prev_y], [own_z, next_z, far_z, prev_z]]
    images, channels, _ = own_y.shape
    image_rows = norm_ref.shape[1] // images
    chunk = channels // 5

    def along_peer(half, d):
        t = torus[half]
        return t.place(t.along + d, t.cross)

    def cross_peer(half, d):
        t = torus[half]
        return t.place(t.along, t.cross + d)

    barrier = pltpu.get_barrier_semaphore()
    for half in range(HALVES):
        for d in range(1, SIDE):
            pl.semaphore_signal(barrier, inc=1, device_id={"tp": along_peer(half, d)}, device_id_type=MESH)
    for d in range(1, ctx_count):
        pl.semaphore_signal(barrier, inc=1, device_id={"ctx": (group + d) % ctx_count}, device_id_type=MESH)

    loads = [
        pltpu.make_async_copy(norm_hbm, norm_ref, load_sem.at[0]),
        pltpu.make_async_copy(normed_hbm, normed_ref, load_sem.at[1]),
    ]
    for load in loads:
        load.start()
    gain_column(gain_row, gain_ref)

    def sum_copy(d):
        return pltpu.make_async_remote_copy(
            src_ref=sums.at[0],
            dst_ref=sums.at[d],
            send_sem=sum_send.at[d - 1],
            recv_sem=sum_recv.at[d - 1],
            device_id={"ctx": (group + d) % ctx_count},
            device_id_type=MESH,
        )

    def near(half, sign, pair):
        piece = pl.ds(pair * (images // 2), images // 2)
        return pltpu.make_async_remote_copy(
            src_ref=held[half][0].at[piece],
            dst_ref=held[half][3 if sign == 1 else 1].at[piece],
            send_sem=near_send.at[half, sign // 2, pair],
            recv_sem=near_recv.at[half, sign // 2, pair],
            device_id={"tp": along_peer(half, sign)},
            device_id_type=MESH,
        )

    def relay(half, sign):
        pair = sign // 2
        piece = pl.ds(pair * (images // 2), images // 2)
        return pltpu.make_async_remote_copy(
            src_ref=held[half][3 if sign == 1 else 1].at[piece],
            dst_ref=held[half][2].at[piece],
            send_sem=relay_send.at[half, pair],
            recv_sem=relay_recv.at[half, pair],
            device_id={"tp": along_peer(half, sign)},
            device_id_type=MESH,
        )

    def across(half, target, d):
        t = torus[half]
        slot = (t.along + d) % SIDE
        source = t.cross * SIDE + slot if half == 0 else slot * SIDE + t.cross
        spot = final.at[half, pl.ds(pl.multiple_of(source * channels, 16), channels)]
        if target == 0:
            return pltpu.make_async_copy(message.at[half, 0, d], spot, own_sem.at[half, d])
        return pltpu.make_async_remote_copy(
            src_ref=message.at[half, target, d],
            dst_ref=spot,
            send_sem=cross_send.at[half, target - 1, d],
            recv_sem=cross_recv.at[half, target - 1, d],
            device_id={"tp": cross_peer(half, target)},
            device_id_type=MESH,
        )

    for load in loads:
        load.wait()
    for i in range(images):
        rows = pl.ds(i * image_rows, image_rows)
        mean_first, mean_second = mean_ref[i : i + 1, :], mean_ref[images + i : images + i + 1, :]
        inverse = std_ref[:, rows]

        def visual(k, carry):
            part = pl.ds(pl.multiple_of(k * chunk, chunk), chunk)
            value = gain_ref[part, :] * norm_ref[part, rows]
            feature = normed_ref[part, rows].astype(jnp.float32)
            seen = (inverse * (value - mean_first - feature * mean_second)).astype(jnp.bfloat16)
            own_y[i, part, :] = seen[:, :LANES]
            own_z[i, part, :] = seen[:, LANES:]
            return carry

        lax.fori_loop(0, 5, visual, 0)
        if i == 1:
            pl.semaphore_wait(barrier, HALVES * (SIDE - 1) + ctx_count - 1)
        if i % 2:
            for half in range(HALVES):
                near(half, 1, i // 2).start()
                near(half, 3, i // 2).start()
    owners = [owner_ref[0, i] for i in range(images)]
    slots = []
    for i in range(images):
        earlier = jnp.int32(0)
        for j in range(i):
            earlier += (owners[j] == owners[i]).astype(jnp.int32)
        slots.append(owners[i] + earlier)

    def choice(place):
        source, present = jnp.int32(0), jnp.int32(0)
        for i in range(images):
            match = (slots[i] == place).astype(jnp.int32)
            source += i * match
            present += match
        return source, present

    chosen = [[choice(cross_peer(half, target)) for target in range(SIDE)] for half in range(HALVES)]

    def forward(half, d):
        block = held[half][d]
        for target in (2, 1, 3, 0):
            source, present = chosen[half][target]
            spot = message.at[half, target, d]

            def pick(k, carry):
                part = pl.ds(pl.multiple_of(k * chunk, chunk), chunk)
                value = block[source, part, :]
                spot[part, :] = jnp.where(present > 0, value, jnp.zeros_like(value))
                return carry

            lax.fori_loop(0, 5, pick, 0)
            across(half, target, d).start()

    for half in range(HALVES):
        forward(half, 0)
    for half in range(HALVES):
        near(half, 1, 0).wait_recv()
        relay(half, 1).start()
    for half in range(HALVES):
        near(half, 3, 1).wait_recv()
        relay(half, 3).start()
    for half in range(HALVES):
        near(half, 1, 1).wait_recv()
        forward(half, 3)
        near(half, 3, 0).wait_recv()
        forward(half, 1)

    ones = jnp.ones((8, image_rows), jnp.float32)
    columns = [jnp.zeros((8, channels), jnp.float32)] * 2
    for i in range(images):
        rows = pl.ds(i * image_rows, image_rows)
        product[...] = norm_ref[:, rows] * normed_ref[:, rows].astype(jnp.float32)
        columns = [
            total
            + lax.dot_general(
                ones,
                right,
                (((1,), (1,)), ((), ())),
                precision=lax.Precision.HIGHEST,
                preferred_element_type=jnp.float32,
            )
            for total, right in zip(columns, (product[...], norm_ref[:, rows]))
        ]
    sums[0, 0:1, 0:channels] = columns[0][0:1]
    sums[0, 1:2, 0:channels] = columns[1][0:1]
    sums[0, 2:4, 0 : bias_ref.shape[1]] = bias_ref[...]
    for d in range(1, ctx_count):
        sum_copy(d).start()

    for half in range(HALVES):
        relay(half, 1).wait_recv()
        relay(half, 3).wait_recv()
        forward(half, 2)

    for d in range(1, ctx_count):
        sum_copy(d).wait_recv()
    whole = sums[0]
    for d in range(1, ctx_count):
        whole = whole + sums[d]
    sum_ref[...] = whole * grad_scale

    for half in range(HALVES):
        for d in range(SIDE):
            for target in range(1, SIDE):
                across(half, target, d).wait_recv()
            across(half, 0, d).wait()
    for half in range(HALVES):
        for sign in (1, 3):
            for pair in range(2):
                near(half, sign, pair).wait_send()
            relay(half, sign).wait_send()
        for d in range(1, SIDE):
            for e in range(SIDE):
                across(half, d, e).wait_send()
    for d in range(1, ctx_count):
        sum_copy(d).wait_send()


def hand_over(norm_t, normed_t, gain, inverse_std, owner_map, bias, means, grad_scale, ctx_count):
    channels, rows = norm_t.shape
    images = owner_map.shape[1]
    image_rows = rows // images
    vmem = pl.BlockSpec(memory_space=pltpu.VMEM)
    block = pltpu.VMEM((images, channels, LANES), jnp.bfloat16)
    dma = pltpu.SemaphoreType.DMA
    return pl.pallas_call(
        functools.partial(hand_kernel, grad_scale),
        out_shape=(
            jax.ShapeDtypeStruct((8, 1024), jnp.float32),
            jax.ShapeDtypeStruct((HALVES, TP * channels, LANES), jnp.bfloat16),
        ),
        in_specs=[
            pl.BlockSpec(memory_space=pl.ANY),
            pl.BlockSpec(memory_space=pl.ANY),
            vmem,
            vmem,
            pl.BlockSpec(memory_space=pltpu.SMEM),
            vmem,
            vmem,
        ],
        out_specs=(vmem, pl.BlockSpec(memory_space=pl.ANY)),
        scratch_shapes=[block] * 8
        + [
            pltpu.VMEM((HALVES, SIDE, SIDE, channels, LANES), jnp.bfloat16),
            pltpu.VMEM((channels, rows), jnp.float32),
            pltpu.VMEM((channels, rows), jnp.bfloat16),
            pltpu.VMEM((channels, 1), jnp.float32),
            pltpu.VMEM((channels, image_rows), jnp.float32),
            pltpu.VMEM((ctx_count, 8, 1024), jnp.float32),
            dma((2,)),
            dma((HALVES, 2, 2)),
            dma((HALVES, 2, 2)),
            dma((HALVES, 2)),
            dma((HALVES, 2)),
            dma((HALVES, SIDE - 1, SIDE)),
            dma((HALVES, SIDE - 1, SIDE)),
            dma((HALVES, SIDE)),
            dma((ctx_count - 1,)),
            dma((ctx_count - 1,)),
        ],
        compiler_params=pltpu.CompilerParams(
            collective_id=1, has_side_effects=True, vmem_limit_bytes=VMEM_LIMIT
        ),
        cost_estimate=pl.CostEstimate(
            flops=20 * rows * channels, bytes_accessed=200 * 2**20, transcendentals=0
        ),
        name="hand_over",
    )(norm_t, normed_t, gain, inverse_std, owner_map, bias, means)


STEPS = 4


def finish_kernel(
    grad_scale, final_hbm, weight_hbm, sum_ref, out_hbm, grad_w2_hbm, grad_w1_hbm, ln_ref, up_ref, down_ref,
    final, out, weight, grad_w2, grad_w1, in_sem, out_sem,
):
    wide = final.shape[1] // STEPS
    small_in = pltpu.make_async_copy(weight_hbm, weight, in_sem.at[STEPS])
    small_out = [
        pltpu.make_async_copy(grad_w2, grad_w2_hbm, out_sem.at[STEPS]),
        pltpu.make_async_copy(grad_w1, grad_w1_hbm, out_sem.at[STEPS + 1]),
    ]

    def load(k):
        part = pl.ds(pl.multiple_of(k * wide, wide), wide)
        return pltpu.make_async_copy(final_hbm.at[:, part], final.at[:, part], in_sem.at[k])

    def store(k):
        part = pl.ds(pl.multiple_of(k * wide, wide), wide)
        return pltpu.make_async_copy(out.at[:, part], out_hbm.at[:, part], out_sem.at[k])

    load(0).start()
    load(1).start()
    small_in.start()
    for k in range(2, STEPS):
        load(k).start()
    lanes = out.shape[0]
    row = lax.broadcasted_iota(jnp.int32, (lanes, lanes), 0)
    column = lax.broadcasted_iota(jnp.int32, (lanes, lanes), 1)
    identity = jnp.where(row == column, 1.0, 0.0).astype(jnp.bfloat16)

    def turn(k, carry):
        part = pl.ds(pl.multiple_of(k * wide, wide), wide)
        load(k).wait()
        block = jnp.concatenate([final[0, part, :], final[1, part, :]], axis=1)
        out[:, part] = dot_last(identity, block).astype(jnp.bfloat16)
        store(k).start()
        return carry

    lax.fori_loop(0, STEPS // 2, turn, 0)
    small_in.wait()
    channels = grad_w1.shape[0]
    tall, width = grad_w2.shape
    for i in range(tall * width // ((weight.shape[0] - channels) * width)):
        part = weight.shape[0] - channels
        grad_w2[i * part : (i + 1) * part, :] = (
            weight[channels:, i * width : (i + 1) * width].astype(jnp.float32) * grad_scale
        )
    small_out[0].start()
    grad_w1[...] = weight[:channels, :].astype(jnp.float32) * grad_scale
    small_out[1].start()
    lax.fori_loop(STEPS // 2, STEPS, turn, 0)
    ln_ref[...] = sum_ref[0:2, 0 : ln_ref.shape[1]]
    down_ref[...] = sum_ref[2:3, 0 : down_ref.shape[1]]
    up_ref[...] = sum_ref[3:4, 0 : up_ref.shape[1]]
    for copy in small_out:
        copy.wait()
    for k in range(STEPS):
        store(k).wait()


def finish(final, weight, sums, width, grad_scale):
    each = weight.shape[1]
    channels = weight.shape[0] - width
    vmem = pl.BlockSpec(memory_space=pltpu.VMEM)
    anywhere = pl.BlockSpec(memory_space=pl.ANY)
    return pl.pallas_call(
        functools.partial(finish_kernel, grad_scale),
        out_shape=(
            jax.ShapeDtypeStruct((HALVES * LANES, final.shape[1]), jnp.bfloat16),
            jax.ShapeDtypeStruct((each, width), jnp.float32),
            jax.ShapeDtypeStruct((channels, each), jnp.float32),
            jax.ShapeDtypeStruct((2, channels), jnp.float32),
            jax.ShapeDtypeStruct((1, width), jnp.float32),
            jax.ShapeDtypeStruct((1, width), jnp.float32),
        ),
        in_specs=[anywhere, anywhere, vmem],
        out_specs=(anywhere, anywhere, anywhere, vmem, vmem, vmem),
        scratch_shapes=[
            pltpu.VMEM(final.shape, jnp.bfloat16),
            pltpu.VMEM((HALVES * LANES, final.shape[1]), jnp.bfloat16),
            pltpu.VMEM(weight.shape, jnp.bfloat16),
            pltpu.VMEM((each, width), jnp.float32),
            pltpu.VMEM((channels, each), jnp.float32),
            pltpu.SemaphoreType.DMA((STEPS + 1,)),
            pltpu.SemaphoreType.DMA((STEPS + 2,)),
        ],
        compiler_params=pltpu.CompilerParams(vmem_limit_bytes=VMEM_LIMIT),
        name="finish",
    )(final, weight, sums)


def per_device(out_grad, pre_act, normed, inverse_std, w_up, w_down, ln_gain, owner_map):
    ctx_count = lax.axis_size("ctx")
    tp_count = lax.axis_size("tp")
    row_count = out_grad.shape[0]
    grad_scale = float(row_count * ctx_count) ** (-0.5)
    gain = ln_gain
    normed_t = normed.T
    norm_t, weight, means, bias = gather(
        out_grad,
        pre_act,
        gain,
        w_down,
        w_up.T,
        normed_t,
        ctx_count,
        owner_map.shape[1],
        float(normed.shape[1] * tp_count),
    )
    weight = lax.psum_scatter(weight, "ctx", scatter_dimension=0, tiled=True)
    sums, final = hand_over(
        norm_t,
        normed_t,
        gain,
        inverse_std[None, :],
        owner_map,
        bias,
        means,
        grad_scale,
        ctx_count,
    )
    vit_grad, grad_w2, grad_w1_t, ln_grads, bias_up, bias_down = finish(
        final, weight[0], sums, bias.shape[1], grad_scale
    )
    return (grad_w2, grad_w1_t.T, bias_up[0], bias_down[0], ln_grads, vit_grad)


def solution(mesh):
    return jax.shard_map(
        per_device,
        mesh=mesh,
        in_specs=(
            P("ctx", "tp"),
            P("ctx", "tp"),
            P("ctx", "tp"),
            P("ctx"),
            P(None, "tp"),
            P(None, "tp"),
            P("tp"),
            P("ctx", None),
        ),
        out_specs=(
            P("ctx", "tp"),
            P("ctx", "tp"),
            P("tp"),
            P("tp"),
            P(None, "tp"),
            P(("ctx", "tp"), None),
        ),
        check_vma=False,
    )
```

```python
import functools
import math

import jax
import jax.numpy as jnp
from jax import lax
from jax.experimental import pallas as pl
from jax.experimental.pallas import tpu as pltpu
from jax.sharding import PartitionSpec as P

MESH = pl.DeviceIdType.MESH
SIDE = 4
TP = SIDE * SIDE
VMEM_LIMIT = 60 * 2**20


def gelu_parts(linear):
    normal_cdf = 0.5 * (1.0 + lax.erf(linear * 2.0 ** (-0.5)))
    density = jnp.exp(-0.5 * linear * linear) * (2.0 * math.pi) ** (-0.5)
    return (linear * normal_cdf, normal_cdf + linear * density)


def dot(left, right):
    return lax.dot_general(
        left, right, (((1,), (0,)), ((), ())), preferred_element_type=jnp.float32
    )


def row_product(left, right):
    return lax.dot_general(
        left, right, (((0,), (0,)), ((), ())), preferred_element_type=jnp.float32
    )


def dot_last(left, right):
    return lax.dot_general(
        left, right, (((1,), (1,)), ((), ())), preferred_element_type=jnp.float32
    )


def greet(half_targets):
    barrier = pltpu.get_barrier_semaphore()
    for target in half_targets:
        pl.semaphore_signal(barrier, inc=1, device_id={"tp": target}, device_id_type=MESH)


def met(count):
    pl.semaphore_wait(pltpu.get_barrier_semaphore(), count)


def peers(me, steps):
    torus = [Torus(half, me) for half in range(2)]
    return [t.place(t.along + d, t.cross) for t in torus for d in steps]


class Torus:
    def __init__(self, half, me):
        z, y = me // SIDE, me % SIDE
        self.half = half
        self.along, self.cross = (y, z) if half == 0 else (z, y)

    def place(self, along, cross):
        along, cross = along % SIDE, cross % SIDE
        return cross * SIDE + along if self.half == 0 else along * SIDE + cross


QUARTERS = 4
ARRIVALS = (
    (3, 0), (1, 0), (0, 3), (0, 1), (2, 0), (3, 3), (3, 1), (1, 3),
    (1, 1), (0, 2), (2, 3), (2, 1), (3, 2), (1, 2), (2, 2),
)


def full_at(y, z):
    turns = ((y, z), (-y % SIDE, -z % SIDE), (z, y), (-z % SIDE, -y % SIDE))
    return max(ARRIVALS.index(turn) for turn in turns if turn != (0, 0))


FULL_AT = {(y, z): full_at(y, z) for y in range(SIDE) for z in range(SIDE) if (y, z) != (0, 0)}
FULL_AT[(0, 0)] = min(FULL_AT.values())


def gain_column(gain_ref, column_ref):
    channels = gain_ref.shape[0]
    rows = channels // 5
    at = lax.broadcasted_iota(jnp.int32, (rows, channels), 1) - lax.broadcasted_iota(
        jnp.int32, (rows, channels), 0
    )

    def some(k, carry):
        picked = jnp.where(at == k * rows, jnp.broadcast_to(gain_ref[...], (rows, channels)), 0.0)
        column_ref[pl.ds(pl.multiple_of(k * rows, rows), rows), :] = jnp.sum(picked, axis=1, keepdims=True)
        return carry

    lax.fori_loop(0, 5, some, 0)


def numbered(values, index):
    out = jnp.int32(values[0])
    for i, value in enumerate(values[1:], 1):
        out = jnp.where(index == i, jnp.int32(value), out)
    return out


def tree_gather(prepare, me, full_ref, send_sem, recv_sem, consume, complete):
    rows = full_ref.shape[1] // QUARTERS
    torus = [Torus(half, me) for half in range(2)]

    def origin(quarter, along, cross):
        t, sign = torus[quarter // 2], 1 - quarter % 2 * 2
        return t.place(t.along + sign * along + SIDE, t.cross + sign * cross + SIDE)

    def copy(quarter, block, number, target):
        spot = full_ref.at[origin(quarter, *block), pl.ds(quarter * rows, rows)]
        return pltpu.make_async_remote_copy(
            src_ref=spot,
            dst_ref=spot,
            send_sem=send_sem.at[quarter, number],
            recv_sem=recv_sem.at[quarter, number],
            device_id={"tp": origin(quarter, *target)},
            device_id_type=MESH,
        )

    def send(block, seen):
        target = ((block[0] - seen[0]) % SIDE, (block[1] - seen[1]) % SIDE)
        for quarter in range(QUARTERS):
            copy(quarter, block, ARRIVALS.index(seen), target).start()

    send((0, 0), (3, 0))
    send((0, 0), (1, 0))
    send((0, 0), (0, 3))
    send((0, 0), (0, 1))
    prepare()
    for quarter in range(QUARTERS):
        consume(me, quarter)

    def arrive(k, carry):
        along = numbered([block[0] for block in ARRIVALS], k)
        cross = numbered([block[1] for block in ARRIVALS], k)
        for quarter in range(QUARTERS):
            copy(quarter, (along, cross), k, (1, 0)).wait_recv()
        for number, block in enumerate(ARRIVALS):
            if block[1] not in (0, 3):
                continue

            @pl.when(k == number)
            def _():
                if block == (3, 0):
                    send(block, (2, 0))
                if block[1] == 0:
                    send(block, (block[0], 3))
                    send(block, (block[0], 1))
                else:
                    send(block, (block[0], 2))

        for quarter in range(QUARTERS):
            consume(origin(quarter, along, cross), quarter)
        for number in sorted(set(FULL_AT.values())):

            @pl.when(k == number)
            def _():
                for block, at in FULL_AT.items():
                    if at == number:
                        complete(torus[0].place(torus[0].along + block[0], torus[0].cross + block[1]))

        return carry

    lax.fori_loop(0, TP - 1, arrive, 0)

    def drain(k, carry):
        for quarter in range(QUARTERS):
            copy(quarter, (0, 0), k, (1, 0)).wait_send()
        return carry

    return lambda: lax.fori_loop(0, TP - 1, drain, 0)


def gather_kernel(
    full_width, grad_ref, pre_ref, gain_ref, w_down_hbm, w_up_hbm, normed_hbm, norm_hbm, weight_hbm, mean_ref, bias_ref,
    grads, parts, w_down, w_up, normed, total, hidden, slope, gw2, norm, gw1, short, column, stats_y, stats_z,
    load_sem, out_sem, down_send, down_recv, up_send, up_recv, stat_send, stat_recv,
):
    me = lax.axis_index("tp")
    greet(peers(me, (1, 2, 3)))
    loads = [
        pltpu.make_async_copy(source, target, load_sem.at[i])
        for i, (source, target) in enumerate(((w_down_hbm, w_down), (w_up_hbm, w_up), (normed_hbm, normed)))
    ]
    for load in loads:
        load.start()
    grads[me] = grad_ref[...]
    met(6)
    rows_all, width = grad_ref.shape
    quarter = rows_all // QUARTERS
    per_owner = gw1.shape[2] // width
    channels = norm.shape[0]
    chunk = channels // 5
    images = mean_ref.shape[0] // 2
    image_rows = rows_all // images

    def block_of(ref, origin, first, count):
        within = pl.ds(pl.multiple_of(origin % per_owner * width, width), width)
        return ref.at[origin // per_owner, pl.ds(first, count), within]

    def write_down(origin):
        return pltpu.make_async_copy(
            block_of(short, origin, 0, width), block_of(weight_hbm, origin, channels, width), out_sem.at[0, origin]
        )

    def prepare_down():
        def rows_of(i, carry):
            rows = pl.ds(pl.multiple_of(i * 64, 64), 64)
            value, steep = gelu_parts(pre_ref[rows, :].astype(jnp.float32))
            hidden[rows, :] = value.astype(jnp.bfloat16)
            slope[rows, :] = steep
            return carry

        lax.fori_loop(0, rows_all // 64, rows_of, 0)
        bias_ref[0:1, :] = jnp.sum(grad_ref[...].astype(jnp.float32), axis=0, keepdims=True)
        total[...] = jnp.zeros_like(total)
        gw2[...] = jnp.zeros_like(gw2)
        loads[0].wait()

    def consume_down(origin, part):
        rows = pl.ds(part * quarter, quarter)
        features = pl.ds(pl.multiple_of(origin * width, width), width)
        block = grads[origin, rows, :]
        total[rows, :] += dot(block, w_down[features, :])
        gw2[features, :] += row_product(block, hidden[rows, :])

    def complete_down(origin):
        features = pl.ds(pl.multiple_of(origin * width, width), width)
        block_of(short, origin, 0, width)[...] = gw2[features, :].astype(jnp.bfloat16)
        write_down(origin).start()

    drain_down = tree_gather(prepare_down, me, grads, down_send, down_recv, consume_down, complete_down)
    part = (total[...] * slope[...]).astype(jnp.bfloat16)
    parts[me] = part

    def write_up(origin):
        return pltpu.make_async_copy(
            block_of(short, origin, 0, channels), block_of(weight_hbm, origin, 0, channels), out_sem.at[1, origin]
        )

    def prepare_up():
        bias_ref[1:2, :] = jnp.sum(parts[me].astype(jnp.float32), axis=0, keepdims=True)
        norm[...] = jnp.zeros_like(norm)
        gw1[...] = jnp.zeros_like(gw1)
        gain_column(gain_ref, column)
        for origin in range(TP):
            write_down(origin).wait()
        for load in loads[1:]:
            load.wait()

    def consume_up(origin, part):
        rows = pl.ds(part * quarter, quarter)
        units = pl.ds(pl.multiple_of(origin * width, width), width)
        within = pl.ds(pl.multiple_of(origin % per_owner * width, width), width)
        block = parts[origin, rows, :]
        norm[:, rows] += dot_last(w_up[:, units], block)
        gw1[origin // per_owner, :, within] += dot(normed[:, rows], block)

    def complete_up(origin):
        within = pl.ds(pl.multiple_of(origin % per_owner * width, width), width)
        owner = origin // per_owner

        def some(k, carry):
            part = pl.ds(pl.multiple_of(k * chunk, chunk), chunk)
            short[owner, part, within] = gw1[owner, part, within].astype(jnp.bfloat16)
            return carry

        lax.fori_loop(0, 5, some, 0)
        write_up(origin).start()

    drain_up = tree_gather(prepare_up, me, parts, up_send, up_recv, consume_up, complete_up)
    store = pltpu.make_async_copy(norm, norm_hbm, load_sem.at[0])
    store.start()

    for i in range(images):
        rows = pl.ds(i * image_rows, image_rows)

        def some(k, carry):
            part = pl.ds(pl.multiple_of(k * chunk, chunk), chunk)
            feature = normed[part, rows].astype(jnp.float32)
            gained = column[part, :] * norm[part, rows]
            return (
                carry[0] + jnp.sum(gained, axis=0, keepdims=True),
                carry[1] + jnp.sum(gained * feature, axis=0, keepdims=True),
            )

        zero = jnp.zeros((1, image_rows), jnp.float32)
        first, second = lax.fori_loop(0, 5, some, (zero, zero))
        stats_y[0, i : i + 1, :] = first
        stats_y[0, images + i : images + i + 1, :] = second

    def stat_copy(half, d):
        buffer = (stats_y, stats_z)[half]
        return pltpu.make_async_remote_copy(
            src_ref=buffer.at[0],
            dst_ref=buffer.at[d],
            send_sem=stat_send.at[half, d - 1],
            recv_sem=stat_recv.at[half, d - 1],
            device_id={"tp": peers(me, (d,))[half]},
            device_id_type=MESH,
        )

    for d in range(1, SIDE):
        stat_copy(0, d).start()
    for d in range(1, SIDE):
        stat_copy(0, d).wait_recv()
    stats_z[0] = stats_y[0] + stats_y[1] + stats_y[2] + stats_y[3]
    for d in range(1, SIDE):
        stat_copy(1, d).start()
    drain_down()
    drain_up()
    store.wait()
    for origin in range(TP):
        write_up(origin).wait()
    for d in range(1, SIDE):
        stat_copy(1, d).wait_recv()
    mean_ref[...] = (stats_z[0] + stats_z[1] + stats_z[2] + stats_z[3]) * (1.0 / full_width)
    for half in range(2):
        for d in range(1, SIDE):
            stat_copy(half, d).wait_send()


def gather(out_grad, pre_act, gain, w_down, w_up_t, normed_t, ctx_count, images, full_width):
    rows, width = out_grad.shape
    channels, units = w_up_t.shape
    features = w_down.shape[0]
    vmem = pl.BlockSpec(memory_space=pltpu.VMEM)
    anywhere = pl.BlockSpec(memory_space=pl.ANY)
    dma = pltpu.SemaphoreType.DMA
    each = units // ctx_count
    return pl.pallas_call(
        functools.partial(gather_kernel, full_width),
        out_shape=(
            jax.ShapeDtypeStruct((channels, rows), jnp.float32),
            jax.ShapeDtypeStruct((ctx_count, channels + width, each), jnp.bfloat16),
            jax.ShapeDtypeStruct((2 * images, rows // images), jnp.float32),
            jax.ShapeDtypeStruct((2, width), jnp.float32),
        ),
        in_specs=[vmem, vmem, vmem, anywhere, anywhere, anywhere],
        out_specs=(anywhere, anywhere, vmem, vmem),
        scratch_shapes=[
            pltpu.VMEM((TP, rows, width), jnp.bfloat16),
            pltpu.VMEM((TP, rows, width), jnp.bfloat16),
            pltpu.VMEM((features, width), jnp.bfloat16),
            pltpu.VMEM((channels, units), jnp.bfloat16),
            pltpu.VMEM((channels, rows), jnp.bfloat16),
            pltpu.VMEM((rows, width), jnp.float32),
            pltpu.VMEM((rows, width), jnp.bfloat16),
            pltpu.VMEM((rows, width), jnp.float32),
            pltpu.VMEM((features, width), jnp.float32),
            pltpu.VMEM((channels, rows), jnp.float32),
            pltpu.VMEM((ctx_count, channels, each), jnp.float32),
            pltpu.VMEM((ctx_count, channels, each), jnp.bfloat16),
            pltpu.VMEM((channels, 1), jnp.float32),
            pltpu.VMEM((SIDE, 2 * images, rows // images), jnp.float32),
            pltpu.VMEM((SIDE, 2 * images, rows // images), jnp.float32),
            dma((3,)),
            dma((2, TP)),
            dma((QUARTERS, TP - 1)),
            dma((QUARTERS, TP - 1)),
            dma((QUARTERS, TP - 1)),
            dma((QUARTERS, TP - 1)),
            dma((2, SIDE - 1)),
            dma((2, SIDE - 1)),
        ],
        compiler_params=pltpu.CompilerParams(
            collective_id=0, has_side_effects=True, vmem_limit_bytes=VMEM_LIMIT
        ),
        cost_estimate=pl.CostEstimate(
            flops=4 * rows * units * (channels + width), bytes_accessed=30 * 2**20, transcendentals=0
        ),
        name="gather",
    )(out_grad, pre_act, gain, w_down, w_up_t, normed_t)


HALVES = 2
LANES = 128


def hand_kernel(
    grad_scale,
    norm_hbm,
    normed_hbm,
    gain_row,
    std_ref,
    owner_ref,
    bias_ref,
    mean_ref,
    sum_ref,
    final,
    own_y, next_y, far_y, prev_y,
    own_z, next_z, far_z, prev_z,
    message,
    norm_ref,
    normed_ref,
    gain_ref,
    product,
    sums,
    load_sem, near_send, near_recv, relay_send, relay_recv, cross_send, cross_recv, own_sem, sum_send, sum_recv,
):
    me = lax.axis_index("tp")
    group = lax.axis_index("ctx")
    ctx_count = sums.shape[0]
    torus = [Torus(half, me) for half in range(HALVES)]
    held = [[own_y, next_y, far_y, prev_y], [own_z, next_z, far_z, prev_z]]
    images, channels, _ = own_y.shape
    image_rows = norm_ref.shape[1] // images
    chunk = channels // 5

    def along_peer(half, d):
        t = torus[half]
        return t.place(t.along + d, t.cross)

    def cross_peer(half, d):
        t = torus[half]
        return t.place(t.along, t.cross + d)

    barrier = pltpu.get_barrier_semaphore()
    for half in range(HALVES):
        for d in range(1, SIDE):
            pl.semaphore_signal(barrier, inc=1, device_id={"tp": along_peer(half, d)}, device_id_type=MESH)
    for d in range(1, ctx_count):
        pl.semaphore_signal(barrier, inc=1, device_id={"ctx": (group + d) % ctx_count}, device_id_type=MESH)

    loads = [
        pltpu.make_async_copy(norm_hbm, norm_ref, load_sem.at[0]),
        pltpu.make_async_copy(normed_hbm, normed_ref, load_sem.at[1]),
    ]
    for load in loads:
        load.start()
    gain_column(gain_row, gain_ref)

    def sum_copy(d):
        return pltpu.make_async_remote_copy(
            src_ref=sums.at[0],
            dst_ref=sums.at[d],
            send_sem=sum_send.at[d - 1],
            recv_sem=sum_recv.at[d - 1],
            device_id={"ctx": (group + d) % ctx_count},
            device_id_type=MESH,
        )

    def near(half, sign, pair):
        piece = pl.ds(pair * (images // 2), images // 2)
        return pltpu.make_async_remote_copy(
            src_ref=held[half][0].at[piece],
            dst_ref=held[half][3 if sign == 1 else 1].at[piece],
            send_sem=near_send.at[half, sign // 2, pair],
            recv_sem=near_recv.at[half, sign // 2, pair],
            device_id={"tp": along_peer(half, sign)},
            device_id_type=MESH,
        )

    def relay(half, sign):
        pair = sign // 2
        piece = pl.ds(pair * (images // 2), images // 2)
        return pltpu.make_async_remote_copy(
            src_ref=held[half][3 if sign == 1 else 1].at[piece],
            dst_ref=held[half][2].at[piece],
            send_sem=relay_send.at[half, pair],
            recv_sem=relay_recv.at[half, pair],
            device_id={"tp": along_peer(half, sign)},
            device_id_type=MESH,
        )

    def across(half, target, d):
        t = torus[half]
        slot = (t.along + d) % SIDE
        source = t.cross * SIDE + slot if half == 0 else slot * SIDE + t.cross
        spot = final.at[half, pl.ds(pl.multiple_of(source * channels, 16), channels)]
        if target == 0:
            return pltpu.make_async_copy(message.at[half, 0, d], spot, own_sem.at[half, d])
        return pltpu.make_async_remote_copy(
            src_ref=message.at[half, target, d],
            dst_ref=spot,
            send_sem=cross_send.at[half, target - 1, d],
            recv_sem=cross_recv.at[half, target - 1, d],
            device_id={"tp": cross_peer(half, target)},
            device_id_type=MESH,
        )

    for load in loads:
        load.wait()
    for i in range(images):
        rows = pl.ds(i * image_rows, image_rows)
        mean_first, mean_second = mean_ref[i : i + 1, :], mean_ref[images + i : images + i + 1, :]
        inverse = std_ref[:, rows]

        def visual(k, carry):
            part = pl.ds(pl.multiple_of(k * chunk, chunk), chunk)
            value = gain_ref[part, :] * norm_ref[part, rows]
            feature = normed_ref[part, rows].astype(jnp.float32)
            seen = (inverse * (value - mean_first - feature * mean_second)).astype(jnp.bfloat16)
            own_y[i, part, :] = seen[:, :LANES]
            own_z[i, part, :] = seen[:, LANES:]
            return carry

        lax.fori_loop(0, 5, visual, 0)
        if i == 1:
            pl.semaphore_wait(barrier, HALVES * (SIDE - 1) + ctx_count - 1)
        if i % 2:
            for half in range(HALVES):
                near(half, 1, i // 2).start()
                near(half, 3, i // 2).start()
    owners = [owner_ref[0, i] for i in range(images)]
    slots = []
    for i in range(images):
        earlier = jnp.int32(0)
        for j in range(i):
            earlier += (owners[j] == owners[i]).astype(jnp.int32)
        slots.append(owners[i] + earlier)

    def choice(place):
        source, present = jnp.int32(0), jnp.int32(0)
        for i in range(images):
            match = (slots[i] == place).astype(jnp.int32)
            source += i * match
            present += match
        return source, present

    chosen = [[choice(cross_peer(half, target)) for target in range(SIDE)] for half in range(HALVES)]

    def forward(half, d):
        block = held[half][d]
        for target in (2, 1, 3, 0):
            source, present = chosen[half][target]
            spot = message.at[half, target, d]

            def pick(k, carry):
                part = pl.ds(pl.multiple_of(k * chunk, chunk), chunk)
                value = block[source, part, :]
                spot[part, :] = jnp.where(present > 0, value, jnp.zeros_like(value))
                return carry

            lax.fori_loop(0, 5, pick, 0)
            across(half, target, d).start()

    for half in range(HALVES):
        forward(half, 0)
    for half in range(HALVES):
        near(half, 1, 0).wait_recv()
        relay(half, 1).start()
    for half in range(HALVES):
        near(half, 3, 1).wait_recv()
        relay(half, 3).start()
    for half in range(HALVES):
        near(half, 1, 1).wait_recv()
        forward(half, 3)
        near(half, 3, 0).wait_recv()
        forward(half, 1)

    ones = jnp.ones((8, image_rows), jnp.float32)
    columns = [jnp.zeros((8, channels), jnp.float32)] * 2
    for i in range(images):
        rows = pl.ds(i * image_rows, image_rows)
        product[...] = norm_ref[:, rows] * normed_ref[:, rows].astype(jnp.float32)
        columns = [
            total
            + lax.dot_general(
                ones,
                right,
                (((1,), (1,)), ((), ())),
                precision=lax.Precision.HIGHEST,
                preferred_element_type=jnp.float32,
            )
            for total, right in zip(columns, (product[...], norm_ref[:, rows]))
        ]
    sums[0, 0:1, 0:channels] = columns[0][0:1]
    sums[0, 1:2, 0:channels] = columns[1][0:1]
    sums[0, 2:4, 0 : bias_ref.shape[1]] = bias_ref[...]
    for d in range(1, ctx_count):
        sum_copy(d).start()

    for half in range(HALVES):
        relay(half, 1).wait_recv()
        relay(half, 3).wait_recv()
        forward(half, 2)

    for d in range(1, ctx_count):
        sum_copy(d).wait_recv()
    whole = sums[0]
    for d in range(1, ctx_count):
        whole = whole + sums[d]
    sum_ref[...] = whole * grad_scale

    for half in range(HALVES):
        for d in range(SIDE):
            for target in range(1, SIDE):
                across(half, target, d).wait_recv()
            across(half, 0, d).wait()
    for half in range(HALVES):
        for sign in (1, 3):
            for pair in range(2):
                near(half, sign, pair).wait_send()
            relay(half, sign).wait_send()
        for d in range(1, SIDE):
            for e in range(SIDE):
                across(half, d, e).wait_send()
    for d in range(1, ctx_count):
        sum_copy(d).wait_send()


def hand_over(norm_t, normed_t, gain, inverse_std, owner_map, bias, means, grad_scale, ctx_count):
    channels, rows = norm_t.shape
    images = owner_map.shape[1]
    image_rows = rows // images
    vmem = pl.BlockSpec(memory_space=pltpu.VMEM)
    block = pltpu.VMEM((images, channels, LANES), jnp.bfloat16)
    dma = pltpu.SemaphoreType.DMA
    return pl.pallas_call(
        functools.partial(hand_kernel, grad_scale),
        out_shape=(
            jax.ShapeDtypeStruct((8, 1024), jnp.float32),
            jax.ShapeDtypeStruct((HALVES, TP * channels, LANES), jnp.bfloat16),
        ),
        in_specs=[
            pl.BlockSpec(memory_space=pl.ANY),
            pl.BlockSpec(memory_space=pl.ANY),
            vmem,
            vmem,
            pl.BlockSpec(memory_space=pltpu.SMEM),
            vmem,
            vmem,
        ],
        out_specs=(vmem, pl.BlockSpec(memory_space=pl.ANY)),
        scratch_shapes=[block] * 8
        + [
            pltpu.VMEM((HALVES, SIDE, SIDE, channels, LANES), jnp.bfloat16),
            pltpu.VMEM((channels, rows), jnp.float32),
            pltpu.VMEM((channels, rows), jnp.bfloat16),
            pltpu.VMEM((channels, 1), jnp.float32),
            pltpu.VMEM((channels, image_rows), jnp.float32),
            pltpu.VMEM((ctx_count, 8, 1024), jnp.float32),
            dma((2,)),
            dma((HALVES, 2, 2)),
            dma((HALVES, 2, 2)),
            dma((HALVES, 2)),
            dma((HALVES, 2)),
            dma((HALVES, SIDE - 1, SIDE)),
            dma((HALVES, SIDE - 1, SIDE)),
            dma((HALVES, SIDE)),
            dma((ctx_count - 1,)),
            dma((ctx_count - 1,)),
        ],
        compiler_params=pltpu.CompilerParams(
            collective_id=1, has_side_effects=True, vmem_limit_bytes=VMEM_LIMIT
        ),
        cost_estimate=pl.CostEstimate(
            flops=20 * rows * channels, bytes_accessed=200 * 2**20, transcendentals=0
        ),
        name="hand_over",
    )(norm_t, normed_t, gain, inverse_std, owner_map, bias, means)


STEPS = 4


def finish_kernel(
    grad_scale, final_hbm, weight_hbm, sum_ref, out_hbm, grad_w2_hbm, grad_w1_hbm, ln_ref, up_ref, down_ref,
    final, out, weight, grad_w2, grad_w1, in_sem, out_sem,
):
    wide = final.shape[1] // STEPS
    small_in = pltpu.make_async_copy(weight_hbm, weight, in_sem.at[STEPS])
    small_out = [
        pltpu.make_async_copy(grad_w2, grad_w2_hbm, out_sem.at[STEPS]),
        pltpu.make_async_copy(grad_w1, grad_w1_hbm, out_sem.at[STEPS + 1]),
    ]

    def load(k):
        part = pl.ds(pl.multiple_of(k * wide, wide), wide)
        return pltpu.make_async_copy(final_hbm.at[:, part], final.at[:, part], in_sem.at[k])

    def store(k):
        part = pl.ds(pl.multiple_of(k * wide, wide), wide)
        return pltpu.make_async_copy(out.at[:, part], out_hbm.at[:, part], out_sem.at[k])

    load(0).start()
    load(1).start()
    small_in.start()
    for k in range(2, STEPS):
        load(k).start()
    lanes = out.shape[0]
    row = lax.broadcasted_iota(jnp.int32, (lanes, lanes), 0)
    column = lax.broadcasted_iota(jnp.int32, (lanes, lanes), 1)
    identity = jnp.where(row == column, 1.0, 0.0).astype(jnp.bfloat16)

    def turn(k, carry):
        part = pl.ds(pl.multiple_of(k * wide, wide), wide)
        load(k).wait()
        block = jnp.concatenate([final[0, part, :], final[1, part, :]], axis=1)
        out[:, part] = dot_last(identity, block).astype(jnp.bfloat16)
        store(k).start()
        return carry

    lax.fori_loop(0, STEPS // 2, turn, 0)
    small_in.wait()
    channels = grad_w1.shape[0]
    tall, width = grad_w2.shape
    for i in range(tall * width // ((weight.shape[0] - channels) * width)):
        part = weight.shape[0] - channels
        grad_w2[i * part : (i + 1) * part, :] = (
            weight[channels:, i * width : (i + 1) * width].astype(jnp.float32) * grad_scale
        )
    small_out[0].start()
    grad_w1[...] = weight[:channels, :].astype(jnp.float32) * grad_scale
    small_out[1].start()
    lax.fori_loop(STEPS // 2, STEPS, turn, 0)
    ln_ref[...] = sum_ref[0:2, 0 : ln_ref.shape[1]]
    down_ref[...] = sum_ref[2:3, 0 : down_ref.shape[1]]
    up_ref[...] = sum_ref[3:4, 0 : up_ref.shape[1]]
    for copy in small_out:
        copy.wait()
    for k in range(STEPS):
        store(k).wait()


def finish(final, weight, sums, width, grad_scale):
    each = weight.shape[1]
    channels = weight.shape[0] - width
    vmem = pl.BlockSpec(memory_space=pltpu.VMEM)
    anywhere = pl.BlockSpec(memory_space=pl.ANY)
    return pl.pallas_call(
        functools.partial(finish_kernel, grad_scale),
        out_shape=(
            jax.ShapeDtypeStruct((HALVES * LANES, final.shape[1]), jnp.bfloat16),
            jax.ShapeDtypeStruct((each, width), jnp.float32),
            jax.ShapeDtypeStruct((channels, each), jnp.float32),
            jax.ShapeDtypeStruct((2, channels), jnp.float32),
            jax.ShapeDtypeStruct((1, width), jnp.float32),
            jax.ShapeDtypeStruct((1, width), jnp.float32),
        ),
        in_specs=[anywhere, anywhere, vmem],
        out_specs=(anywhere, anywhere, anywhere, vmem, vmem, vmem),
        scratch_shapes=[
            pltpu.VMEM(final.shape, jnp.bfloat16),
            pltpu.VMEM((HALVES * LANES, final.shape[1]), jnp.bfloat16),
            pltpu.VMEM(weight.shape, jnp.bfloat16),
            pltpu.VMEM((each, width), jnp.float32),
            pltpu.VMEM((channels, each), jnp.float32),
            pltpu.SemaphoreType.DMA((STEPS + 1,)),
            pltpu.SemaphoreType.DMA((STEPS + 2,)),
        ],
        compiler_params=pltpu.CompilerParams(vmem_limit_bytes=VMEM_LIMIT),
        name="finish",
    )(final, weight, sums)


def per_device(out_grad, pre_act, normed, inverse_std, w_up, w_down, ln_gain, owner_map):
    ctx_count = lax.axis_size("ctx")
    tp_count = lax.axis_size("tp")
    row_count = out_grad.shape[0]
    grad_scale = float(row_count * ctx_count) ** (-0.5)
    gain = ln_gain
    normed_t = normed.T
    norm_t, weight, means, bias = gather(
        out_grad,
        pre_act,
        gain,
        w_down,
        w_up.T,
        normed_t,
        ctx_count,
        owner_map.shape[1],
        float(normed.shape[1] * tp_count),
    )
    weight = lax.psum_scatter(weight, "ctx", scatter_dimension=0, tiled=True)
    sums, final = hand_over(
        norm_t,
        normed_t,
        gain,
        inverse_std[None, :],
        owner_map,
        bias,
        means,
        grad_scale,
        ctx_count,
    )
    vit_grad, grad_w2, grad_w1_t, ln_grads, bias_up, bias_down = finish(
        final, weight[0], sums, bias.shape[1], grad_scale
    )
    return (grad_w2, grad_w1_t.T, bias_up[0], bias_down[0], ln_grads, vit_grad)


def solution(mesh):
    return jax.shard_map(
        per_device,
        mesh=mesh,
        in_specs=(
            P("ctx", "tp"),
            P("ctx", "tp"),
            P("ctx", "tp"),
            P("ctx"),
            P(None, "tp"),
            P(None, "tp"),
            P("tp"),
            P("ctx", None),
        ),
        out_specs=(
            P("ctx", "tp"),
            P("ctx", "tp"),
            P("tp"),
            P("tp"),
            P(None, "tp"),
            P(("ctx", "tp"), None),
        ),
        check_vma=False,
    )
```

```python
import functools
import math

import jax
import jax.numpy as jnp
from jax import lax
from jax.experimental import pallas as pl
from jax.experimental.pallas import tpu as pltpu
from jax.sharding import PartitionSpec as P

MESH = pl.DeviceIdType.MESH
SIDE = 4
TP = SIDE * SIDE
VMEM_LIMIT = 60 * 2**20


def gelu_parts(linear):
    normal_cdf = 0.5 * (1.0 + lax.erf(linear * 2.0 ** (-0.5)))
    density = jnp.exp(-0.5 * linear * linear) * (2.0 * math.pi) ** (-0.5)
    return (linear * normal_cdf, normal_cdf + linear * density)


def dot(left, right):
    return lax.dot_general(
        left, right, (((1,), (0,)), ((), ())), preferred_element_type=jnp.float32
    )


def row_product(left, right):
    return lax.dot_general(
        left, right, (((0,), (0,)), ((), ())), preferred_element_type=jnp.float32
    )


def dot_last(left, right):
    return lax.dot_general(
        left, right, (((1,), (1,)), ((), ())), preferred_element_type=jnp.float32
    )


def greet(half_targets):
    barrier = pltpu.get_barrier_semaphore()
    for target in half_targets:
        pl.semaphore_signal(barrier, inc=1, device_id={"tp": target}, device_id_type=MESH)


def met(count):
    pl.semaphore_wait(pltpu.get_barrier_semaphore(), count)


def peers(me, steps):
    torus = [Torus(half, me) for half in range(2)]
    return [t.place(t.along + d, t.cross) for t in torus for d in steps]


class Torus:
    def __init__(self, half, me):
        z, y = me // SIDE, me % SIDE
        self.half = half
        self.along, self.cross = (y, z) if half == 0 else (z, y)

    def place(self, along, cross):
        along, cross = along % SIDE, cross % SIDE
        return cross * SIDE + along if self.half == 0 else along * SIDE + cross


QUARTERS = 4
ARRIVALS = (
    (3, 0), (1, 0), (0, 3), (0, 1), (2, 0), (3, 3), (3, 1), (1, 3),
    (1, 1), (0, 2), (2, 3), (2, 1), (3, 2), (1, 2), (2, 2),
)


def full_at(y, z):
    turns = ((y, z), (-y % SIDE, -z % SIDE), (z, y), (-z % SIDE, -y % SIDE))
    return max(ARRIVALS.index(turn) for turn in turns if turn != (0, 0))


FULL_AT = {(y, z): full_at(y, z) for y in range(SIDE) for z in range(SIDE) if (y, z) != (0, 0)}
FULL_AT[(0, 0)] = min(FULL_AT.values())


def gain_column(gain_ref, column_ref):
    channels = gain_ref.shape[0]
    rows = channels // 5
    at = lax.broadcasted_iota(jnp.int32, (rows, channels), 1) - lax.broadcasted_iota(
        jnp.int32, (rows, channels), 0
    )

    def some(k, carry):
        picked = jnp.where(at == k * rows, jnp.broadcast_to(gain_ref[...], (rows, channels)), 0.0)
        column_ref[pl.ds(pl.multiple_of(k * rows, rows), rows), :] = jnp.sum(picked, axis=1, keepdims=True)
        return carry

    lax.fori_loop(0, 5, some, 0)


def numbered(values, index):
    out = jnp.int32(values[0])
    for i, value in enumerate(values[1:], 1):
        out = jnp.where(index == i, jnp.int32(value), out)
    return out


def tree_gather(prepare, me, full_ref, send_sem, recv_sem, consume, complete):
    rows = full_ref.shape[1] // QUARTERS
    torus = [Torus(half, me) for half in range(2)]

    def origin(quarter, along, cross):
        t, sign = torus[quarter // 2], 1 - quarter % 2 * 2
        return t.place(t.along + sign * along + SIDE, t.cross + sign * cross + SIDE)

    def copy(quarter, block, number, target):
        spot = full_ref.at[origin(quarter, *block), pl.ds(quarter * rows, rows)]
        return pltpu.make_async_remote_copy(
            src_ref=spot,
            dst_ref=spot,
            send_sem=send_sem.at[quarter, number],
            recv_sem=recv_sem.at[quarter, number],
            device_id={"tp": origin(quarter, *target)},
            device_id_type=MESH,
        )

    def send(block, seen):
        target = ((block[0] - seen[0]) % SIDE, (block[1] - seen[1]) % SIDE)
        for quarter in range(QUARTERS):
            copy(quarter, block, ARRIVALS.index(seen), target).start()

    send((0, 0), (3, 0))
    send((0, 0), (1, 0))
    send((0, 0), (0, 3))
    send((0, 0), (0, 1))
    prepare()
    for quarter in range(QUARTERS):
        consume(me, quarter)

    def arrive(k, carry):
        along = numbered([block[0] for block in ARRIVALS], k)
        cross = numbered([block[1] for block in ARRIVALS], k)
        for quarter in range(QUARTERS):
            copy(quarter, (along, cross), k, (1, 0)).wait_recv()
        for number, block in enumerate(ARRIVALS):
            if block[1] not in (0, 3):
                continue

            @pl.when(k == number)
            def _():
                if block == (3, 0):
                    send(block, (2, 0))
                if block[1] == 0:
                    send(block, (block[0], 3))
                    send(block, (block[0], 1))
                else:
                    send(block, (block[0], 2))

        for quarter in range(QUARTERS):
            consume(origin(quarter, along, cross), quarter)
        for number in sorted(set(FULL_AT.values())):

            @pl.when(k == number)
            def _():
                for block, at in FULL_AT.items():
                    if at == number:
                        complete(torus[0].place(torus[0].along + block[0], torus[0].cross + block[1]))

        return carry

    lax.fori_loop(0, TP - 1, arrive, 0)

    def drain(k, carry):
        for quarter in range(QUARTERS):
            copy(quarter, (0, 0), k, (1, 0)).wait_send()
        return carry

    return lambda: lax.fori_loop(0, TP - 1, drain, 0)


def gather_kernel(
    full_width, grad_ref, pre_ref, gain_ref, w_down_hbm, w_up_hbm, normed_hbm, norm_hbm, weight_hbm, mean_ref, bias_ref,
    grads, parts, w_down, w_up, normed, total, hidden, slope, gw2, norm, gw1, short, column, stats_y, stats_z,
    load_sem, out_sem, down_send, down_recv, up_send, up_recv, stat_send, stat_recv,
):
    me = lax.axis_index("tp")
    greet(peers(me, (1, 2, 3)))
    loads = [
        pltpu.make_async_copy(source, target, load_sem.at[i])
        for i, (source, target) in enumerate(((w_down_hbm, w_down), (w_up_hbm, w_up), (normed_hbm, normed)))
    ]
    for load in loads:
        load.start()
    grads[me] = grad_ref[...]
    met(6)
    rows_all, width = grad_ref.shape
    quarter = rows_all // QUARTERS
    per_owner = gw1.shape[2] // width
    channels = norm.shape[0]
    chunk = channels // 5
    images = mean_ref.shape[0] // 2
    image_rows = rows_all // images

    def block_of(ref, origin, first, count):
        within = pl.ds(pl.multiple_of(origin % per_owner * width, width), width)
        return ref.at[origin // per_owner, pl.ds(first, count), within]

    def write_down(origin):
        return pltpu.make_async_copy(
            block_of(short, origin, 0, width), block_of(weight_hbm, origin, channels, width), out_sem.at[0, origin]
        )

    def prepare_down():
        def rows_of(i, carry):
            rows = pl.ds(pl.multiple_of(i * 64, 64), 64)
            value, steep = gelu_parts(pre_ref[rows, :].astype(jnp.float32))
            hidden[rows, :] = value.astype(jnp.bfloat16)
            slope[rows, :] = steep
            return carry

        lax.fori_loop(0, rows_all // 64, rows_of, 0)
        bias_ref[0:1, :] = jnp.sum(grad_ref[...].astype(jnp.float32), axis=0, keepdims=True)
        total[...] = jnp.zeros_like(total)
        gw2[...] = jnp.zeros_like(gw2)
        loads[0].wait()

    def consume_down(origin, part):
        rows = pl.ds(part * quarter, quarter)
        features = pl.ds(pl.multiple_of(origin * width, width), width)
        block = grads[origin, rows, :]
        total[rows, :] += dot(block, w_down[features, :])
        gw2[features, :] += row_product(block, hidden[rows, :])

    def complete_down(origin):
        features = pl.ds(pl.multiple_of(origin * width, width), width)
        block_of(short, origin, 0, width)[...] = gw2[features, :].astype(jnp.bfloat16)
        write_down(origin).start()

    drain_down = tree_gather(prepare_down, me, grads, down_send, down_recv, consume_down, complete_down)
    part = (total[...] * slope[...]).astype(jnp.bfloat16)
    parts[me] = part

    def write_up(origin):
        return pltpu.make_async_copy(
            block_of(short, origin, 0, channels), block_of(weight_hbm, origin, 0, channels), out_sem.at[1, origin]
        )

    def prepare_up():
        bias_ref[1:2, :] = jnp.sum(parts[me].astype(jnp.float32), axis=0, keepdims=True)
        norm[...] = jnp.zeros_like(norm)
        gw1[...] = jnp.zeros_like(gw1)
        gain_column(gain_ref, column)
        for origin in range(TP):
            write_down(origin).wait()
        for load in loads[1:]:
            load.wait()

    def consume_up(origin, part):
        rows = pl.ds(part * quarter, quarter)
        units = pl.ds(pl.multiple_of(origin * width, width), width)
        within = pl.ds(pl.multiple_of(origin % per_owner * width, width), width)
        block = parts[origin, rows, :]
        norm[:, rows] += dot_last(w_up[:, units], block)
        gw1[origin // per_owner, :, within] += dot(normed[:, rows], block)

    def complete_up(origin):
        within = pl.ds(pl.multiple_of(origin % per_owner * width, width), width)
        owner = origin // per_owner

        def some(k, carry):
            part = pl.ds(pl.multiple_of(k * chunk, chunk), chunk)
            short[owner, part, within] = gw1[owner, part, within].astype(jnp.bfloat16)
            return carry

        lax.fori_loop(0, 5, some, 0)
        write_up(origin).start()

    drain_up = tree_gather(prepare_up, me, parts, up_send, up_recv, consume_up, complete_up)
    store = pltpu.make_async_copy(norm, norm_hbm, load_sem.at[0])
    store.start()

    for i in range(images):
        rows = pl.ds(i * image_rows, image_rows)

        def some(k, carry):
            part = pl.ds(pl.multiple_of(k * chunk, chunk), chunk)
            feature = normed[part, rows].astype(jnp.float32)
            gained = column[part, :] * norm[part, rows]
            return (
                carry[0] + jnp.sum(gained, axis=0, keepdims=True),
                carry[1] + jnp.sum(gained * feature, axis=0, keepdims=True),
            )

        zero = jnp.zeros((1, image_rows), jnp.float32)
        first, second = lax.fori_loop(0, 5, some, (zero, zero))
        stats_y[0, i : i + 1, :] = first
        stats_y[0, images + i : images + i + 1, :] = second

    def stat_copy(half, d):
        buffer = (stats_y, stats_z)[half]
        return pltpu.make_async_remote_copy(
            src_ref=buffer.at[0],
            dst_ref=buffer.at[d],
            send_sem=stat_send.at[half, d - 1],
            recv_sem=stat_recv.at[half, d - 1],
            device_id={"tp": peers(me, (d,))[half]},
            device_id_type=MESH,
        )

    for d in range(1, SIDE):
        stat_copy(0, d).start()
    for d in range(1, SIDE):
        stat_copy(0, d).wait_recv()
    stats_z[0] = stats_y[0] + stats_y[1] + stats_y[2] + stats_y[3]
    for d in range(1, SIDE):
        stat_copy(1, d).start()
    drain_down()
    drain_up()
    store.wait()
    for origin in range(TP):
        write_up(origin).wait()
    for d in range(1, SIDE):
        stat_copy(1, d).wait_recv()
    mean_ref[...] = (stats_z[0] + stats_z[1] + stats_z[2] + stats_z[3]) * (1.0 / full_width)
    for half in range(2):
        for d in range(1, SIDE):
            stat_copy(half, d).wait_send()


def gather(out_grad, pre_act, gain, w_down, w_up_t, normed_t, ctx_count, images, full_width):
    rows, width = out_grad.shape
    channels, units = w_up_t.shape
    features = w_down.shape[0]
    vmem = pl.BlockSpec(memory_space=pltpu.VMEM)
    anywhere = pl.BlockSpec(memory_space=pl.ANY)
    dma = pltpu.SemaphoreType.DMA
    each = units // ctx_count
    return pl.pallas_call(
        functools.partial(gather_kernel, full_width),
        out_shape=(
            jax.ShapeDtypeStruct((channels, rows), jnp.float32),
            jax.ShapeDtypeStruct((ctx_count, channels + width, each), jnp.bfloat16),
            jax.ShapeDtypeStruct((2 * images, rows // images), jnp.float32),
            jax.ShapeDtypeStruct((2, width), jnp.float32),
        ),
        in_specs=[vmem, vmem, vmem, anywhere, anywhere, anywhere],
        out_specs=(anywhere, anywhere, vmem, vmem),
        scratch_shapes=[
            pltpu.VMEM((TP, rows, width), jnp.bfloat16),
            pltpu.VMEM((TP, rows, width), jnp.bfloat16),
            pltpu.VMEM((features, width), jnp.bfloat16),
            pltpu.VMEM((channels, units), jnp.bfloat16),
            pltpu.VMEM((channels, rows), jnp.bfloat16),
            pltpu.VMEM((rows, width), jnp.float32),
            pltpu.VMEM((rows, width), jnp.bfloat16),
            pltpu.VMEM((rows, width), jnp.float32),
            pltpu.VMEM((features, width), jnp.float32),
            pltpu.VMEM((channels, rows), jnp.float32),
            pltpu.VMEM((ctx_count, channels, each), jnp.float32),
            pltpu.VMEM((ctx_count, channels, each), jnp.bfloat16),
            pltpu.VMEM((channels, 1), jnp.float32),
            pltpu.VMEM((SIDE, 2 * images, rows // images), jnp.float32),
            pltpu.VMEM((SIDE, 2 * images, rows // images), jnp.float32),
            dma((3,)),
            dma((2, TP)),
            dma((QUARTERS, TP - 1)),
            dma((QUARTERS, TP - 1)),
            dma((QUARTERS, TP - 1)),
            dma((QUARTERS, TP - 1)),
            dma((2, SIDE - 1)),
            dma((2, SIDE - 1)),
        ],
        compiler_params=pltpu.CompilerParams(
            collective_id=0, has_side_effects=True, vmem_limit_bytes=VMEM_LIMIT
        ),
        cost_estimate=pl.CostEstimate(
            flops=4 * rows * units * (channels + width), bytes_accessed=30 * 2**20, transcendentals=0
        ),
        name="gather",
    )(out_grad, pre_act, gain, w_down, w_up_t, normed_t)


HALVES = 2
LANES = 128


def hand_kernel(
    grad_scale,
    norm_hbm,
    normed_hbm,
    gain_row,
    std_ref,
    owner_ref,
    bias_ref,
    mean_ref,
    sum_ref,
    final,
    own_y, next_y, far_y, prev_y,
    own_z, next_z, far_z, prev_z,
    message,
    norm_ref,
    normed_ref,
    gain_ref,
    product,
    sums,
    load_sem, near_send, near_recv, relay_send, relay_recv, cross_send, cross_recv, own_sem, sum_send, sum_recv,
):
    me = lax.axis_index("tp")
    group = lax.axis_index("ctx")
    ctx_count = sums.shape[0]
    torus = [Torus(half, me) for half in range(HALVES)]
    held = [[own_y, next_y, far_y, prev_y], [own_z, next_z, far_z, prev_z]]
    images, channels, _ = own_y.shape
    image_rows = norm_ref.shape[1] // images
    chunk = channels // 5

    def along_peer(half, d):
        t = torus[half]
        return t.place(t.along + d, t.cross)

    def cross_peer(half, d):
        t = torus[half]
        return t.place(t.along, t.cross + d)

    barrier = pltpu.get_barrier_semaphore()
    for half in range(HALVES):
        for d in range(1, SIDE):
            pl.semaphore_signal(barrier, inc=1, device_id={"tp": along_peer(half, d)}, device_id_type=MESH)
    for d in range(1, ctx_count):
        pl.semaphore_signal(barrier, inc=1, device_id={"ctx": (group + d) % ctx_count}, device_id_type=MESH)

    loads = [
        pltpu.make_async_copy(norm_hbm, norm_ref, load_sem.at[0]),
        pltpu.make_async_copy(normed_hbm, normed_ref, load_sem.at[1]),
    ]
    for load in loads:
        load.start()
    gain_column(gain_row, gain_ref)

    def sum_copy(d):
        return pltpu.make_async_remote_copy(
            src_ref=sums.at[0],
            dst_ref=sums.at[d],
            send_sem=sum_send.at[d - 1],
            recv_sem=sum_recv.at[d - 1],
            device_id={"ctx": (group + d) % ctx_count},
            device_id_type=MESH,
        )

    def near(half, sign, pair):
        piece = pl.ds(pair * (images // 2), images // 2)
        return pltpu.make_async_remote_copy(
            src_ref=held[half][0].at[piece],
            dst_ref=held[half][3 if sign == 1 else 1].at[piece],
            send_sem=near_send.at[half, sign // 2, pair],
            recv_sem=near_recv.at[half, sign // 2, pair],
            device_id={"tp": along_peer(half, sign)},
            device_id_type=MESH,
        )

    def relay(half, sign):
        pair = sign // 2
        piece = pl.ds(pair * (images // 2), images // 2)
        return pltpu.make_async_remote_copy(
            src_ref=held[half][3 if sign == 1 else 1].at[piece],
            dst_ref=held[half][2].at[piece],
            send_sem=relay_send.at[half, pair],
            recv_sem=relay_recv.at[half, pair],
            device_id={"tp": along_peer(half, sign)},
            device_id_type=MESH,
        )

    def across(half, target, d):
        t = torus[half]
        slot = (t.along + d) % SIDE
        source = t.cross * SIDE + slot if half == 0 else slot * SIDE + t.cross
        spot = final.at[half, pl.ds(pl.multiple_of(source * channels, 16), channels)]
        if target == 0:
            return pltpu.make_async_copy(message.at[half, 0, d], spot, own_sem.at[half, d])
        return pltpu.make_async_remote_copy(
            src_ref=message.at[half, target, d],
            dst_ref=spot,
            send_sem=cross_send.at[half, target - 1, d],
            recv_sem=cross_recv.at[half, target - 1, d],
            device_id={"tp": cross_peer(half, target)},
            device_id_type=MESH,
        )

    for load in loads:
        load.wait()
    for i in range(images):
        rows = pl.ds(i * image_rows, image_rows)
        mean_first, mean_second = mean_ref[i : i + 1, :], mean_ref[images + i : images + i + 1, :]
        inverse = std_ref[:, rows]

        def visual(k, carry):
            part = pl.ds(pl.multiple_of(k * chunk, chunk), chunk)
            value = gain_ref[part, :] * norm_ref[part, rows]
            feature = normed_ref[part, rows].astype(jnp.float32)
            seen = (inverse * (value - mean_first - feature * mean_second)).astype(jnp.bfloat16)
            own_y[i, part, :] = seen[:, :LANES]
            own_z[i, part, :] = seen[:, LANES:]
            return carry

        lax.fori_loop(0, 5, visual, 0)
        if i == 1:
            pl.semaphore_wait(barrier, HALVES * (SIDE - 1) + ctx_count - 1)
        if i % 2:
            for half in range(HALVES):
                near(half, 1, i // 2).start()
                near(half, 3, i // 2).start()
    owners = [owner_ref[0, i] for i in range(images)]
    slots = []
    for i in range(images):
        earlier = jnp.int32(0)
        for j in range(i):
            earlier += (owners[j] == owners[i]).astype(jnp.int32)
        slots.append(owners[i] + earlier)

    def choice(place):
        source, present = jnp.int32(0), jnp.int32(0)
        for i in range(images):
            match = (slots[i] == place).astype(jnp.int32)
            source += i * match
            present += match
        return source, present

    chosen = [[choice(cross_peer(half, target)) for target in range(SIDE)] for half in range(HALVES)]

    def forward(half, d):
        block = held[half][d]
        for target in (2, 1, 3, 0):
            source, present = chosen[half][target]
            spot = message.at[half, target, d]

            def pick(k, carry):
                part = pl.ds(pl.multiple_of(k * chunk, chunk), chunk)
                value = block[source, part, :]
                spot[part, :] = jnp.where(present > 0, value, jnp.zeros_like(value))
                return carry

            lax.fori_loop(0, 5, pick, 0)
            across(half, target, d).start()

    for half in range(HALVES):
        forward(half, 0)
    for half in range(HALVES):
        near(half, 1, 0).wait_recv()
        relay(half, 1).start()
    for half in range(HALVES):
        near(half, 3, 1).wait_recv()
        relay(half, 3).start()
    for half in range(HALVES):
        near(half, 1, 1).wait_recv()
        forward(half, 3)
        near(half, 3, 0).wait_recv()
        forward(half, 1)

    for half in range(HALVES):
        relay(half, 1).wait_recv()
        relay(half, 3).wait_recv()
        forward(half, 2)

    ones = jnp.ones((8, image_rows), jnp.float32)
    columns = [jnp.zeros((8, channels), jnp.float32)] * 2
    for i in range(images):
        rows = pl.ds(i * image_rows, image_rows)
        product[...] = norm_ref[:, rows] * normed_ref[:, rows].astype(jnp.float32)
        columns = [
            total
            + lax.dot_general(
                ones,
                right,
                (((1,), (1,)), ((), ())),
                precision=lax.Precision.HIGHEST,
                preferred_element_type=jnp.float32,
            )
            for total, right in zip(columns, (product[...], norm_ref[:, rows]))
        ]
    sums[0, 0:1, 0:channels] = columns[0][0:1]
    sums[0, 1:2, 0:channels] = columns[1][0:1]
    sums[0, 2:4, 0 : bias_ref.shape[1]] = bias_ref[...]
    for d in range(1, ctx_count):
        sum_copy(d).start()

    for d in range(1, ctx_count):
        sum_copy(d).wait_recv()
    whole = sums[0]
    for d in range(1, ctx_count):
        whole = whole + sums[d]
    sum_ref[...] = whole * grad_scale

    for half in range(HALVES):
        for d in range(SIDE):
            for target in range(1, SIDE):
                across(half, target, d).wait_recv()
            across(half, 0, d).wait()
    for half in range(HALVES):
        for sign in (1, 3):
            for pair in range(2):
                near(half, sign, pair).wait_send()
            relay(half, sign).wait_send()
        for d in range(1, SIDE):
            for e in range(SIDE):
                across(half, d, e).wait_send()
    for d in range(1, ctx_count):
        sum_copy(d).wait_send()


def hand_over(norm_t, normed_t, gain, inverse_std, owner_map, bias, means, grad_scale, ctx_count):
    channels, rows = norm_t.shape
    images = owner_map.shape[1]
    image_rows = rows // images
    vmem = pl.BlockSpec(memory_space=pltpu.VMEM)
    block = pltpu.VMEM((images, channels, LANES), jnp.bfloat16)
    dma = pltpu.SemaphoreType.DMA
    return pl.pallas_call(
        functools.partial(hand_kernel, grad_scale),
        out_shape=(
            jax.ShapeDtypeStruct((8, 1024), jnp.float32),
            jax.ShapeDtypeStruct((HALVES, TP * channels, LANES), jnp.bfloat16),
        ),
        in_specs=[
            pl.BlockSpec(memory_space=pl.ANY),
            pl.BlockSpec(memory_space=pl.ANY),
            vmem,
            vmem,
            pl.BlockSpec(memory_space=pltpu.SMEM),
            vmem,
            vmem,
        ],
        out_specs=(vmem, pl.BlockSpec(memory_space=pl.ANY)),
        scratch_shapes=[block] * 8
        + [
            pltpu.VMEM((HALVES, SIDE, SIDE, channels, LANES), jnp.bfloat16),
            pltpu.VMEM((channels, rows), jnp.float32),
            pltpu.VMEM((channels, rows), jnp.bfloat16),
            pltpu.VMEM((channels, 1), jnp.float32),
            pltpu.VMEM((channels, image_rows), jnp.float32),
            pltpu.VMEM((ctx_count, 8, 1024), jnp.float32),
            dma((2,)),
            dma((HALVES, 2, 2)),
            dma((HALVES, 2, 2)),
            dma((HALVES, 2)),
            dma((HALVES, 2)),
            dma((HALVES, SIDE - 1, SIDE)),
            dma((HALVES, SIDE - 1, SIDE)),
            dma((HALVES, SIDE)),
            dma((ctx_count - 1,)),
            dma((ctx_count - 1,)),
        ],
        compiler_params=pltpu.CompilerParams(
            collective_id=1, has_side_effects=True, vmem_limit_bytes=VMEM_LIMIT
        ),
        cost_estimate=pl.CostEstimate(
            flops=20 * rows * channels, bytes_accessed=200 * 2**20, transcendentals=0
        ),
        name="hand_over",
    )(norm_t, normed_t, gain, inverse_std, owner_map, bias, means)


STEPS = 4


def finish_kernel(
    grad_scale, final_hbm, weight_hbm, sum_ref, out_hbm, grad_w2_hbm, grad_w1_hbm, ln_ref, up_ref, down_ref,
    final, out, weight, grad_w2, grad_w1, in_sem, out_sem,
):
    wide = final.shape[1] // STEPS
    small_in = pltpu.make_async_copy(weight_hbm, weight, in_sem.at[STEPS])
    small_out = [
        pltpu.make_async_copy(grad_w2, grad_w2_hbm, out_sem.at[STEPS]),
        pltpu.make_async_copy(grad_w1, grad_w1_hbm, out_sem.at[STEPS + 1]),
    ]

    def load(k):
        part = pl.ds(pl.multiple_of(k * wide, wide), wide)
        return pltpu.make_async_copy(final_hbm.at[:, part], final.at[:, part], in_sem.at[k])

    def store(k):
        part = pl.ds(pl.multiple_of(k * wide, wide), wide)
        return pltpu.make_async_copy(out.at[:, part], out_hbm.at[:, part], out_sem.at[k])

    load(0).start()
    load(1).start()
    small_in.start()
    for k in range(2, STEPS):
        load(k).start()
    lanes = out.shape[0]
    row = lax.broadcasted_iota(jnp.int32, (lanes, lanes), 0)
    column = lax.broadcasted_iota(jnp.int32, (lanes, lanes), 1)
    identity = jnp.where(row == column, 1.0, 0.0).astype(jnp.bfloat16)

    def turn(k, carry):
        part = pl.ds(pl.multiple_of(k * wide, wide), wide)
        load(k).wait()
        block = jnp.concatenate([final[0, part, :], final[1, part, :]], axis=1)
        out[:, part] = dot_last(identity, block).astype(jnp.bfloat16)
        store(k).start()
        return carry

    lax.fori_loop(0, STEPS // 2, turn, 0)
    small_in.wait()
    channels = grad_w1.shape[0]
    tall, width = grad_w2.shape
    for i in range(tall * width // ((weight.shape[0] - channels) * width)):
        part = weight.shape[0] - channels
        grad_w2[i * part : (i + 1) * part, :] = (
            weight[channels:, i * width : (i + 1) * width].astype(jnp.float32) * grad_scale
        )
    small_out[0].start()
    grad_w1[...] = weight[:channels, :].astype(jnp.float32) * grad_scale
    small_out[1].start()
    lax.fori_loop(STEPS // 2, STEPS, turn, 0)
    ln_ref[...] = sum_ref[0:2, 0 : ln_ref.shape[1]]
    down_ref[...] = sum_ref[2:3, 0 : down_ref.shape[1]]
    up_ref[...] = sum_ref[3:4, 0 : up_ref.shape[1]]
    for copy in small_out:
        copy.wait()
    for k in range(STEPS):
        store(k).wait()


def finish(final, weight, sums, width, grad_scale):
    each = weight.shape[1]
    channels = weight.shape[0] - width
    vmem = pl.BlockSpec(memory_space=pltpu.VMEM)
    anywhere = pl.BlockSpec(memory_space=pl.ANY)
    return pl.pallas_call(
        functools.partial(finish_kernel, grad_scale),
        out_shape=(
            jax.ShapeDtypeStruct((HALVES * LANES, final.shape[1]), jnp.bfloat16),
            jax.ShapeDtypeStruct((each, width), jnp.float32),
            jax.ShapeDtypeStruct((channels, each), jnp.float32),
            jax.ShapeDtypeStruct((2, channels), jnp.float32),
            jax.ShapeDtypeStruct((1, width), jnp.float32),
            jax.ShapeDtypeStruct((1, width), jnp.float32),
        ),
        in_specs=[anywhere, anywhere, vmem],
        out_specs=(anywhere, anywhere, anywhere, vmem, vmem, vmem),
        scratch_shapes=[
            pltpu.VMEM(final.shape, jnp.bfloat16),
            pltpu.VMEM((HALVES * LANES, final.shape[1]), jnp.bfloat16),
            pltpu.VMEM(weight.shape, jnp.bfloat16),
            pltpu.VMEM((each, width), jnp.float32),
            pltpu.VMEM((channels, each), jnp.float32),
            pltpu.SemaphoreType.DMA((STEPS + 1,)),
            pltpu.SemaphoreType.DMA((STEPS + 2,)),
        ],
        compiler_params=pltpu.CompilerParams(vmem_limit_bytes=VMEM_LIMIT),
        name="finish",
    )(final, weight, sums)


def per_device(out_grad, pre_act, normed, inverse_std, w_up, w_down, ln_gain, owner_map):
    ctx_count = lax.axis_size("ctx")
    tp_count = lax.axis_size("tp")
    row_count = out_grad.shape[0]
    grad_scale = float(row_count * ctx_count) ** (-0.5)
    gain = ln_gain
    normed_t = normed.T
    norm_t, weight, means, bias = gather(
        out_grad,
        pre_act,
        gain,
        w_down,
        w_up.T,
        normed_t,
        ctx_count,
        owner_map.shape[1],
        float(normed.shape[1] * tp_count),
    )
    weight = lax.psum_scatter(weight, "ctx", scatter_dimension=0, tiled=True)
    sums, final = hand_over(
        norm_t,
        normed_t,
        gain,
        inverse_std[None, :],
        owner_map,
        bias,
        means,
        grad_scale,
        ctx_count,
    )
    vit_grad, grad_w2, grad_w1_t, ln_grads, bias_up, bias_down = finish(
        final, weight[0], sums, bias.shape[1], grad_scale
    )
    return (grad_w2, grad_w1_t.T, bias_up[0], bias_down[0], ln_grads, vit_grad)


def solution(mesh):
    return jax.shard_map(
        per_device,
        mesh=mesh,
        in_specs=(
            P("ctx", "tp"),
            P("ctx", "tp"),
            P("ctx", "tp"),
            P("ctx"),
            P(None, "tp"),
            P(None, "tp"),
            P("tp"),
            P("ctx", None),
        ),
        out_specs=(
            P("ctx", "tp"),
            P("ctx", "tp"),
            P("tp"),
            P("tp"),
            P(None, "tp"),
            P(("ctx", "tp"), None),
        ),
        check_vma=False,
    )
```
